32 devices in a mesh: seq: 8 (over z, x), tp: 4 (over y, core).
Axes of the slice: x: 2, y: 2, z: 4, core: 2. Of those that a mesh axis runs over, the one named last changes fastest.
Arguments:
- x_tokens: bfloat16 [2048, 1536], P('seq'), may hold values from -6 to 6
- caption: bfloat16 [2048, 4096], P('seq'), may hold values from -6 to 6
- timesteps: float32 [8], replicated, may hold values from 0 to 1, as said below
- segment_ids: int32 [2048], P('seq'), may hold values from 0 to 7, never falling along the last dimension, each value on 1 to 1792 neighbouring positions
- out_grad: bfloat16 [2048, 1536], P('seq'), may hold values from -6 to 6
- mod_weight: float32 [1024, 9216], P('seq'), may hold values from -0.1875 to 0.1875
- mod_first: float32 [1024, 9216], P('seq'), may hold values from -9.1552734e-05 to 9.1552734e-05
- mod_second: float32 [1024, 9216], P('seq'), may hold values from 9.934108e-10 to 7.947286e-09
- norm_gains: float32 [2, 1536], P(None, 'seq'), may hold values from 0.5 to 1.5
- gains_first: float32 [2, 1536], P(None, 'seq'), may hold values from -0.00024414062 to 0.00024414062
- gains_second: float32 [2, 1536], P(None, 'seq'), may hold values from 8.940697e-09 to 7.152558e-08
- qkv_weight: float32 [3, 1536, 1536], P(None, 'seq', 'tp'), may hold values from -0.15625 to 0.15625
- qkv_first: float32 [3, 1536, 1536], P(None, 'seq', 'tp'), may hold values from -9.1552734e-05 to 9.1552734e-05
- qkv_second: float32 [3, 1536, 1536], P(None, 'seq', 'tp'), may hold values from 9.934108e-10 to 7.947286e-09
- out_weight: float32 [1536, 1536], P('tp', 'seq'), may hold values from -0.625 to 0.625
- out_first: float32 [1536, 1536], P('tp', 'seq'), may hold values from -9.1552734e-05 to 9.1552734e-05
- out_second: float32 [1536, 1536], P('tp', 'seq'), may hold values from 9.934108e-10 to 7.947286e-09
- text_weight: float32 [2, 4096, 1536], P(None, 'seq', 'tp'), may hold values from -0.09375 to 0.09375
- text_first: float32 [2, 4096, 1536], P(None, 'seq', 'tp'), may hold values from -9.1552734e-05 to 9.1552734e-05
- text_second: float32 [2, 4096, 1536], P(None, 'seq', 'tp'), may hold values from 9.934108e-10 to 7.947286e-09
- cross_gates: float32 [24], P('tp'), may hold values from 0.4 to 1.6
- cross_first: float32 [24], P('tp'), may hold values from -0.00048828125 to 0.00048828125
- cross_second: float32 [24], P('tp'), may hold values from 2.4835268e-08 to 1.9868214e-07
- updown_weight: float32 [2, 1536, 4096], P(None, 'seq', 'tp'), may hold values from -0.15625 to 0.15625
- updown_first: float32 [2, 1536, 4096], P(None, 'seq', 'tp'), may hold values from -9.1552734e-05 to 9.1552734e-05
- updown_second: float32 [2, 1536, 4096], P(None, 'seq', 'tp'), may hold values from 9.934108e-10 to 7.947286e-09
- down_weight: float32 [4096, 1536], P('tp', 'seq'), may hold values from -0.09375 to 0.09375
- down_first: float32 [4096, 1536], P('tp', 'seq'), may hold values from -9.1552734e-05 to 9.1552734e-05
- down_second: float32 [4096, 1536], P('tp', 'seq'), may hold values from 9.934108e-10 to 7.947286e-09
Outputs:
- block_out: float32 [2048, 1536], P('seq')
- input_grad: float32 [2048, 1536], P('seq')
- grad_norm: float32 [], replicated
- mod_weight_new: float32 [1024, 9216], P('seq')
- mod_first_new: float32 [1024, 9216], P('seq')
- mod_second_new: float32 [1024, 9216], P('seq')
- gains_new: float32 [2, 1536], P(None, 'seq')
- gains_first_new: float32 [2, 1536], P(None, 'seq')
- gains_second_new: float32 [2, 1536], P(None, 'seq')
- qkv_weight_new: float32 [3, 1536, 1536], P(None, 'seq', 'tp')
- qkv_first_new: float32 [3, 1536, 1536], P(None, 'seq', 'tp')
- qkv_second_new: float32 [3, 1536, 1536], P(None, 'seq', 'tp')
- out_weight_new: float32 [1536, 1536], P('tp', 'seq')
- out_first_new: float32 [1536, 1536], P('tp', 'seq')
- out_second_new: float32 [1536, 1536], P('tp', 'seq')
- text_weight_new: float32 [2, 4096, 1536], P(None, 'seq', 'tp')
- text_first_new: float32 [2, 4096, 1536], P(None, 'seq', 'tp')
- text_second_new: float32 [2, 4096, 1536], P(None, 'seq', 'tp')
- cross_gates_new: float32 [24], P('tp')
- cross_first_new: float32 [24], P('tp')
- cross_second_new: float32 [24], P('tp')
- updown_weight_new: float32 [2, 1536, 4096], P(None, 'seq', 'tp')
- updown_first_new: float32 [2, 1536, 4096], P(None, 'seq', 'tp')
- updown_second_new: float32 [2, 1536, 4096], P(None, 'seq', 'tp')
- down_weight_new: float32 [4096, 1536], P('tp', 'seq')
- down_first_new: float32 [4096, 1536], P('tp', 'seq')
- down_second_new: float32 [4096, 1536], P('tp', 'seq')
The draws below stay inside these ranges and needn't reach their ends.
Inputs may be any that keep to these rules, and one draw needn't show every extreme that they name: `segment_ids`: never falling along the tokens; every one of the 8 images has 1 to 1792 tokens and one has exactly 1792. `timesteps`: logistic function of a random draw.
All inputs are finite; a program needn't handle non-finite values.
Results may differ from the reference program's by a relative error of at most 0.015.
Values may be sent and summed in bfloat16 or wider, within the bound.
No kernel may reach another device: no remote copies, remote signals or barrier semaphores. Data moves between devices by JAX's collectives and lax.ppermute only.
A program may use at most 320 MiB of HBM per device.

```python
import math
from functools import partial
import jax
import jax.numpy as jnp
import numpy as np
from jax import lax

D = 1536
HEADS = 24
HD = 64
FF = 4096
TE = 1024
TD = 4096
TEXT = 256
ITEMS = 8
ADAM_STEP = 10
TOKENS = 2048
ITEM_MOST = 1792
P_ALL = 50331648


def draw_timesteps(key, part):
    raw_values = jax.random.normal(key, (ITEMS,), jnp.float32)
    return jax.nn.sigmoid(raw_values)


def steps_of(own_key, extent, shards, least, high):
    level, own = 1.0, jax.random.fold_in(own_key, 6)
    for dim, parts in shards:
        draws = jnp.exp(jax.random.uniform(jax.random.fold_in(own, dim), (parts,), jnp.float32, least / len(shards), high / len(shards)))
        level = level * jnp.repeat(draws, extent[dim] // parts).reshape([-1 if axis == dim else 1 for axis in range(len(extent))])
    return level


def profile(number_of, total, bound, slope):
    weights = [(1 << 20) // math.isqrt(rank ** slope) + 1 for rank in range(2, number_of + 1)]
    spare, counts = total - bound - (number_of - 1), [1] * (number_of - 1)
    while spare > 0:
        free = [i for i in range(number_of - 1) if counts[i] < bound]
        whole, budget = sum([weights[i] for i in free]), spare
        for i in free:
            extra = min(bound - counts[i], max(1, budget * weights[i] // whole), spare)
            counts[i] = counts[i] + extra
            spare = spare - extra
    return np.array([bound] + counts)


def uneven_parts(stream_key, amount, total, most, lean):
    if amount == 2:
        one = jax.random.randint(stream_key, (), max(1, total - most), min(most, total - 1) + 1)
        return jnp.stack([one, total - one])
    lengths = jnp.asarray(profile(amount, total, most, lean), jnp.int32)
    pairs = (amount - 1) // 2
    source_of, taker = lengths[1:1 + 2 * pairs:2], lengths[2:2 + 2 * pairs:2]
    slack = jnp.minimum(source_of - 1, most - taker)
    passed = jax.random.randint(jax.random.fold_in(stream_key, 1), (pairs,), 0, 1 << 20) % (slack + 1)
    lengths = lengths.at[1:1 + 2 * pairs:2].set(source_of - passed).at[2:2 + 2 * pairs:2].set(taker + passed)
    return lengths[jax.random.permutation(jax.random.fold_in(stream_key, 2), amount)]


def scatter_about(rng, dims, scale, most, cuts=(), kind=jnp.bfloat16):
    loudness = steps_of(rng, dims, cuts, -0.22, 0.18) if cuts else 1.0
    values = jax.random.normal(rng, dims, jnp.float32) * scale * loudness
    return jnp.minimum(jnp.maximum(values, -most), most).astype(kind)


def setup_inputs(seed: int = 0) -> dict:
    key_list = jax.random.split(jax.random.key(seed), 30)
    x_tokens = scatter_about(key_list[0], (TOKENS, D), 1.0, 6.0, ((0, 8),))
    caption = scatter_about(key_list[1], (ITEMS * TEXT, TD), 1.0, 6.0, ((0, 8),))
    timesteps = draw_timesteps(jax.random.fold_in(key_list[29], 71), 0)
    segment_ids = jnp.searchsorted(jnp.cumsum(uneven_parts(key_list[3], ITEMS, TOKENS, ITEM_MOST, 2)), jnp.arange(TOKENS), side="right").astype(jnp.int32)
    out_grad = scatter_about(key_list[4], (TOKENS, D), 1.0, 6.0, ((0, 8),))
    mod_weight = scatter_about(key_list[5], (TE, 6 * D), TE ** -0.5, 0.1875, ((0, 8),), jnp.float32)
    mod_first = scatter_about(key_list[6], (TE, 6 * D), (0.11 / P_ALL ** 0.5), 9.1552734375e-05, ((0, 8),), jnp.float32)
    mod_second = jnp.clip(jnp.exp(math.log(7.947286384535346e-09) - 2.0794415 * jax.random.uniform(key_list[7], (TE, 6 * D), jnp.float32) ** steps_of(key_list[7], (TE, 6 * D), ((0, 8),), -0.2, 0.2)), 9.934107980669182e-10, 7.947286384535346e-09)
    norm_gains = jnp.clip(1.0 + 0.1 * jax.random.normal(key_list[8], (2, D), jnp.float32), 0.5, 1.5)
    gains_first = scatter_about(key_list[9], (2, D), (0.33 / P_ALL ** 0.5), 0.00024414062, ((1, 8),), jnp.float32)
    gains_second = jnp.clip(jnp.exp(math.log(7.152557657263969e-08) - 2.0794415 * jax.random.uniform(key_list[10], (2, D), jnp.float32) ** steps_of(key_list[10], (2, D), ((1, 8),), -0.2, 0.2)), 8.940697071579962e-09, 7.152557657263969e-08)
    qkv_weight = scatter_about(key_list[11], (3, D, D), D ** -0.5, 0.15625, ((1, 8), (2, 4)), jnp.float32)
    qkv_first = scatter_about(key_list[12], (3, D, D), (0.11 / P_ALL ** 0.5), 9.1552734375e-05, ((1, 8), (2, 4)), jnp.float32)
    qkv_second = jnp.clip(jnp.exp(math.log(7.947286384535346e-09) - 2.0794415 * jax.random.uniform(key_list[13], (3, D, D), jnp.float32) ** steps_of(key_list[13], (3, D, D), ((1, 8), (2, 4)), -0.2, 0.2)), 9.934107980669182e-10, 7.947286384535346e-09)
    out_weight = scatter_about(key_list[14], (D, D), (max(4, D * 16 // (TOKENS // ITEMS))) ** -0.5, 0.625, ((0, 4), (1, 8)), jnp.float32)
    out_first = scatter_about(key_list[15], (D, D), (0.11 / P_ALL ** 0.5), 9.1552734375e-05, ((0, 4), (1, 8)), jnp.float32)
    out_second = jnp.clip(jnp.exp(math.log(7.947286384535346e-09) - 2.0794415 * jax.random.uniform(key_list[16], (D, D), jnp.float32) ** steps_of(key_list[16], (D, D), ((0, 4), (1, 8)), -0.2, 0.2)), 9.934107980669182e-10, 7.947286384535346e-09)
    text_weight = scatter_about(key_list[17], (2, TD, D), TD ** -0.5, 0.09375, ((1, 8), (2, 4)), jnp.float32)
    text_first = scatter_about(key_list[18], (2, TD, D), (0.11 / P_ALL ** 0.5), 9.1552734375e-05, ((1, 8), (2, 4)), jnp.float32)
    text_second = jnp.clip(jnp.exp(math.log(7.947286384535346e-09) - 2.0794415 * jax.random.uniform(key_list[19], (2, TD, D), jnp.float32) ** steps_of(key_list[19], (2, TD, D), ((1, 8), (2, 4)), -0.2, 0.2)), 9.934107980669182e-10, 7.947286384535346e-09)
    cross_gates = jnp.clip(0.4 + 1.2 * jax.random.uniform(key_list[20], (HEADS,), jnp.float32) ** steps_of(key_list[20], (HEADS,), ((0, 4),), -0.2, 0.2), 0.4, 1.6)
    cross_first = scatter_about(key_list[21], (HEADS,), (0.55 / P_ALL ** 0.5), 0.00048828125, ((0, 4),), jnp.float32)
    cross_second = jnp.clip(jnp.exp(math.log(1.986821445143505e-07) - 2.0794415 * jax.random.uniform(key_list[22], (HEADS,), jnp.float32) ** steps_of(key_list[22], (HEADS,), ((0, 4),), -0.2, 0.2)), 2.4835268064293814e-08, 1.986821445143505e-07)
    updown_weight = scatter_about(key_list[23], (2, D, FF), D ** -0.5, 0.15625, ((1, 8), (2, 4)), jnp.float32)
    updown_first = scatter_about(key_list[24], (2, D, FF), (0.11 / P_ALL ** 0.5), 9.1552734375e-05, ((1, 8), (2, 4)), jnp.float32)
    updown_second = jnp.clip(jnp.exp(math.log(7.947286384535346e-09) - 2.0794415 * jax.random.uniform(key_list[25], (2, D, FF), jnp.float32) ** steps_of(key_list[25], (2, D, FF), ((1, 8), (2, 4)), -0.2, 0.2)), 9.934107980669182e-10, 7.947286384535346e-09)
    down_weight = scatter_about(key_list[26], (FF, D), FF ** -0.5, 0.09375, ((0, 4), (1, 8)), jnp.float32)
    down_first = scatter_about(key_list[27], (FF, D), (0.11 / P_ALL ** 0.5), 9.1552734375e-05, ((0, 4), (1, 8)), jnp.float32)
    down_second = jnp.clip(jnp.exp(math.log(7.947286384535346e-09) - 2.0794415 * jax.random.uniform(key_list[28], (FF, D), jnp.float32) ** steps_of(key_list[28], (FF, D), ((0, 4), (1, 8)), -0.2, 0.2)), 9.934107980669182e-10, 7.947286384535346e-09)
    return {"x_tokens": x_tokens, "caption": caption, "timesteps": timesteps, "segment_ids": segment_ids, "out_grad": out_grad, "mod_weight": mod_weight, "mod_first": mod_first, "mod_second": mod_second, "norm_gains": norm_gains, "gains_first": gains_first, "gains_second": gains_second, "qkv_weight": qkv_weight, "qkv_first": qkv_first, "qkv_second": qkv_second, "out_weight": out_weight, "out_first": out_first, "out_second": out_second, "text_weight": text_weight, "text_first": text_first, "text_second": text_second, "cross_gates": cross_gates, "cross_first": cross_first, "cross_second": cross_second, "updown_weight": updown_weight, "updown_first": updown_first, "updown_second": updown_second, "down_weight": down_weight, "down_first": down_first, "down_second": down_second}


highest = lax.Precision.HIGHEST
eps_norm = 1e-06
huge_negative = -1e+30
clip_limit = 1.0
beta_first = 0.9
beta_second = 0.95
adam_eps = 1e-08
rate_matrix = 0.05
rate_small = 0.5
decay_matrix = 0.1

@jax.custom_vjp
def low(v):
    return lax.optimization_barrier(v.astype(jnp.bfloat16)).astype(jnp.float32)

@jax.custom_vjp
def low_back(v):
    return v

def low_keep(v):
    return (low(v), None)

def low_pass(kept, grad):
    return (grad,)

def back_keep(v):
    return (v, None)

def back_low(kept, grad):
    return (low(grad),)
low.defvjp(low_keep, low_pass)
low_back.defvjp(back_keep, back_low)

def matmul(factor, weight):
    return jnp.dot(factor, weight, precision=highest, preferred_element_type=jnp.float32)

def time_embed(timesteps):
    half_width = TE // 2
    frequency = jnp.exp(-math.log(10000.0) * jnp.arange(half_width, dtype=jnp.float32) / half_width)
    angles = 1000.0 * timesteps[:, None] * frequency[None, :]
    return jnp.concatenate([jnp.cos(angles), jnp.sin(angles)], axis=1)

def rms_norm(values):
    return values * lax.rsqrt(lax.optimization_barrier(jnp.mean(values * values, axis=-1, keepdims=True)) + eps_norm)

def masked_softmax(scores, allowed):
    masked = jnp.where(allowed, scores, huge_negative)
    top_score = lax.optimization_barrier(jnp.max(masked, axis=-1, keepdims=True))
    weights = jnp.where(allowed, jnp.exp(masked - top_score), 0.0)
    return weights / lax.optimization_barrier(jnp.sum(weights, axis=-1, keepdims=True))

def attend(query_heads, key_heads, value_heads, query_items, key_items):
    total_rows = query_heads.shape[0]
    block_rows = math.gcd(total_rows, 512)
    block_count = total_rows // block_rows
    score_scale = HD ** (-0.5)

    def one_block(inputs):
        query_part, item_part = inputs
        scores = low_back(jnp.einsum('qhd,khd->hqk', query_part, key_heads, precision=highest) * score_scale)
        probs = masked_softmax(scores, (item_part[:, None] == key_items[None, :])[None])
        return jnp.einsum('hqk,khd->qhd', low(probs), value_heads, precision=highest)
    outputs = lax.map(jax.checkpoint(one_block), (query_heads.reshape(block_count, block_rows, HEADS, HD), query_items.reshape(block_count, block_rows)))
    return outputs.reshape(total_rows, HEADS, HD)

def block(mod_weight, norm_gains, qkv_weight, out_weight, text_weight, cross_gates, updown_weight, down_weight, x_value, caption_value, silu_embed, segment_ids):
    token_count = x_value.shape[0]
    modulation = low_back(matmul(silu_embed, low(mod_weight)))
    per_token = modulation[segment_ids]
    shift_attn, scale_attn, gate_attn, shift_ffn, scale_ffn, gate_ffn = jnp.split(per_token, 6, axis=1)
    gains = low(norm_gains)
    hidden_attn = low(rms_norm(x_value) * gains[0] * (1.0 + scale_attn) + shift_attn)
    qkv_copy = low(qkv_weight)
    queries = low_back(low(matmul(hidden_attn, qkv_copy[0]))).reshape(token_count, HEADS, HD)
    keys = low_back(low(matmul(hidden_attn, qkv_copy[1]))).reshape(token_count, HEADS, HD)
    values = low_back(low(matmul(hidden_attn, qkv_copy[2]))).reshape(token_count, HEADS, HD)
    text_copy = low(text_weight)
    text_rows = caption_value.shape[0]
    text_keys = low_back(low(matmul(caption_value, text_copy[0]))).reshape(text_rows, HEADS, HD)
    text_values = low_back(low(matmul(caption_value, text_copy[1]))).reshape(text_rows, HEADS, HD)
    text_items = jnp.arange(text_rows, dtype=jnp.int32) // TEXT
    self_out = attend(queries, keys, values, segment_ids, segment_ids)
    text_out = low_back(attend(queries, text_keys, text_values, segment_ids, text_items))
    mixed = self_out + jnp.tanh(cross_gates)[None, :, None] * text_out
    mixed = low_back(low(mixed.reshape(token_count, D)))
    attn = low_back(matmul(mixed, low(out_weight)))
    x_mid = x_value + jnp.tanh(gate_attn) * attn
    hidden_ffn = low(rms_norm(x_mid) * gains[1] * (1.0 + scale_ffn) + shift_ffn)
    updown_copy = low(updown_weight)
    gate_pre = low_back(matmul(hidden_ffn, updown_copy[0]))
    up_pre = low_back(matmul(hidden_ffn, updown_copy[1]))
    inner = low(jax.nn.silu(gate_pre) * up_pre)
    ffn_out = low_back(matmul(inner, low(down_weight)))
    return x_mid + jnp.tanh(gate_ffn) * ffn_out

def adam_update(weight, first, second, grad, clip, rate, decay):
    clipped = grad * clip
    first_new = beta_first * first + (1.0 - beta_first) * clipped
    second_new = beta_second * second + (1.0 - beta_second) * clipped * clipped
    first_hat = first_new / (1.0 - beta_first ** ADAM_STEP)
    second_hat = second_new / (1.0 - beta_second ** ADAM_STEP)
    weight_new = weight - rate * (first_hat / (jnp.sqrt(second_hat) + adam_eps) + decay * weight)
    return (weight_new, first_new, second_new)

def reference(x_tokens, caption, timesteps, segment_ids, out_grad, mod_weight, mod_first, mod_second, norm_gains, gains_first, gains_second, qkv_weight, qkv_first, qkv_second, out_weight, out_first, out_second, text_weight, text_first, text_second, cross_gates, cross_first, cross_second, updown_weight, updown_first, updown_second, down_weight, down_first, down_second):
    silu_embed = low(jax.nn.silu(time_embed(timesteps)))
    forward = partial(block, caption_value=caption.astype(jnp.float32), silu_embed=silu_embed, segment_ids=segment_ids)
    output, pullback = jax.vjp(forward, mod_weight, norm_gains, qkv_weight, out_weight, text_weight, cross_gates, updown_weight, down_weight, x_tokens.astype(jnp.float32))
    gradients = pullback(out_grad.astype(jnp.float32))
    weight_grads = gradients[:8]
    total_square = jnp.sum(jnp.stack([jnp.sum(grad_item * grad_item) for grad_item in weight_grads]))
    grad_norm = jnp.sqrt(total_square)
    clip = jnp.minimum(1.0, clip_limit / (grad_norm + 1e-06))
    mod_new = adam_update(mod_weight, mod_first, mod_second, weight_grads[0], clip, rate_matrix, decay_matrix)
    gains_new = adam_update(norm_gains, gains_first, gains_second, weight_grads[1], clip, rate_small, 0.0)
    qkv_new = adam_update(qkv_weight, qkv_first, qkv_second, weight_grads[2], clip, rate_matrix, decay_matrix)
    out_new = adam_update(out_weight, out_first, out_second, weight_grads[3], clip, rate_matrix, decay_matrix)
    text_new = adam_update(text_weight, text_first, text_second, weight_grads[4], clip, rate_matrix, decay_matrix)
    cross_new = adam_update(cross_gates, cross_first, cross_second, weight_grads[5], clip, rate_small, 0.0)
    updown_new = adam_update(updown_weight, updown_first, updown_second, weight_grads[6], clip, rate_matrix, decay_matrix)
    down_new = adam_update(down_weight, down_first, down_second, weight_grads[7], clip, rate_matrix, decay_matrix)
    block_out = output
    input_grad = gradients[8]
    return (block_out, input_grad, grad_norm, mod_new[0], mod_new[1], mod_new[2], gains_new[0], gains_new[1], gains_new[2], qkv_new[0], qkv_new[1], qkv_new[2], out_new[0], out_new[1], out_new[2], text_new[0], text_new[1], text_new[2], cross_new[0], cross_new[1], cross_new[2], updown_new[0], updown_new[1], updown_new[2], down_new[0], down_new[1], down_new[2])
```

```python
import functools
import math

import jax
import jax.numpy as jnp
from jax import lax
from jax.experimental import pallas as pl
from jax.experimental.pallas import tpu as pltpu
from jax.sharding import PartitionSpec as P

HD = 64
TE = 1024
TEXT = 256
ITEMS = 8
ADAM_STEP = 10

bf16 = jnp.bfloat16
f32 = jnp.float32
highest = lax.Precision.HIGHEST
eps_norm = 1e-06
masked_score = -1e30
lowest_max = -1e20
clip_limit = 1.0
beta_first = 0.9
beta_second = 0.95
adam_eps = 1e-08
rate_matrix = 0.05
rate_small = 0.5
decay_matrix = 0.1
score_scale = HD ** (-0.5)

CORE_SWAP = [(0, 1), (1, 0), (2, 3), (3, 2)]
Y_SWAP = [(0, 2), (2, 0), (1, 3), (3, 1)]
CYCLE = (0, 2, 4, 6, 7, 5, 3, 1)


def time_embed(timesteps):
    half_width = TE // 2
    frequency = jnp.exp(-math.log(10000.0) * jnp.arange(half_width, dtype=f32) / half_width)
    angles = 1000.0 * timesteps[:, None] * frequency[None, :]
    return jnp.concatenate([jnp.cos(angles), jnp.sin(angles)], axis=1)


def rms_parts(values):
    inverse = lax.rsqrt(jnp.mean(values * values, axis=-1, keepdims=True) + eps_norm)
    return (values * inverse, inverse)


def rms_back(normed, inverse, normed_grad):
    return inverse * (normed_grad - normed * jnp.mean(normed_grad * normed, axis=-1, keepdims=True))


def adam_update(weight, first, second, grad, clip, rate, decay):
    clipped = grad * clip
    first_new = beta_first * first + (1.0 - beta_first) * clipped
    second_new = beta_second * second + (1.0 - beta_second) * clipped * clipped
    first_hat = first_new / (1.0 - beta_first**ADAM_STEP)
    second_hat = second_new / (1.0 - beta_second**ADAM_STEP)
    weight_new = weight - rate * (first_hat / (jnp.sqrt(second_hat) + adam_eps) + decay * weight)
    return (weight_new, first_new, second_new)


def square_sum(values):
    return jnp.sum(values * values)


def dot(a, b, dims):
    return lax.dot_general(a, b, (dims, ((), ())), preferred_element_type=f32)


class Ring:
    def __init__(self, size):
        self.size = size
        self.ring = size == len(CYCLE)
        self.seq = lax.axis_index("seq")
        if self.ring:
            place_of = [CYCLE.index(s) for s in range(size)]
            self.place = jnp.asarray(place_of, jnp.int32)[self.seq]
            self.cycle = jnp.asarray(CYCLE + CYCLE, jnp.int32)

    def at(self, offset):
        return self.cycle[self.place + offset % self.size]

    def pairs(self, step, sends=None):
        n = self.size
        return [
            (CYCLE[p], CYCLE[(p + step) % n]) for p in range(n) if sends is None or sends(p)
        ]

    def hop(self, value, step, sends=None):
        return lax.ppermute(value, "seq", self.pairs(step, sends))

    def gather_rows(self, own):
        if not self.ring:
            return lax.all_gather(own, "seq", axis=0, tiled=True)
        rows = own.shape[0]
        half = rows // 2
        whole = jnp.zeros((self.size * rows, own.shape[1]), own.dtype)

        def put(whole, part, offset, start):
            return lax.dynamic_update_slice(whole, part, (self.at(offset) * rows + start, 0))

        whole = put(whole, own, 0, 0)
        ahead = behind = own
        for k in range(1, 4):
            ahead = self.hop(ahead, 1)
            behind = self.hop(behind, -1)
            whole = put(whole, ahead, -k, 0)
            whole = put(whole, behind, k, 0)
        whole = put(whole, self.hop(ahead[:half], 1), 4, 0)
        return put(whole, self.hop(behind[half:], -1), 4, half)

    def reduce_rows(self, chunk_of, active=None):
        if not self.ring:
            chunks = jnp.concatenate([chunk_of(s).astype(bf16) for s in range(self.size)], 0)
            return lax.psum_scatter(chunks, "seq", scatter_dimension=0, tiled=True).astype(f32)

        def sends(k):
            if active is None:
                return None
            return lambda p: CYCLE[(p + k) % self.size] in active

        ahead = chunk_of(self.at(4)).astype(bf16)
        behind = chunk_of(self.at(-3)).astype(bf16)
        for k in (3, 2, 1):
            moved = self.hop(ahead, 1, sends(k + 1))
            ahead = (moved.astype(f32) + chunk_of(self.at(k))).astype(bf16)
            if k > 1:
                moved = self.hop(behind, -1, sends(-k))
                behind = (moved.astype(f32) + chunk_of(self.at(1 - k))).astype(bf16)
        ahead = self.hop(ahead, 1, sends(1))
        behind = self.hop(behind, -1, sends(-1))
        return chunk_of(self.at(0)) + ahead.astype(f32) + behind.astype(f32)


def butterfly(value, axis, size):
    step = 1
    while step < size:
        value = value + lax.ppermute(value, axis, [(i, i ^ step) for i in range(size)])
        step *= 2
    return value


def join_pair(second, mine, other, axis):
    low = jnp.where(second, other, mine)
    high = jnp.where(second, mine, other)
    return jnp.concatenate([low, high], axis)


def gather_tp(value, axis):
    tp = lax.axis_index("tp")
    pair = join_pair(tp % 2 == 1, value, lax.ppermute(value, "tp", CORE_SWAP), axis)
    return join_pair(tp >= 2, pair, lax.ppermute(pair, "tp", Y_SWAP), axis)


def psum_tp(part):
    second = lax.axis_index("tp") % 2
    part = part.astype(bf16)
    half = part.shape[0] // 2
    mine = lax.dynamic_slice_in_dim(part, second * half, half, 0)
    other = lax.dynamic_slice_in_dim(part, (1 - second) * half, half, 0)
    mine = (mine.astype(f32) + lax.ppermute(other, "tp", CORE_SWAP).astype(f32)).astype(bf16)
    mine = (mine.astype(f32) + lax.ppermute(mine, "tp", Y_SWAP).astype(f32)).astype(bf16)
    return join_pair(second == 1, mine, lax.ppermute(mine, "tp", CORE_SWAP), 0).astype(f32)


def attend_kernel(
    table, gate, q_ref, k_ref, vt_ref, tk_ref, tvt_ref, sq_ref, sk_ref,
    mixed_ref, self_ref, text_ref, stats_ref, *, block_k,
):
    i = pl.program_id(0)
    q = q_ref[...]
    item_of_q = sq_ref[...]
    width = q.shape[0]

    def self_step(j, carry):
        top, total, out = carry
        at = pl.ds(pl.multiple_of(j * block_k, block_k), block_k)
        scores = dot(k_ref[at, :], q, ((1,), (1,)))
        scores = jnp.where(sk_ref[at, :] == item_of_q, scores, masked_score)
        new_top = jnp.maximum(top, jnp.max(scores, axis=0, keepdims=True))
        weights = jnp.exp(scores - new_top)
        shrink = jnp.exp(top - new_top)
        total = total * shrink + jnp.sum(weights, axis=0, keepdims=True)
        out = out * shrink + dot(vt_ref[:, at], weights.astype(bf16), ((1,), (0,)))
        return (new_top, total, out)

    start = (
        jnp.full((1, width), lowest_max, f32),
        jnp.zeros((1, width), f32),
        jnp.zeros((HD, width), f32),
    )
    top, total, out = lax.fori_loop(table[0, i], table[1, i], self_step, start)
    self_out = out / total
    self_ref[...] = self_out
    stats_ref[0:1, :] = top + jnp.log(total)

    def text_step(item, carry):
        out, stat = carry
        at = pl.ds(pl.multiple_of(item * TEXT, TEXT), TEXT)
        scores = dot(tk_ref[at, :], q, ((1,), (1,)))
        top = jnp.max(scores, axis=0, keepdims=True)
        weights = jnp.exp(scores - top)
        total = jnp.sum(weights, axis=0, keepdims=True)
        probs = (weights / total).astype(bf16)
        part = dot(tvt_ref[:, at], probs, ((1,), (0,)))
        here = item_of_q == item
        return (jnp.where(here, part, out), jnp.where(here, top + jnp.log(total), stat))

    start = (jnp.zeros((HD, width), f32), jnp.zeros((1, width), f32))
    text_out, text_stat = lax.fori_loop(table[2, i], table[3, i], text_step, start)
    text_ref[...] = text_out
    stats_ref[1:2, :] = text_stat
    mixed_ref[...] = jnp.transpose(self_out + gate[0] * text_out).astype(bf16)


def attend_back_kernel(
    table, gate, q_ref, g_ref, k_ref, v_ref, kt_ref, tk_ref, tv_ref, tkt_ref,
    self_ref, text_ref, stats_ref, sq_ref, sk_ref,
    dq_ref, dk_ref, dv_ref, tdk_ref, tdv_ref, cross_ref,
    dk_sum, dv_sum, tdk_sum, tdv_sum, *, block_k,
):
    i = pl.program_id(0)

    @pl.when(i == 0)
    def _():
        dk_sum[...] = jnp.zeros_like(dk_sum)
        dv_sum[...] = jnp.zeros_like(dv_sum)
        tdk_sum[...] = jnp.zeros_like(tdk_sum)
        tdv_sum[...] = jnp.zeros_like(tdv_sum)

    q = q_ref[...]
    g = g_ref[...]
    item_of_q = sq_ref[...]
    g_value = g.astype(f32)
    gt_value = (g_value * gate[0]).astype(bf16)
    g_turned = jnp.transpose(g_value)
    gt_turned = jnp.transpose(gt_value.astype(f32))
    text_out = text_ref[...]
    cross_ref[...] = jnp.sum(g_turned * text_out, axis=0, keepdims=True)
    delta = jnp.sum(g_turned * self_ref[...], axis=0, keepdims=True)
    text_delta = jnp.sum(gt_turned * text_out, axis=0, keepdims=True)
    stat = stats_ref[0:1, :]
    text_stat = stats_ref[1:2, :]

    def self_step(j, total):
        at = pl.ds(pl.multiple_of(j * block_k, block_k), block_k)
        scores = dot(k_ref[at, :], q, ((1,), (1,)))
        allowed = sk_ref[at, :] == item_of_q
        probs = jnp.exp(jnp.where(allowed, scores - stat, masked_score))
        prob_grad = dot(v_ref[at, :], g, ((1,), (1,)))
        score_grad = (probs * (prob_grad - delta)).astype(bf16)
        dk_sum[at, :] += dot(score_grad, q, ((1,), (0,)))
        dv_sum[at, :] += dot(probs.astype(bf16), g, ((1,), (0,)))
        return total + dot(kt_ref[:, at], score_grad, ((1,), (0,)))

    total = lax.fori_loop(
        table[0, i], table[1, i], self_step, jnp.zeros((HD, q.shape[0]), f32)
    )

    def text_step(item, total):
        at = pl.ds(pl.multiple_of(item * TEXT, TEXT), TEXT)
        scores = dot(tk_ref[at, :], q, ((1,), (1,)))
        probs = jnp.exp(jnp.where(item_of_q == item, scores - text_stat, masked_score))
        prob_grad = dot(tv_ref[at, :], gt_value, ((1,), (1,)))
        score_grad = (probs * (prob_grad - text_delta)).astype(bf16)
        tdk_sum[at, :] += dot(score_grad, q, ((1,), (0,)))
        tdv_sum[at, :] += dot(probs.astype(bf16), gt_value, ((1,), (0,)))
        return total + dot(tkt_ref[:, at], score_grad, ((1,), (0,)))

    total = lax.fori_loop(table[2, i], table[3, i], text_step, total)
    dq_ref[...] = jnp.transpose(total * score_scale).astype(bf16)

    @pl.when(i == pl.num_programs(0) - 1)
    def _():
        dk_ref[...] = dk_sum[...].astype(bf16)
        dv_ref[...] = dv_sum[...].astype(bf16)
        tdk_ref[...] = tdk_sum[...].astype(bf16)
        tdv_ref[...] = tdv_sum[...].astype(bf16)


def whole(shape):
    return pl.BlockSpec(shape, lambda i, *_: (0, 0), pipeline_mode=pl.Buffered(1))


def rows_block(block, width):
    return pl.BlockSpec((block, width), lambda i, *_: (i, 0))


def lanes_block(rows, block):
    return pl.BlockSpec((rows, block), lambda i, *_: (0, i))


def attention_table(segments, block_q, block_k):
    by_block = segments.reshape(-1, block_q)
    low_item, high_item = by_block[:, 0], by_block[:, -1]
    first_key = jnp.sum(segments[None, :] < low_item[:, None], axis=1)
    end_key = jnp.sum(segments[None, :] <= high_item[:, None], axis=1)
    return jnp.stack(
        [first_key // block_k, (end_key + block_k - 1) // block_k, low_item, high_item + 1]
    ).astype(jnp.int32)


def attend(table, gate, q, k, vt, tk, tvt, segments, block_q, block_k):
    count, rows = q.shape[0], tk.shape[0]
    return pl.pallas_call(
        functools.partial(attend_kernel, block_k=block_k),
        out_shape=(
            jax.ShapeDtypeStruct((count, HD), bf16),
            jax.ShapeDtypeStruct((HD, count), f32),
            jax.ShapeDtypeStruct((HD, count), f32),
            jax.ShapeDtypeStruct((2, count), f32),
        ),
        grid_spec=pltpu.PrefetchScalarGridSpec(
            num_scalar_prefetch=2,
            grid=(count // block_q,),
            in_specs=[
                rows_block(block_q, HD),
                whole((count, HD)),
                whole((HD, count)),
                whole((rows, HD)),
                whole((HD, rows)),
                lanes_block(1, block_q),
                whole((count, 1)),
            ],
            out_specs=(
                rows_block(block_q, HD),
                lanes_block(HD, block_q),
                lanes_block(HD, block_q),
                lanes_block(2, block_q),
            ),
        ),
        cost_estimate=pl.CostEstimate(
            flops=4 * count * count * HD, bytes_accessed=8 * count * HD, transcendentals=count * count
        ),
        name="attend",
    )(table, gate, q, k, vt, tk, tvt, segments[None, :], segments[:, None])


def attend_back(
    table, gate, q, g, k, v, kt, tk, tv, tkt, self_out, text_out, stats, segments, block_q, block_k
):
    count, rows = q.shape[0], tk.shape[0]
    return pl.pallas_call(
        functools.partial(attend_back_kernel, block_k=block_k),
        out_shape=(
            jax.ShapeDtypeStruct((count, HD), bf16),
            jax.ShapeDtypeStruct((count, HD), bf16),
            jax.ShapeDtypeStruct((count, HD), bf16),
            jax.ShapeDtypeStruct((rows, HD), bf16),
            jax.ShapeDtypeStruct((rows, HD), bf16),
            jax.ShapeDtypeStruct((1, count), f32),
        ),
        grid_spec=pltpu.PrefetchScalarGridSpec(
            num_scalar_prefetch=2,
            grid=(count // block_q,),
            in_specs=[
                rows_block(block_q, HD),
                rows_block(block_q, HD),
                whole((count, HD)),
                whole((count, HD)),
                whole((HD, count)),
                whole((rows, HD)),
                whole((rows, HD)),
                whole((HD, rows)),
                lanes_block(HD, block_q),
                lanes_block(HD, block_q),
                lanes_block(2, block_q),
                lanes_block(1, block_q),
                whole((count, 1)),
            ],
            out_specs=(
                rows_block(block_q, HD),
                whole((count, HD)),
                whole((count, HD)),
                whole((rows, HD)),
                whole((rows, HD)),
                lanes_block(1, block_q),
            ),
            scratch_shapes=[
                pltpu.VMEM((count, HD), f32),
                pltpu.VMEM((count, HD), f32),
                pltpu.VMEM((rows, HD), f32),
                pltpu.VMEM((rows, HD), f32),
            ],
        ),
        cost_estimate=pl.CostEstimate(
            flops=10 * count * count * HD, bytes_accessed=24 * count * HD, transcendentals=count * count
        ),
        name="attend_back",
    )(
        table, gate, q, g, k, v, kt, tk, tv, tkt, self_out, text_out, stats,
        segments[None, :], segments[:, None],
    )


def per_device(
    x_tokens, caption, timesteps, segment_ids, out_grad,
    mod_weight, mod_first, mod_second,
    norm_gains, gains_first, gains_second,
    qkv_weight, qkv_first, qkv_second,
    out_weight, out_first, out_second,
    text_weight, text_first, text_second,
    cross_gates, cross_first, cross_second,
    updown_weight, updown_first, updown_second,
    down_weight, down_first, down_second,
    *, seq_size, tp_size,
):
    seq_index = lax.axis_index("seq")
    tp_index = lax.axis_index("tp")
    ring = Ring(seq_size)
    here, width = x_tokens.shape
    heads = cross_gates.shape[0]
    local_width = heads * HD
    count = here * seq_size
    first_owner = 1 if seq_size >= heads + 2 else 0
    owners = range(first_owner, first_owner + heads)
    my_head = jnp.clip(seq_index - first_owner, 0, heads - 1)
    is_owner = (seq_index >= first_owner) & (seq_index < first_owner + heads)

    def to_owners(by_head):
        spare = ((first_owner, seq_size - heads - first_owner), (0, 0), (0, 0))
        out = lax.all_to_all(jnp.pad(by_head, spare), "seq", 0, 0, tiled=True)
        return out.reshape(count, by_head.shape[2])

    def from_owner(rows):
        out = lax.all_to_all(rows.reshape(seq_size, here, -1), "seq", 0, 0, tiled=True)
        return out[first_owner : first_owner + heads]

    slots = jnp.zeros((seq_size, here), f32)
    slots = lax.dynamic_update_slice(slots, segment_ids.astype(f32)[None], (seq_index, 0))
    gain_cols = norm_gains.shape[1]
    gain_slots = jnp.zeros((2, width), f32)
    gain_slots = lax.dynamic_update_slice(gain_slots, norm_gains, (0, seq_index * gain_cols))

    silu_embed = jax.nn.silu(time_embed(timesteps)).astype(bf16)
    mod_rows = mod_weight.shape[0]
    quarter = width // tp_size
    embed_rows = lax.dynamic_slice_in_dim(silu_embed, seq_index * mod_rows, mod_rows, 1)
    mod_quarter = lax.dynamic_slice_in_dim(
        mod_weight.reshape(mod_rows, 6, width), tp_index * quarter, quarter, 2
    ).astype(bf16)
    mod_part = dot(embed_rows, mod_quarter.reshape(mod_rows, 6 * quarter), ((1,), (0,)))
    packed = jnp.concatenate(
        [mod_part.reshape(-1), slots.reshape(-1), gain_slots.reshape(-1)]
    ).reshape(-1, 128)
    packed = butterfly(packed, "seq", seq_size).reshape(-1)
    mod_end = mod_part.size
    modulation = gather_tp(packed[:mod_end].reshape(ITEMS, 6, quarter), 2)
    modulation = modulation.reshape(ITEMS, 6 * width)
    segments = packed[mod_end : mod_end + count].astype(jnp.int32)
    gains_value = packed[mod_end + count :].reshape(2, width).astype(bf16).astype(f32)

    def turned(shard):
        return jnp.transpose(shard.astype(bf16), (1, 0, 2)).reshape(shard.shape[1], -1)

    qkv_all = ring.gather_rows(turned(qkv_weight))

    cap_cols = caption.shape[1] // seq_size
    cap_part = cap_cols // tp_size
    cap_own = lax.dynamic_index_in_dim(
        caption.reshape(here_rows := caption.shape[0], seq_size, tp_size, cap_part),
        tp_index, 2, keepdims=False,
    )
    cap_own = lax.all_to_all(cap_own, "seq", 1, 0, tiled=True)
    text_rows = here_rows * seq_size
    caption_cols = gather_tp(cap_own.reshape(text_rows, cap_part), 1)
    text_by_head = jnp.transpose(
        text_weight.astype(bf16).reshape(2, cap_cols, heads, HD), (2, 1, 0, 3)
    ).reshape(heads, cap_cols, 2 * HD)

    def text_chunk(s):
        head = jnp.clip(s - first_owner, 0, heads - 1)
        return dot(
            caption_cols,
            lax.dynamic_index_in_dim(text_by_head, head, 0, keepdims=False),
            ((1,), (0,)),
        )

    text_kv = ring.reduce_rows(text_chunk, owners).astype(bf16)
    text_keys = text_kv[:, :HD]
    text_values = text_kv[:, HD:]

    out_all = ring.gather_rows(out_weight.astype(bf16).T)
    updown_all = ring.gather_rows(turned(updown_weight))
    down_all = ring.gather_rows(down_weight.astype(bf16).T)
    hidden_units = down_weight.shape[0]

    item_onehot = (segment_ids[:, None] == jnp.arange(ITEMS, dtype=jnp.int32)[None, :]).astype(f32)
    per_token = jnp.dot(item_onehot, modulation, precision=highest, preferred_element_type=f32)
    shift_attn, scale_attn, gate_attn, shift_ffn, scale_ffn, gate_ffn = jnp.split(
        per_token, 6, axis=1
    )
    x_value = x_tokens.astype(f32)
    normed_attn, inverse_attn = rms_parts(x_value)
    hidden_attn = (normed_attn * gains_value[0] * (1.0 + scale_attn) + shift_attn).astype(bf16)
    projected = dot(hidden_attn, qkv_all, ((1,), (0,))).astype(bf16)
    by_head = jnp.transpose(projected.reshape(here, 3, heads, HD), (2, 0, 1, 3))
    head_qkv = to_owners(by_head.reshape(heads, here, 3 * HD))
    queries = head_qkv[:, :HD] * jnp.asarray(score_scale, bf16)
    keys = head_qkv[:, HD : 2 * HD]
    values = head_qkv[:, 2 * HD :]

    block_q = math.gcd(count, 512)
    block_k = math.gcd(count, 512)
    table = attention_table(segments, block_q, block_k)
    tanh_cross = jnp.tanh(cross_gates)
    my_gate = lax.dynamic_slice_in_dim(tanh_cross, my_head, 1)
    mixed_head, self_out, text_out, stats = attend(
        table, my_gate, queries, keys, values.T, text_keys, text_values.T, segments,
        block_q, block_k,
    )
    mixed = jnp.transpose(from_owner(mixed_head), (1, 0, 2)).reshape(here, local_width)
    attn = psum_tp(dot(mixed, out_all, ((1,), (1,))))
    tanh_attn = jnp.tanh(gate_attn)
    x_mid = x_value + tanh_attn * attn
    normed_ffn, inverse_ffn = rms_parts(x_mid)
    hidden_ffn = (normed_ffn * gains_value[1] * (1.0 + scale_ffn) + shift_ffn).astype(bf16)
    both_pre = dot(hidden_ffn, updown_all, ((1,), (0,)))
    gate_pre = both_pre[:, :hidden_units]
    up_pre = both_pre[:, hidden_units:]
    silu_gate = jax.nn.silu(gate_pre)
    inner = (silu_gate * up_pre).astype(bf16)
    ffn_out = psum_tp(dot(inner, down_all, ((1,), (1,))))
    tanh_ffn = jnp.tanh(gate_ffn)
    block_out = x_mid + tanh_ffn * ffn_out

    grad_value = out_grad.astype(f32)
    ffn_grad = (grad_value * tanh_ffn).astype(bf16)
    inner_grad = dot(ffn_grad, down_all, ((1,), (0,)))
    sigmoid_gate = jax.nn.sigmoid(gate_pre)
    gate_grad = (
        inner_grad * up_pre * sigmoid_gate * (1.0 + gate_pre * (1.0 - sigmoid_gate))
    ).astype(bf16)
    up_grad = (inner_grad * silu_gate).astype(bf16)
    both_grads = jnp.concatenate([gate_grad, up_grad], axis=1)
    hidden_ffn_grad = psum_tp(dot(both_grads, updown_all, ((1,), (1,))))

    def slabs(value):
        return jnp.transpose(value.reshape(here, seq_size, -1), (1, 0, 2))

    def slab_product(left_slabs, right):
        return lambda s: dot(
            lax.dynamic_index_in_dim(left_slabs, s, 0, keepdims=False), right, ((0,), (0,))
        )

    down_owned = ring.reduce_rows(slab_product(slabs(ffn_grad), inner)).T
    updown_rows = ring.reduce_rows(slab_product(slabs(hidden_ffn), both_grads))
    mid_grad = grad_value + rms_back(
        normed_ffn, inverse_ffn, hidden_ffn_grad * gains_value[1] * (1.0 + scale_ffn)
    )
    attn_grad = (mid_grad * tanh_attn).astype(bf16)
    mixed_grad = dot(attn_grad, out_all, ((1,), (0,))).astype(bf16)
    out_owned = ring.reduce_rows(slab_product(slabs(attn_grad), mixed)).T
    head_grad = to_owners(jnp.transpose(mixed_grad.reshape(here, heads, HD), (1, 0, 2)))
    query_grad, key_grad, value_grad, text_key_grad, text_value_grad, cross_rows = attend_back(
        table, my_gate, queries, head_grad, keys, values, keys.T, text_keys, text_values,
        text_keys.T, self_out, text_out, stats, segments, block_q, block_k,
    )
    back = from_owner(jnp.concatenate([query_grad, key_grad, value_grad], axis=1))
    qkv_grads = jnp.transpose(back.reshape(heads, here, 3, HD), (1, 2, 0, 3))
    qkv_grads = qkv_grads.reshape(here, 3 * local_width)
    hidden_attn_grad = psum_tp(dot(qkv_grads, qkv_all, ((1,), (1,))))
    qkv_rows = ring.reduce_rows(slab_product(slabs(hidden_attn), qkv_grads))
    text_grads = ring.gather_rows(jnp.concatenate([text_key_grad, text_value_grad], axis=1))
    text_grads = text_grads.reshape(seq_size, text_rows, 2, HD)
    text_grads = text_grads[first_owner : first_owner + heads]
    text_grads = jnp.transpose(text_grads, (1, 2, 0, 3)).reshape(text_rows, 2 * local_width)
    text_cols = dot(caption_cols, text_grads, ((0,), (0,)))

    input_grad = mid_grad + rms_back(
        normed_attn, inverse_attn, hidden_attn_grad * gains_value[0] * (1.0 + scale_attn)
    )

    def part(value):
        return lax.dynamic_slice_in_dim(value, tp_index * quarter, quarter, 1)

    hidden_attn_part = part(hidden_attn_grad)
    hidden_ffn_part = part(hidden_ffn_grad)
    tanh_attn_part = part(tanh_attn)
    tanh_ffn_part = part(tanh_ffn)
    token_mod = jnp.concatenate(
        [
            hidden_attn_part,
            hidden_attn_part * part(normed_attn) * part(gains_value[0:1]),
            part(mid_grad) * part(attn) * (1.0 - tanh_attn_part * tanh_attn_part),
            hidden_ffn_part,
            hidden_ffn_part * part(normed_ffn) * part(gains_value[1:2]),
            part(grad_value) * part(ffn_out) * (1.0 - tanh_ffn_part * tanh_ffn_part),
        ],
        axis=1,
    )
    item_mod_part = lax.dot_general(
        item_onehot, token_mod, (((0,), (0,)), ((), ())),
        precision=highest, preferred_element_type=f32,
    )
    gain_attn_grad = jnp.sum(hidden_attn_grad * normed_attn * (1.0 + scale_attn), axis=0)
    gain_ffn_grad = jnp.sum(hidden_ffn_grad * normed_ffn * (1.0 + scale_ffn), axis=0)
    cross_here = jnp.where(
        is_owner & (jnp.arange(128) == my_head), jnp.sum(cross_rows), 0.0
    )
    packed = jnp.concatenate(
        [item_mod_part.reshape(-1), gain_attn_grad, gain_ffn_grad, cross_here]
    ).reshape(-1, 128)
    packed = butterfly(packed, "seq", seq_size).reshape(-1)
    item_mod_low = packed[:mod_end].reshape(ITEMS, 6 * quarter).astype(bf16)
    gain_grads = packed[mod_end : mod_end + 2 * width].reshape(2, width)
    gains_owned = lax.dynamic_slice_in_dim(gain_grads, seq_index * gain_cols, gain_cols, 1)
    cross_total = packed[mod_end + 2 * width :][:heads] * (1.0 - tanh_cross * tanh_cross)
    item_mod_all = gather_tp(item_mod_low.reshape(ITEMS, 6, quarter), 2).reshape(ITEMS, -1)
    mod_weight_grad = dot(embed_rows, item_mod_all, ((0,), (0,)))
    mod_quarter_grad = dot(embed_rows, item_mod_low, ((0,), (0,)))

    owned_square = (
        square_sum(qkv_rows)
        + square_sum(out_owned)
        + square_sum(text_cols)
        + square_sum(updown_rows)
        + square_sum(down_owned)
        + square_sum(mod_quarter_grad)
    )
    owned_square = owned_square + jnp.where(tp_index == 0, square_sum(gains_owned), 0.0)
    owned_square = owned_square + jnp.where(seq_index == 0, square_sum(cross_total), 0.0)
    total_square = jnp.full((8, 128), owned_square)
    total_square = butterfly(butterfly(total_square, "tp", tp_size), "seq", seq_size)[0, 0]
    grad_norm = jnp.sqrt(total_square)
    clip = jnp.minimum(1.0, clip_limit / (grad_norm + 1e-06))

    def unturned(rows, blocks):
        return jnp.transpose(rows.reshape(rows.shape[0], blocks, -1), (1, 0, 2))

    matrix = functools.partial(adam_update, clip=clip, rate=rate_matrix, decay=decay_matrix)
    small = functools.partial(adam_update, clip=clip, rate=rate_small, decay=0.0)
    return (
        block_out,
        input_grad,
        grad_norm,
        *matrix(mod_weight, mod_first, mod_second, mod_weight_grad),
        *small(norm_gains, gains_first, gains_second, gains_owned),
        *matrix(qkv_weight, qkv_first, qkv_second, unturned(qkv_rows, 3)),
        *matrix(out_weight, out_first, out_second, out_owned),
        *matrix(text_weight, text_first, text_second, unturned(text_cols, 2)),
        *small(cross_gates, cross_first, cross_second, cross_total),
        *matrix(updown_weight, updown_first, updown_second, unturned(updown_rows, 2)),
        *matrix(down_weight, down_first, down_second, down_owned),
    )


def solution(mesh):
    rows = P("seq", None)
    cols = P(None, "seq")
    split = P(None, "seq", "tp")
    turned = P("tp", "seq")
    heads = P("tp")
    weights = (rows,) * 3 + (cols,) * 3 + (split,) * 3 + (turned,) * 3 + (split,) * 3
    weights = weights + (heads,) * 3 + (split,) * 3 + (turned,) * 3
    return jax.shard_map(
        functools.partial(per_device, seq_size=mesh.shape["seq"], tp_size=mesh.shape["tp"]),
        mesh=mesh,
        in_specs=(rows, rows, P(), P("seq"), rows) + weights,
        out_specs=(rows, rows, P()) + weights,
        check_vma=False,
    )
```

```python
import functools
import math

import jax
import jax.numpy as jnp
from jax import lax
from jax.experimental import pallas as pl
from jax.experimental.pallas import tpu as pltpu
from jax.sharding import PartitionSpec as P

HD = 64
TE = 1024
TEXT = 256
ITEMS = 8
ADAM_STEP = 10

bf16 = jnp.bfloat16
f32 = jnp.float32
highest = lax.Precision.HIGHEST
eps_norm = 1e-06
masked_score = -1e30
lowest_max = -1e20
clip_limit = 1.0
beta_first = 0.9
beta_second = 0.95
adam_eps = 1e-08
rate_matrix = 0.05
rate_small = 0.5
decay_matrix = 0.1
score_scale = HD ** (-0.5)

WIDE = 256
ROWS = 64

CORE_SWAP = [(0, 1), (1, 0), (2, 3), (3, 2)]
Y_SWAP = [(0, 2), (2, 0), (1, 3), (3, 1)]
CYCLE = (0, 2, 4, 6, 7, 5, 3, 1)


def time_embed(timesteps):
    half_width = TE // 2
    frequency = jnp.exp(-math.log(10000.0) * jnp.arange(half_width, dtype=f32) / half_width)
    angles = 1000.0 * timesteps[:, None] * frequency[None, :]
    return jnp.concatenate([jnp.cos(angles), jnp.sin(angles)], axis=1)


def rms_parts(values):
    inverse = lax.rsqrt(jnp.mean(values * values, axis=-1, keepdims=True) + eps_norm)
    return (values * inverse, inverse)


def rms_back(normed, inverse, normed_grad):
    return inverse * (normed_grad - normed * jnp.mean(normed_grad * normed, axis=-1, keepdims=True))


def adam_update(weight, first, second, grad, clip, rate, decay):
    clipped = grad * clip
    first_new = beta_first * first + (1.0 - beta_first) * clipped
    second_new = beta_second * second + (1.0 - beta_second) * clipped * clipped
    first_hat = first_new / (1.0 - beta_first**ADAM_STEP)
    second_hat = second_new / (1.0 - beta_second**ADAM_STEP)
    weight_new = weight - rate * (first_hat / (jnp.sqrt(second_hat) + adam_eps) + decay * weight)
    return (weight_new, first_new, second_new)


def square_sum(values):
    return jnp.sum(values * values)


def dot(a, b, dims):
    return lax.dot_general(a, b, (dims, ((), ())), preferred_element_type=f32)


class Ring:
    def __init__(self, size):
        self.size = size
        self.ring = size == len(CYCLE)

    def hop(self, value, step, sends=None):
        n = self.size
        pairs = [(CYCLE[p], CYCLE[(p + step) % n]) for p in range(n) if sends is None or sends(p)]
        return lax.ppermute(value, "seq", pairs)

    def gather(self, own):
        if not self.ring:
            return [lax.all_gather(own, "seq", axis=0, tiled=True)]
        half = own.shape[0] // 2
        ahead, behind = [own], [own]
        for _ in range(3):
            ahead.append(self.hop(ahead[-1], 1))
            behind.append(self.hop(behind[-1], -1))
        far = [self.hop(behind[-1][:half], -1), self.hop(ahead[-1][half:], 1)]
        return behind + far + ahead[:0:-1]

    def reduce(self, step, first, active=None):
        def sends(k):
            if active is None:
                return None
            return lambda p: CYCLE[(p + k) % self.size] in active

        ahead, behind = first(4), first(5)
        for k in (3, 2, 1):
            ahead = step(k, self.hop(ahead, 1, sends(k + 1)))
            if k > 1:
                behind = step(9 - k, self.hop(behind, -1, sends(-k)))
        return step(0, self.hop(ahead, 1, sends(1)), self.hop(behind, -1, sends(-1)))

    def reduce_product(self, left, right):
        slab = left.shape[1] // self.size

        def block(k):
            return dot(left[:, k * slab : (k + 1) * slab], right, ((0,), (0,)))

        if not self.ring:
            blocks = jnp.concatenate([block(k).astype(bf16) for k in range(self.size)], 0)
            return lax.psum_scatter(blocks, "seq", scatter_dimension=0, tiled=True).astype(f32)

        def step(k, *moved):
            total = block(k)
            for one in moved:
                total = total + one.astype(f32)
            return total.astype(bf16) if k else total

        return self.reduce(step, step)


def butterfly(value, axis, size):
    step = 1
    while step < size:
        value = value + lax.ppermute(value, axis, [(i, i ^ step) for i in range(size)])
        step *= 2
    return value


def gather_tp(value, axis):
    tp = lax.axis_index("tp")

    def join(second, mine, other):
        low = jnp.where(second, other, mine)
        high = jnp.where(second, mine, other)
        return jnp.concatenate([low, high], axis)

    pair = join(tp % 2 == 1, value, lax.ppermute(value, "tp", CORE_SWAP))
    return join(tp >= 2, pair, lax.ppermute(pair, "tp", Y_SWAP))


def psum_tp(halves):
    mine, other = halves
    mine = (mine.astype(f32) + lax.ppermute(other, "tp", CORE_SWAP).astype(f32)).astype(bf16)
    mine = (mine.astype(f32) + lax.ppermute(mine, "tp", Y_SWAP).astype(f32)).astype(bf16)
    return (mine, lax.ppermute(mine, "tp", CORE_SWAP))


def exact_dot(a, b):
    return lax.dot_general(
        a, b, (((1,), (0,)), ((), ())), precision=highest, preferred_element_type=f32
    )


def anywhere():
    return pl.BlockSpec(memory_space=pl.ANY)


def whole(shape):
    return pl.BlockSpec(
        shape, lambda i, *_: (0,) * len(shape), pipeline_mode=pl.Buffered(1)
    )


def rows_block(block, width):
    return pl.BlockSpec((block, width), lambda i, *_: (i, 0))


def lanes_block(rows, block):
    return pl.BlockSpec((rows, block), lambda i, *_: (0, i))


def shape_of(shape, dtype):
    return jax.ShapeDtypeStruct(shape, dtype)


def call(kernel, name, grid, scalars, ins, outs, scratch=(), flops=0, moved=0, exps=0):
    return pl.pallas_call(
        kernel,
        out_shape=tuple(shape_of(shape, dtype) for shape, dtype, _ in outs),
        grid_spec=pltpu.PrefetchScalarGridSpec(
            num_scalar_prefetch=len(scalars),
            grid=(grid,),
            in_specs=[spec for _, spec in ins],
            out_specs=tuple(spec for _, _, spec in outs),
            scratch_shapes=list(scratch),
        ),
        cost_estimate=pl.CostEstimate(flops=flops, bytes_accessed=moved, transcendentals=exps),
        name=name,
    )(*scalars, *[array for array, _ in ins])


def starts_of(chunks):
    at = 0
    for chunk in chunks:
        yield at
        at += chunk.shape[0]


def chunk_copies(chunks, low, high, held, sems):
    return [
        pltpu.make_async_copy(
            chunk.at[:, low:high], held.at[start : start + chunk.shape[0], :], sems.at[j]
        )
        for j, (chunk, start) in enumerate(zip(chunks, starts_of(chunks)))
    ]


def relative_store(ring_size, ring, place, out_ref, value):
    slab = value.shape[1] // ring_size
    if not ring:
        out_ref[...] = value
        return
    for p in range(ring_size):

        @pl.when(place == p)
        def _(p=p):
            for k in range(ring_size):
                s = CYCLE[(p + k) % ring_size]
                out_ref[:, k * slab : (k + 1) * slab] = value[:, s * slab : (s + 1) * slab]


def absolute_store(ring_size, ring, place, out_ref, value):
    slab = value.shape[1] // ring_size
    if not ring:
        out_ref[...] = value
        return
    for p in range(ring_size):

        @pl.when(place == p)
        def _(p=p):
            for k in range(ring_size):
                s = CYCLE[(p + k) % ring_size]
                out_ref[:, s * slab : (s + 1) * slab] = value[:, k * slab : (k + 1) * slab]


def onehot_rows(segment_col):
    items = lax.broadcasted_iota(jnp.int32, (segment_col.shape[0], ITEMS), 1)
    return (segment_col == items).astype(f32)


def onehot_cols(segment_row):
    items = lax.broadcasted_iota(jnp.int32, (ITEMS, segment_row.shape[1]), 0)
    return (segment_row == items).astype(f32)


def modulate(onehot, mod_ref, block):
    return exact_dot(onehot, mod_ref[block * ITEMS : (block + 1) * ITEMS, :])


def enter_kernel(scal, x_ref, g_ref, mod_ref, gain_ref, sc_ref,
                 xr_ref, gr_ref, modr_ref, gainr_ref, hidden_ref, *, size, ring):
    place = scal[0]

    @pl.when(pl.program_id(0) == 0)
    def _():
        relative_store(size, ring, place, modr_ref, mod_ref[...])
        relative_store(size, ring, place, gainr_ref, gain_ref[...])

    relative_store(size, ring, place, xr_ref, x_ref[...])
    relative_store(size, ring, place, gr_ref, g_ref[...])
    x = xr_ref[...].astype(f32)
    normed, _ = rms_parts(x)
    onehot = onehot_rows(sc_ref[...])
    scale = modulate(onehot, modr_ref, 1)
    shift = modulate(onehot, modr_ref, 0)
    hidden_ref[...] = (normed * gainr_ref[0:1, :] * (1.0 + scale) + shift).astype(bf16)


def project_kernel(hidden_ref, *refs, heads, first_owner, count):
    chunks, (slab_ref, held, sems) = refs[:count], refs[count:]
    width = heads * HD
    copies = chunk_copies(chunks, 0, 3 * width, held, sems)
    for one in copies:
        one.start()
    for s in range(slab_ref.shape[0]):
        if not first_owner <= s < first_owner + heads:
            slab_ref[s] = jnp.zeros(slab_ref.shape[1:], bf16)
    for one in copies:
        one.wait()
    hidden = hidden_ref[...]
    for j in range(3):
        part = dot(hidden, held[:, j * width : (j + 1) * width], ((1,), (0,))).astype(bf16)
        if j == 0:
            part = part * jnp.asarray(score_scale, bf16)
        for h in range(heads):
            slab_ref[first_owner + h, :, j * HD : (j + 1) * HD] = part[:, h * HD : (h + 1) * HD]


def split_halves(core, full_ref, mine_ref, other_ref):
    half = mine_ref.shape[0]
    mine_ref[...] = full_ref[pl.ds(pl.multiple_of(core * half, half), half), :]
    other_ref[...] = full_ref[pl.ds(pl.multiple_of((1 - core) * half, half), half), :]


def join_halves(core, mine_ref, other_ref, full_ref):
    half = mine_ref.shape[0]
    full_ref[pl.ds(pl.multiple_of(core * half, half), half), :] = mine_ref[...]
    full_ref[pl.ds(pl.multiple_of((1 - core) * half, half), half), :] = other_ref[...]


def times_turned(value_ref, held, full_ref):
    tiles = held.shape[0] // WIDE

    def one(i, _):
        at = pl.ds(pl.multiple_of(i * WIDE, WIDE), WIDE)
        full_ref[:, at] = dot(value_ref[...], held[at, :], ((1,), (1,))).astype(bf16)
        return 0

    lax.fori_loop(0, tiles, one, 0)


def out_kernel(scal, slab_ref, *refs, heads, first_owner, count, low, high):
    chunks, (mixed_ref, mine_ref, other_ref, held, full, sems) = refs[:count], refs[count:]
    copies = chunk_copies(chunks, low, high, held, sems)
    for one in copies:
        one.start()
    for h in range(heads):
        mixed_ref[:, h * HD : (h + 1) * HD] = slab_ref[first_owner + h]
    for one in copies:
        one.wait()
    times_turned(mixed_ref, held, full)
    split_halves(scal[1], full, mine_ref, other_ref)


def qkv_back_kernel(scal, slab_ref, *refs, heads, first_owner, count):
    chunks, (grads_ref, mine_ref, other_ref, held, full, sems) = refs[:count], refs[count:]
    width = heads * HD
    copies = chunk_copies(chunks, 0, 3 * width, held, sems)
    for one in copies:
        one.start()
    for j in range(3):
        for h in range(heads):
            at = j * width + h * HD
            grads_ref[:, at : at + HD] = slab_ref[first_owner + h, :, j * HD : (j + 1) * HD]
    for one in copies:
        one.wait()
    times_turned(grads_ref, held, full)
    split_halves(scal[1], full, mine_ref, other_ref)


def ffn_kernel(scal, x_ref, g_ref, am_ref, ao_ref, modr_ref, gainr_ref, sc_ref, *refs,
               count, units):
    chunks = refs[:count]
    (mid_ref, hidden_ref, fgrad_ref, inner_ref, both_ref, hm_ref, ho_ref, fm_ref, fo_ref,
     held, attn, full, sems) = refs[count:]
    core = scal[1]
    copies = chunk_copies(chunks, 0, held.shape[1], held, sems)
    for one in copies:
        one.start()
    join_halves(core, am_ref, ao_ref, attn)

    def prepare(i, _):
        at = pl.ds(pl.multiple_of(i * ROWS, ROWS), ROWS)
        onehot = onehot_rows(sc_ref[at, :])
        x_mid = x_ref[at, :].astype(f32) + jnp.tanh(modulate(onehot, modr_ref, 2)) * attn[
            at, :
        ].astype(f32)
        mid_ref[at, :] = x_mid
        normed, _ = rms_parts(x_mid)
        scale = modulate(onehot, modr_ref, 4)
        shift = modulate(onehot, modr_ref, 3)
        hidden_ref[at, :] = (normed * gainr_ref[1:2, :] * (1.0 + scale) + shift).astype(bf16)
        tanh_ffn = jnp.tanh(modulate(onehot, modr_ref, 5))
        fgrad_ref[at, :] = (g_ref[at, :].astype(f32) * tanh_ffn).astype(bf16)
        return 0

    lax.fori_loop(0, x_ref.shape[0] // ROWS, prepare, 0)
    for one in copies:
        one.wait()

    def tile(i, _):
        def at(base):
            return pl.ds(pl.multiple_of(base + i * WIDE, WIDE), WIDE)

        gate_pre = dot(hidden_ref[...], held[:, at(0)], ((1,), (0,)))
        up_pre = dot(hidden_ref[...], held[:, at(units)], ((1,), (0,)))
        inner_grad = dot(fgrad_ref[...], held[:, at(2 * units)], ((1,), (0,)))
        sigmoid = jax.nn.sigmoid(gate_pre)
        silu = gate_pre * sigmoid
        inner_ref[:, at(0)] = (silu * up_pre).astype(bf16)
        both_ref[:, at(0)] = (
            inner_grad * up_pre * sigmoid * (1.0 + gate_pre * (1.0 - sigmoid))
        ).astype(bf16)
        both_ref[:, at(units)] = (inner_grad * silu).astype(bf16)
        return 0

    lax.fori_loop(0, units // WIDE, tile, 0)
    times_turned(both_ref, held.at[:, 0 : 2 * units], full)
    split_halves(core, full, hm_ref, ho_ref)
    times_turned(inner_ref, held.at[:, 2 * units : 3 * units], full)
    split_halves(core, full, fm_ref, fo_ref)


def mid_kernel(scal, mid_ref, g_ref, hm_ref, ho_ref, modr_ref, gainr_ref, sc_ref, *refs,
               heads, first_owner, count, low, high):
    chunks = refs[:count]
    grad_ref, agrad_ref, slab_ref, held, hgrad, sems = refs[count:]
    copies = chunk_copies(chunks, low, high, held, sems)
    for one in copies:
        one.start()
    join_halves(scal[1], hm_ref, ho_ref, hgrad)
    for s in range(slab_ref.shape[0]):
        if not first_owner <= s < first_owner + heads:
            slab_ref[s] = jnp.zeros(slab_ref.shape[1:], bf16)

    def prepare(i, _):
        at = pl.ds(pl.multiple_of(i * ROWS, ROWS), ROWS)
        onehot = onehot_rows(sc_ref[at, :])
        normed, inverse = rms_parts(mid_ref[at, :])
        scale = modulate(onehot, modr_ref, 4)
        normed_grad = hgrad[at, :].astype(f32) * gainr_ref[1:2, :] * (1.0 + scale)
        grad = g_ref[at, :].astype(f32) + rms_back(normed, inverse, normed_grad)
        grad_ref[at, :] = grad
        agrad_ref[at, :] = (grad * jnp.tanh(modulate(onehot, modr_ref, 2))).astype(bf16)
        return 0

    lax.fori_loop(0, mid_ref.shape[0] // ROWS, prepare, 0)
    for one in copies:
        one.wait()
    mixed = dot(agrad_ref[...], held[...], ((1,), (0,))).astype(bf16)
    for h in range(heads):
        slab_ref[first_owner + h] = mixed[:, h * HD : (h + 1) * HD]


def own_rows(core, mine_ref, other_ref):
    first = pl.program_id(0) < pl.num_programs(0) // 2
    mine = jnp.logical_xor(first, core == 1)
    return jnp.where(mine, mine_ref[...].astype(f32), other_ref[...].astype(f32))


def side_kernel(scal, mid_ref, grad_ref, g_ref, am_ref, ao_ref, fm_ref, fo_ref, hm_ref, ho_ref,
                modr_ref, gainr_ref, sc_ref, sr_ref,
                block_ref, sums_ref, gain_ref, *, size, ring):
    place, core = scal[0], scal[1]

    @pl.when(pl.program_id(0) == 0)
    def _():
        sums_ref[...] = jnp.zeros_like(sums_ref)
        gain_ref[...] = jnp.zeros_like(gain_ref)

    attn = own_rows(core, am_ref, ao_ref)
    ffn_out = own_rows(core, fm_ref, fo_ref)
    hgrad = own_rows(core, hm_ref, ho_ref)
    onehot = onehot_rows(sc_ref[...])
    by_item = onehot_cols(sr_ref[0])
    tanh_attn = jnp.tanh(modulate(onehot, modr_ref, 2))
    tanh_ffn = jnp.tanh(modulate(onehot, modr_ref, 5))
    scale = modulate(onehot, modr_ref, 4)
    x_mid = mid_ref[...]
    absolute_store(size, ring, place, block_ref, x_mid + tanh_ffn * ffn_out)
    normed, _ = rms_parts(x_mid)

    def add(block, value):
        sums_ref[block * ITEMS : (block + 1) * ITEMS, :] += exact_dot(by_item, value)

    add(0, grad_ref[...] * attn * (1.0 - tanh_attn * tanh_attn))
    add(1, hgrad)
    add(2, hgrad * normed * gainr_ref[1:2, :])
    add(3, g_ref[...].astype(f32) * ffn_out * (1.0 - tanh_ffn * tanh_ffn))
    gain_ref[0:1, :] += jnp.sum(hgrad * normed * (1.0 + scale), axis=0, keepdims=True)


def leave_kernel(scal, x_ref, grad_ref, hm_ref, ho_ref, modr_ref, gainr_ref, sc_ref, sr_ref,
                 early_ref, egain_ref, input_ref, sums_ref, gain_ref, total, turned, *, size, ring):
    place, core = scal[0], scal[1]

    @pl.when(pl.program_id(0) == 0)
    def _():
        total[...] = jnp.zeros_like(total)
        total[2 * ITEMS : 6 * ITEMS, :] = early_ref[...]
        total[6 * ITEMS + 1 : 6 * ITEMS + 2, :] = egain_ref[0:1, :]

    hgrad = own_rows(core, hm_ref, ho_ref)
    onehot = onehot_rows(sc_ref[...])
    by_item = onehot_cols(sr_ref[0])
    scale = modulate(onehot, modr_ref, 1)
    normed, inverse = rms_parts(x_ref[...].astype(f32))
    normed_grad = hgrad * gainr_ref[0:1, :] * (1.0 + scale)
    absolute_store(
        size, ring, place, input_ref, grad_ref[...] + rms_back(normed, inverse, normed_grad)
    )
    total[0:ITEMS, :] += exact_dot(by_item, hgrad)
    total[ITEMS : 2 * ITEMS, :] += exact_dot(by_item, hgrad * normed * gainr_ref[0:1, :])
    total[6 * ITEMS : 6 * ITEMS + 1, :] += jnp.sum(
        hgrad * normed * (1.0 + scale), axis=0, keepdims=True
    )

    @pl.when(pl.program_id(0) == pl.num_programs(0) - 1)
    def _():
        absolute_store(size, ring, place, turned, total[...])
        quarter = sums_ref.shape[1]
        at = pl.ds(pl.multiple_of(scal[2] * quarter, quarter), quarter)
        sums_ref[...] = turned[0 : 6 * ITEMS, at]
        gain_ref[...] = turned[6 * ITEMS : 6 * ITEMS + 8, :]


def text_heads_kernel(w_ref, out_ref):
    for h in range(out_ref.shape[0]):
        for j in range(2):
            out_ref[h, :, j * HD : (j + 1) * HD] = w_ref[j, :, h * HD : (h + 1) * HD].astype(bf16)


def text_step_kernel(head_of, cap_ref, w_ref, *refs):
    total = dot(cap_ref[...], w_ref[0], ((1,), (0,)))
    for moved in refs[:-1]:
        total = total + moved[...].astype(f32)
    refs[-1][...] = total.astype(refs[-1].dtype)


def mod_kernel(scal, embed_ref, w_ref, out_ref):
    out_ref[...] = dot(embed_ref[...], w_ref[...].astype(bf16), ((1,), (0,)))


def text_join_kernel(head_at, low_ref, high_ref, k_ref, v_ref):
    for j, ref in enumerate((low_ref, high_ref)):
        k_ref[:, j * HD : (j + 1) * HD] = ref[0, :, :HD]
        v_ref[:, j * HD : (j + 1) * HD] = ref[0, :, HD:]


def turned_copy(source_ref, low, out_ref, block):
    def one(j, _):
        at = pl.ds(pl.multiple_of(j * block, block), block)
        out_ref[:, at] = jnp.transpose(source_ref[at, low : low + HD].astype(f32)).astype(bf16)
        return 0

    lax.fori_loop(0, source_ref.shape[0] // block, one, 0)


def self_kernel(table, q_ref, all_ref, sq_ref, sk_ref, out_ref, stat_ref, k_ref, vt_ref, *, block_k):
    i = pl.program_id(0)

    @pl.when(i == 0)
    def _():
        k_ref[...] = all_ref[:, HD : 2 * HD]
        turned_copy(all_ref, 2 * HD, vt_ref, block_k)

    q = q_ref[:, :HD]
    item_of_q = sq_ref[...]
    width = q.shape[0]

    def step(j, carry):
        top, total, out = carry
        at = pl.ds(pl.multiple_of(j * block_k, block_k), block_k)
        scores = dot(k_ref[at, :], q, ((1,), (1,)))
        scores = jnp.where(sk_ref[at, :] == item_of_q, scores, masked_score)
        new_top = jnp.maximum(top, jnp.max(scores, axis=0, keepdims=True))
        weights = jnp.exp(scores - new_top)
        shrink = jnp.exp(top - new_top)
        total = total * shrink + jnp.sum(weights, axis=0, keepdims=True)
        out = out * shrink + dot(vt_ref[:, at], weights.astype(bf16), ((1,), (0,)))
        return (new_top, total, out)

    start = (
        jnp.full((1, width), lowest_max, f32),
        jnp.zeros((1, width), f32),
        jnp.zeros((HD, width), f32),
    )
    top, total, out = lax.fori_loop(table[0, i], table[1, i], step, start)
    out_ref[...] = out / total
    stat_ref[...] = top + jnp.log(total)


def text_kernel(table, gate, q_ref, kv_ref, self_ref, sq_ref,
                mixed_ref, out_ref, stat_ref, k_ref, vt_ref):
    i = pl.program_id(0)

    @pl.when(i == 0)
    def _():
        k_ref[...] = kv_ref[:, :HD]
        turned_copy(kv_ref, HD, vt_ref, TEXT)

    q = q_ref[:, :HD]
    item_of_q = sq_ref[...]

    def step(item, carry):
        out, stat = carry
        at = pl.ds(pl.multiple_of(item * TEXT, TEXT), TEXT)
        scores = dot(k_ref[at, :], q, ((1,), (1,)))
        top = jnp.max(scores, axis=0, keepdims=True)
        weights = jnp.exp(scores - top)
        total = jnp.sum(weights, axis=0, keepdims=True)
        probs = (weights / total).astype(bf16)
        part = dot(vt_ref[:, at], probs, ((1,), (0,)))
        here = item_of_q == item
        return (jnp.where(here, part, out), jnp.where(here, top + jnp.log(total), stat))

    start = (jnp.zeros((HD, q.shape[0]), f32), jnp.zeros((1, q.shape[0]), f32))
    text_out, stat = lax.fori_loop(table[2, i], table[3, i], step, start)
    out_ref[...] = text_out
    stat_ref[...] = stat
    mixed_ref[...] = jnp.transpose(self_ref[...] + gate[0] * text_out).astype(bf16)


def text_back_kernel(table, gate, q_ref, g_ref, kv_ref, text_ref, stat_ref, sq_ref,
                     dkv_ref, dq_ref, cross_ref, k_ref, v_ref, kt_ref, dk_sum, dv_sum):
    i = pl.program_id(0)

    @pl.when(i == 0)
    def _():
        k_ref[...] = kv_ref[:, :HD]
        v_ref[...] = kv_ref[:, HD:]
        turned_copy(kv_ref, 0, kt_ref, TEXT)
        dk_sum[...] = jnp.zeros_like(dk_sum)
        dv_sum[...] = jnp.zeros_like(dv_sum)

    q = q_ref[:, :HD]
    item_of_q = sq_ref[...]
    g_value = g_ref[...].astype(f32)
    g = (g_value * gate[0]).astype(bf16)
    text_out = text_ref[...]
    cross_ref[...] = jnp.sum(jnp.transpose(g_value) * text_out, axis=0, keepdims=True)
    delta = jnp.sum(jnp.transpose(g.astype(f32)) * text_out, axis=0, keepdims=True)
    stat = stat_ref[...]

    def step(item, total):
        at = pl.ds(pl.multiple_of(item * TEXT, TEXT), TEXT)
        scores = dot(k_ref[at, :], q, ((1,), (1,)))
        probs = jnp.exp(jnp.where(item_of_q == item, scores - stat, masked_score))
        prob_grad = dot(v_ref[at, :], g, ((1,), (1,)))
        score_grad = (probs * (prob_grad - delta)).astype(bf16)
        dk_sum[at, :] += dot(score_grad, q, ((1,), (0,)))
        dv_sum[at, :] += dot(probs.astype(bf16), g, ((1,), (0,)))
        return total + dot(kt_ref[:, at], score_grad, ((1,), (0,)))

    start = jnp.zeros((HD, q.shape[0]), f32)
    dq_ref[...] = lax.fori_loop(table[2, i], table[3, i], step, start)

    @pl.when(i == pl.num_programs(0) - 1)
    def _():
        dkv_ref[:, :HD] = dk_sum[...].astype(bf16)
        dkv_ref[:, HD:] = dv_sum[...].astype(bf16)


def self_back_kernel(table, q_ref, g_ref, all_ref, self_ref, stat_ref, start_ref, sq_ref, sk_ref,
                     dqkv_ref, k_ref, v_ref, kt_ref, dk_sum, dv_sum, *, block_k):
    i = pl.program_id(0)

    @pl.when(i == 0)
    def _():
        k_ref[...] = all_ref[:, HD : 2 * HD]
        v_ref[...] = all_ref[:, 2 * HD :]
        turned_copy(all_ref, HD, kt_ref, block_k)
        dk_sum[...] = jnp.zeros_like(dk_sum)
        dv_sum[...] = jnp.zeros_like(dv_sum)

    q = q_ref[:, :HD]
    g = g_ref[...]
    item_of_q = sq_ref[...]
    delta = jnp.sum(jnp.transpose(g.astype(f32)) * self_ref[...], axis=0, keepdims=True)
    stat = stat_ref[...]

    def step(j, total):
        at = pl.ds(pl.multiple_of(j * block_k, block_k), block_k)
        scores = dot(k_ref[at, :], q, ((1,), (1,)))
        allowed = sk_ref[at, :] == item_of_q
        probs = jnp.exp(jnp.where(allowed, scores - stat, masked_score))
        prob_grad = dot(v_ref[at, :], g, ((1,), (1,)))
        score_grad = (probs * (prob_grad - delta)).astype(bf16)
        dk_sum[at, :] += dot(score_grad, q, ((1,), (0,)))
        dv_sum[at, :] += dot(probs.astype(bf16), g, ((1,), (0,)))
        return total + dot(kt_ref[:, at], score_grad, ((1,), (0,)))

    total = lax.fori_loop(table[0, i], table[1, i], step, start_ref[...])
    rows = q.shape[0]
    dqkv_ref[pl.ds(pl.multiple_of(i * rows, rows), rows), :HD] = jnp.transpose(
        total * score_scale
    ).astype(bf16)

    @pl.when(i == pl.num_programs(0) - 1)
    def _():
        dqkv_ref[:, HD : 2 * HD] = dk_sum[...].astype(bf16)
        dqkv_ref[:, 2 * HD :] = dv_sum[...].astype(bf16)


def attention_table(segments, block_q, block_k):
    by_block = segments.reshape(-1, block_q)
    low_item, high_item = by_block[:, 0], by_block[:, -1]
    first_key = jnp.sum(segments[None, :] < low_item[:, None], axis=1)
    end_key = jnp.sum(segments[None, :] <= high_item[:, None], axis=1)
    return jnp.stack(
        [first_key // block_k, (end_key + block_k - 1) // block_k, low_item, high_item + 1]
    ).astype(jnp.int32)


def per_device(
    x_tokens, caption, timesteps, segment_ids, out_grad,
    mod_weight, mod_first, mod_second,
    norm_gains, gains_first, gains_second,
    qkv_weight, qkv_first, qkv_second,
    out_weight, out_first, out_second,
    text_weight, text_first, text_second,
    cross_gates, cross_first, cross_second,
    updown_weight, updown_first, updown_second,
    down_weight, down_first, down_second,
    *, seq_size, tp_size,
):
    seq_index = lax.axis_index("seq")
    tp_index = lax.axis_index("tp")
    ring = Ring(seq_size)
    here, width = x_tokens.shape
    heads = cross_gates.shape[0]
    local_width = heads * HD
    count = here * seq_size
    units = down_weight.shape[0]
    quarter = width // tp_size
    first_owner = 1 if seq_size >= heads + 2 else 0
    owners = range(first_owner, first_owner + heads)
    seqs = jnp.full((seq_size,), seq_index)
    place = jnp.where(seqs % 2 == 0, seqs // 2, (15 - seqs) // 2)
    places = (place + jnp.arange(seq_size)) % seq_size
    slab_owner = jnp.where(places < 4, 2 * places, 15 - 2 * places)
    slab_head = jnp.clip(slab_owner - first_owner, 0, heads - 1)
    my_head = jnp.clip(seq_index - first_owner, 0, heads - 1)
    is_owner = (seq_index >= first_owner) & (seq_index < first_owner + heads)
    tps = jnp.full((1,), tp_index)
    scal = jnp.concatenate([place[:1], tps % 2, tps]).astype(jnp.int32)
    which = {"size": seq_size, "ring": ring.ring}

    def exchange(slabs):
        return lax.all_to_all(slabs, "seq", 0, 0, tiled=True)

    silu_embed = jax.nn.silu(time_embed(timesteps)).astype(bf16)
    mod_rows = mod_weight.shape[0]
    embed_rows = lax.dynamic_slice_in_dim(silu_embed, seq_index * mod_rows, mod_rows, 1)
    mod_part = call(
        mod_kernel, "modulation", 6, [scal],
        [
            (embed_rows, whole((ITEMS, mod_rows))),
            (mod_weight, pl.BlockSpec((mod_rows, quarter), lambda i, s: (0, i * tp_size + s[2]))),
        ],
        [((6 * ITEMS, quarter), f32, rows_block(ITEMS, quarter))],
        moved=mod_rows * 6 * quarter * 4, flops=2 * ITEMS * mod_rows * 6 * quarter,
    )[0]
    is_here = jnp.arange(seq_size) == seq_index
    slots = jnp.where(is_here[:, None], segment_ids.astype(f32)[None, :], 0.0).reshape(-1)
    gain_cols = norm_gains.shape[1]
    gain_slots = jnp.where(is_here[None, :, None], norm_gains[:, None, :], 0.0).reshape(-1)
    spare = -(slots.size + gain_slots.size) % (8 * quarter)
    packed = jnp.concatenate([slots, gain_slots, jnp.zeros((spare,), f32)]).reshape(-1, quarter)
    packed = butterfly(jnp.concatenate([mod_part, packed]), "seq", seq_size)
    modulation = gather_tp(packed[: 6 * ITEMS], 1)
    packed = packed[6 * ITEMS :].reshape(-1)
    segments = packed[:count].astype(jnp.int32)
    gains_value = packed[count : count + 2 * width].reshape(2, width).astype(bf16).astype(f32)
    gains_value = jnp.concatenate([gains_value] * 4)

    def turned(shard):
        return jnp.transpose(shard.astype(bf16), (1, 0, 2)).reshape(shard.shape[1], -1)

    attn_chunks = ring.gather(
        jnp.concatenate([turned(qkv_weight), out_weight.astype(bf16).T], axis=1)
    )
    pieces = len(attn_chunks)
    piece_sems = pltpu.SemaphoreType.DMA((pieces,))
    attn_ins = [(chunk, anywhere()) for chunk in attn_chunks]
    qkv_width = 3 * local_width

    cap_rows = caption.shape[0]
    cap_cols = caption.shape[1] // seq_size
    cap_part = cap_cols // tp_size
    text_rows = cap_rows * seq_size
    if cap_part % 128 == 0:
        cap_own = call(
            lambda scal, in_ref, out_ref: out_ref.__setitem__(0, in_ref[...]),
            "caption_slabs", seq_size, [scal],
            [(caption, pl.BlockSpec((cap_rows, cap_part), lambda i, s: (0, i * tp_size + s[2])))],
            [
                (
                    (seq_size, cap_rows, cap_part), bf16,
                    pl.BlockSpec((1, cap_rows, cap_part), lambda i, s: (i, 0, 0)),
                )
            ],
            moved=2 * cap_rows * cap_cols * 4,
        )[0]
    else:
        cap_own = lax.dynamic_index_in_dim(
            caption.reshape(cap_rows, seq_size, tp_size, cap_part), tp_index, 2, keepdims=False
        )
        cap_own = jnp.transpose(cap_own, (1, 0, 2))
    caption_cols = gather_tp(exchange(cap_own).reshape(text_rows, cap_part), 1)
    text_by_head = call(
        text_heads_kernel, "text_heads", 1, [],
        [(text_weight, whole(text_weight.shape))],
        [((heads, cap_cols, 2 * HD), bf16, whole((heads, cap_cols, 2 * HD)))],
        moved=text_weight.size * 6,
    )[0]
    text_block = math.gcd(text_rows, 512)

    def text_step(k, *moved):
        block = rows_block(text_block, 2 * HD)
        return call(
            text_step_kernel, "text_step", text_rows // text_block, [slab_head],
            [
                (caption_cols, rows_block(text_block, cap_cols)),
                (
                    text_by_head,
                    pl.BlockSpec((1, cap_cols, 2 * HD), lambda i, head_of: (head_of[k], 0, 0)),
                ),
            ]
            + [(one, block) for one in moved],
            [((text_rows, 2 * HD), bf16, block)],
            moved=text_rows * cap_cols * 2, flops=4 * text_rows * cap_cols * HD,
        )[0]

    if ring.ring:
        text_kv = ring.reduce(text_step, text_step, owners)
    else:
        parts = jnp.einsum("rc,hcw->hrw", caption_cols, text_by_head, preferred_element_type=f32)
        after = seq_size - heads - first_owner
        parts = jnp.pad(parts.astype(bf16), ((first_owner, after), (0, 0), (0, 0)))
        text_kv = lax.psum_scatter(parts, "seq", scatter_dimension=0, tiled=False)

    ffn_chunks = ring.gather(
        jnp.concatenate([turned(updown_weight), down_weight.astype(bf16).T], axis=1)
    )
    ffn_ins = [(chunk, anywhere()) for chunk in ffn_chunks]

    segment_col = segment_ids[:, None]
    steps = here // ROWS
    segment_row = segment_ids.reshape(steps, 1, ROWS)
    row_ins = [
        (segment_col, rows_block(ROWS, 1)),
        (segment_row, pl.BlockSpec((1, 1, ROWS), lambda i, *_: (i, 0, 0))),
    ]
    block = rows_block(ROWS, width)
    mod_shape, gain_shape = modulation.shape, gains_value.shape
    x_rel, g_rel, mod_rel, gain_rel, hidden_attn = call(
        functools.partial(enter_kernel, **which), "enter", steps, [scal],
        [
            (x_tokens, block), (out_grad, block), (modulation, whole(mod_shape)),
            (gains_value, whole(gain_shape)), row_ins[0],
        ],
        [
            ((here, width), bf16, block), ((here, width), bf16, block),
            (mod_shape, f32, whole(mod_shape)), (gain_shape, f32, whole(gain_shape)),
            ((here, width), bf16, block),
        ],
        moved=here * width * 10,
    )
    mod_ins = [(mod_rel, whole(mod_shape)), (gain_rel, whole(gain_shape))]
    full_ins = mod_ins + [(segment_col, whole((here, 1)))]
    slab_shape = (seq_size, here, 3 * HD)
    slabs = call(
        functools.partial(
            project_kernel, heads=heads, first_owner=first_owner, count=pieces
        ),
        "project", 1, [],
        [(hidden_attn, whole((here, width)))] + attn_ins,
        [(slab_shape, bf16, whole(slab_shape))],
        [pltpu.VMEM((width, qkv_width), bf16), piece_sems],
        moved=width * qkv_width * 2, flops=2 * here * width * qkv_width,
    )[0]
    qkv_head = exchange(slabs).reshape(count, 3 * HD)

    block_q = math.gcd(count, 512)
    block_k = math.gcd(count, 512)
    table = attention_table(segments, block_q, block_k)
    tanh_cross = jnp.tanh(cross_gates)
    my_gate = jnp.sum(jnp.where(jnp.arange(heads) == my_head, tanh_cross, 0.0)).reshape(1)
    blocks = count // block_q
    q_ins = [(qkv_head, rows_block(block_q, 3 * HD))]
    seg_row = (segments[None, :], lanes_block(1, block_q))
    seg_col = (segments[:, None], whole((count, 1)))
    turned_out = ((HD, count), f32, lanes_block(HD, block_q))
    stat_out = ((1, count), f32, lanes_block(1, block_q))
    area = count * count * HD
    self_out, stat = call(
        functools.partial(self_kernel, block_k=block_k), "attend", blocks, [table],
        q_ins + [(qkv_head, whole(qkv_head.shape)), seg_row, seg_col],
        [turned_out, stat_out],
        [pltpu.VMEM((count, HD), bf16), pltpu.VMEM((HD, count), bf16)],
        flops=4 * area, moved=count * HD * 20, exps=count * count,
    )
    mixed_head, text_out, text_stat = call(
        text_kernel, "attend_text", blocks, [table, my_gate],
        q_ins
        + [(text_kv, whole(text_kv.shape)), (self_out, lanes_block(HD, block_q)), seg_row],
        [((count, HD), bf16, rows_block(block_q, HD)), turned_out, stat_out],
        [pltpu.VMEM((text_rows, HD), bf16), pltpu.VMEM((HD, text_rows), bf16)],
        flops=4 * count * TEXT * HD, moved=count * HD * 20, exps=count * TEXT,
    )
    mixed_slabs = exchange(mixed_head.reshape(seq_size, here, HD))
    low, high = qkv_width, qkv_width + local_width
    head_args = {"heads": heads, "first_owner": first_owner, "count": pieces}
    half_shape = (here // 2, width)
    half_out = (half_shape, bf16, whole(half_shape))
    slab64 = (seq_size, here, HD)
    held_out = [pltpu.VMEM((width, local_width), bf16)]
    full_sum = [pltpu.VMEM((here, width), bf16), piece_sems]
    mixed, *attn = call(
        functools.partial(out_kernel, low=low, high=high, **head_args), "out", 1, [scal],
        [(mixed_slabs, whole(slab64))] + attn_ins,
        [((here, local_width), bf16, whole((here, local_width))), half_out, half_out],
        held_out + full_sum,
        moved=width * local_width * 2, flops=2 * here * width * local_width,
    )
    attn = psum_tp(attn)

    def halves(pair, spec=None):
        return [(one, spec or whole(half_shape)) for one in pair]

    tokens = (here, width)
    x_mid, hidden_ffn, ffn_grad, inner, both_grads, hm, ho, fm, fo = call(
        functools.partial(ffn_kernel, count=pieces, units=units), "ffn", 1, [scal],
        [(x_rel, whole(tokens)), (g_rel, whole(tokens))] + halves(attn) + full_ins + ffn_ins,
        [
            (tokens, f32, whole(tokens)), (tokens, bf16, whole(tokens)),
            (tokens, bf16, whole(tokens)), ((here, units), bf16, whole((here, units))),
            ((here, 2 * units), bf16, whole((here, 2 * units))),
            half_out, half_out, half_out, half_out,
        ],
        [pltpu.VMEM((width, 3 * units), bf16), pltpu.VMEM(tokens, bf16)] + full_sum,
        moved=width * 3 * units * 2, flops=12 * here * width * units,
    )
    hgrad = psum_tp((hm, ho))
    ffn_out = psum_tp((fm, fo))
    down_owned = ring.reduce_product(ffn_grad, inner)
    updown_rows = ring.reduce_product(hidden_ffn, both_grads)

    mid_grad, attn_grad, grad_slabs = call(
        functools.partial(mid_kernel, low=low, high=high, **head_args), "mid", 1, [scal],
        [(x_mid, whole(tokens)), (g_rel, whole(tokens))] + halves(hgrad) + full_ins + attn_ins,
        [(tokens, f32, whole(tokens)), (tokens, bf16, whole(tokens)), (slab64, bf16, whole(slab64))],
        held_out + full_sum,
        moved=width * local_width * 2, flops=2 * here * width * local_width,
    )
    head_grad = exchange(grad_slabs).reshape(count, HD)
    out_owned = ring.reduce_product(attn_grad, mixed)
    half_block = pl.BlockSpec((ROWS, width), lambda i, *_: (i % (steps // 2), 0))
    sums_shape, one_gain = (4 * ITEMS, width), (8, width)
    block_out, early_sums, early_gain = call(
        functools.partial(side_kernel, **which), "side", steps, [scal],
        [(x_mid, block), (mid_grad, block), (g_rel, block)]
        + halves(attn, half_block) + halves(ffn_out, half_block) + halves(hgrad, half_block)
        + mod_ins + row_ins,
        [(tokens, f32, block), (sums_shape, f32, whole(sums_shape)), (one_gain, f32, whole(one_gain))],
        moved=here * width * 24,
    )

    g_ins = [(head_grad, rows_block(block_q, HD))]
    kv64 = pltpu.VMEM((text_rows, HD), bf16)
    text_dkv, text_dq, cross_rows = call(
        text_back_kernel, "attend_text_back", blocks, [table, my_gate],
        q_ins + g_ins
        + [
            (text_kv, whole(text_kv.shape)), (text_out, lanes_block(HD, block_q)),
            (text_stat, lanes_block(1, block_q)), seg_row,
        ],
        [((text_rows, 2 * HD), bf16, whole((text_rows, 2 * HD))), turned_out, stat_out],
        [kv64, kv64, pltpu.VMEM((HD, text_rows), bf16)] + [pltpu.VMEM((text_rows, HD), f32)] * 2,
        flops=10 * count * TEXT * HD, moved=count * HD * 20, exps=count * TEXT,
    )
    head64 = pltpu.VMEM((count, HD), bf16)
    dqkv = call(
        functools.partial(self_back_kernel, block_k=block_k), "attend_back", blocks, [table],
        q_ins + g_ins
        + [
            (qkv_head, whole(qkv_head.shape)), (self_out, lanes_block(HD, block_q)),
            (stat, lanes_block(1, block_q)), (text_dq, lanes_block(HD, block_q)), seg_row, seg_col,
        ],
        [(qkv_head.shape, bf16, whole(qkv_head.shape))],
        [head64, head64, pltpu.VMEM((HD, count), bf16)] + [pltpu.VMEM((count, HD), f32)] * 2,
        flops=10 * area, moved=count * HD * 20, exps=count * count,
    )[0]

    text_grads = ring.gather(text_dkv)
    text_grads = jnp.concatenate(text_grads, axis=0).reshape(seq_size, text_rows, 2 * HD)
    head_at = jnp.argmax(
        (slab_owner if ring.ring else jnp.arange(seq_size))[None, :]
        == jnp.arange(first_owner, first_owner + heads)[:, None], axis=1,
    ).astype(jnp.int32)
    pair_block = pl.BlockSpec((text_rows, 2 * HD), lambda i, at: (0, i))
    text_grad_keys, text_grad_values = call(
        text_join_kernel, "text_join", heads // 2, [head_at],
        [
            (text_grads, pl.BlockSpec((1, text_rows, 2 * HD), lambda i, at: (at[2 * i], 0, 0))),
            (text_grads, pl.BlockSpec((1, text_rows, 2 * HD), lambda i, at: (at[2 * i + 1], 0, 0))),
        ],
        [((text_rows, local_width), bf16, pair_block)] * 2,
        moved=text_rows * local_width * 8,
    )
    text_owned = jnp.stack(
        [dot(caption_cols, one, ((0,), (0,))) for one in (text_grad_keys, text_grad_values)]
    )

    back_slabs = exchange(dqkv.reshape(slab_shape))
    qkv_grads, *hidden_grad = call(
        functools.partial(qkv_back_kernel, **head_args), "qkv_back", 1, [scal],
        [(back_slabs, whole(slab_shape))] + attn_ins,
        [((here, qkv_width), bf16, whole((here, qkv_width))), half_out, half_out],
        [pltpu.VMEM((width, qkv_width), bf16)] + full_sum,
        moved=width * qkv_width * 2, flops=2 * here * width * qkv_width,
    )
    qkv_rows = ring.reduce_product(hidden_attn, qkv_grads)
    hidden_grad = psum_tp(hidden_grad)
    all_sums = (6 * ITEMS, quarter)
    input_grad, item_sums, gain_sums = call(
        functools.partial(leave_kernel, **which), "leave", steps, [scal],
        [(x_rel, block), (mid_grad, block)] + halves(hidden_grad, half_block) + mod_ins + row_ins
        + [(early_sums, whole(sums_shape)), (early_gain, whole(one_gain))],
        [(tokens, f32, block), (all_sums, f32, whole(all_sums)), (one_gain, f32, whole(one_gain))],
        [pltpu.VMEM((6 * ITEMS + 8, width), f32)] * 2,
        moved=here * width * 16,
    )

    cross_here = jnp.where(
        is_owner & (jnp.arange(quarter) == my_head), jnp.sum(cross_rows), 0.0
    )
    packed = jnp.concatenate(
        [
            item_sums, gain_sums[:2].reshape(-1, quarter), cross_here[None],
            jnp.zeros((-(2 * tp_size + 1) % 8, quarter), f32),
        ]
    )
    packed = butterfly(packed, "seq", seq_size)
    item_mod_low = packed[: 6 * ITEMS].astype(bf16)
    gain_grads = packed[6 * ITEMS : 6 * ITEMS + 2 * tp_size].reshape(2, seq_size, gain_cols)
    gains_owned = jnp.sum(jnp.where(is_here[None, :, None], gain_grads, 0.0), axis=1)
    cross_total = packed[6 * ITEMS + 2 * tp_size, :heads] * (1.0 - tanh_cross * tanh_cross)

    def by_block(sums):
        return jnp.transpose(sums.reshape(6, ITEMS, -1), (1, 0, 2)).reshape(ITEMS, -1)

    mod_weight_grad = dot(embed_rows, by_block(gather_tp(item_mod_low, 1)), ((0,), (0,)))
    mod_quarter_grad = dot(embed_rows, by_block(item_mod_low), ((0,), (0,)))

    owned_square = (
        square_sum(qkv_rows)
        + square_sum(out_owned)
        + square_sum(text_owned)
        + square_sum(updown_rows)
        + square_sum(down_owned)
        + square_sum(mod_quarter_grad)
    )
    owned_square = owned_square + jnp.where(tp_index == 0, square_sum(gains_owned), 0.0)
    owned_square = owned_square + jnp.where(seq_index == 0, square_sum(cross_total), 0.0)
    total_square = jnp.full((8, 128), owned_square)
    total_square = butterfly(butterfly(total_square, "tp", tp_size), "seq", seq_size)[0, 0]
    grad_norm = jnp.sqrt(total_square)
    clip = jnp.minimum(1.0, clip_limit / (grad_norm + 1e-06))

    def unturned(rows, blocks):
        return jnp.transpose(rows.reshape(rows.shape[0], blocks, -1), (1, 0, 2))

    matrix = functools.partial(adam_update, clip=clip, rate=rate_matrix, decay=decay_matrix)
    small = functools.partial(adam_update, clip=clip, rate=rate_small, decay=0.0)
    return (
        block_out,
        input_grad,
        grad_norm,
        *matrix(mod_weight, mod_first, mod_second, mod_weight_grad),
        *small(norm_gains, gains_first, gains_second, gains_owned),
        *matrix(qkv_weight, qkv_first, qkv_second, unturned(qkv_rows, 3)),
        *matrix(out_weight, out_first, out_second, out_owned.T),
        *matrix(text_weight, text_first, text_second, text_owned),
        *small(cross_gates, cross_first, cross_second, cross_total),
        *matrix(updown_weight, updown_first, updown_second, unturned(updown_rows, 2)),
        *matrix(down_weight, down_first, down_second, down_owned.T),
    )


def solution(mesh):
    rows = P("seq", None)
    cols = P(None, "seq")
    split = P(None, "seq", "tp")
    turned = P("tp", "seq")
    heads = P("tp")
    weights = (rows,) * 3 + (cols,) * 3 + (split,) * 3 + (turned,) * 3 + (split,) * 3
    weights = weights + (heads,) * 3 + (split,) * 3 + (turned,) * 3
    return jax.shard_map(
        functools.partial(per_device, seq_size=mesh.shape["seq"], tp_size=mesh.shape["tp"]),
        mesh=mesh,
        in_specs=(rows, rows, P(), P("seq"), rows) + weights,
        out_specs=(rows, rows, P()) + weights,
        check_vma=False,
    )
```

```python
import functools
import math

import jax
import jax.numpy as jnp
from jax import lax
from jax.experimental import pallas as pl
from jax.experimental.pallas import tpu as pltpu
from jax.sharding import PartitionSpec as P

HD = 64
TE = 1024
TEXT = 256
ITEMS = 8
ADAM_STEP = 10

bf16 = jnp.bfloat16
f32 = jnp.float32
highest = lax.Precision.HIGHEST
eps_norm = 1e-06
masked_score = -1e30
lowest_max = -1e20
clip_limit = 1.0
beta_first = 0.9
beta_second = 0.95
adam_eps = 1e-08
rate_matrix = 0.05
rate_small = 0.5
decay_matrix = 0.1
score_scale = HD ** (-0.5)

WIDE = 256
ROWS = 64

CORE_SWAP = [(0, 1), (1, 0), (2, 3), (3, 2)]
Y_SWAP = [(0, 2), (2, 0), (1, 3), (3, 1)]
CYCLE = (0, 2, 4, 6, 7, 5, 3, 1)


def time_embed(timesteps):
    half_width = TE // 2
    frequency = jnp.exp(-math.log(10000.0) * jnp.arange(half_width, dtype=f32) / half_width)
    angles = 1000.0 * timesteps[:, None] * frequency[None, :]
    return jnp.concatenate([jnp.cos(angles), jnp.sin(angles)], axis=1)


def rms_parts(values):
    inverse = lax.rsqrt(jnp.mean(values * values, axis=-1, keepdims=True) + eps_norm)
    return (values * inverse, inverse)


def rms_back(normed, inverse, normed_grad):
    return inverse * (normed_grad - normed * jnp.mean(normed_grad * normed, axis=-1, keepdims=True))


def adam_update(weight, first, second, grad, clip, rate, decay):
    clipped = grad * clip
    first_new = beta_first * first + (1.0 - beta_first) * clipped
    second_new = beta_second * second + (1.0 - beta_second) * clipped * clipped
    first_hat = first_new / (1.0 - beta_first**ADAM_STEP)
    second_hat = second_new / (1.0 - beta_second**ADAM_STEP)
    weight_new = weight - rate * (first_hat / (jnp.sqrt(second_hat) + adam_eps) + decay * weight)
    return (weight_new, first_new, second_new)


def square_sum(values):
    return jnp.sum(values * values)


def dot(a, b, dims):
    return lax.dot_general(a, b, (dims, ((), ())), preferred_element_type=f32)


class Ring:
    def __init__(self, size):
        self.size = size
        self.ring = size == len(CYCLE)

    def hop(self, value, step, sends=None):
        n = self.size
        pairs = [(CYCLE[p], CYCLE[(p + step) % n]) for p in range(n) if sends is None or sends(p)]
        return lax.ppermute(value, "seq", pairs)

    def gather(self, own, held=((), (), ())):
        if not self.ring:
            return [lax.all_gather(own, "seq", axis=0, tiled=True)]
        half = own.shape[0] // 2
        ahead, behind = [own], [own]
        for i in range(3):
            ahead.append(self.hop(ahead[-1], 1))
            behind.append(self.hop(behind[-1], -1))
            if held[i]:
                ahead[-1], behind[-1] = lax.optimization_barrier(
                    (ahead[-1], behind[-1], *held[i])
                )[:2]
        far = [self.hop(behind[-1][:half], -1), self.hop(ahead[-1][half:], 1)]
        return behind + far + ahead[:0:-1]

    def reduce(self, block, active=None):
        rows = block(0).shape[0]
        half = rows // 2

        def sends(k):
            if active is None:
                return None
            return lambda p: CYCLE[(p + k) % self.size] in active

        def wait(held, *values):
            return lax.optimization_barrier((*values, *held))[: len(values)] if held else values

        def plus(part, moved):
            return (part.astype(f32) + moved.astype(f32)).astype(bf16)

        ahead, behind = block(4)[:half], block(4)[half:]
        for k in (3, 2, 1, 0):
            sent = (ahead, behind)
            ahead = self.hop(ahead, 1, sends(k + 1))
            behind = self.hop(behind, -1, sends(-k - 1))
            ahead, behind = wait((yield sent), ahead, behind)
            if k == 3:
                near, far = block(3), block(5)
                ahead = jnp.concatenate([plus(near[:half], ahead), near[half:]])
                behind = jnp.concatenate([far[:half], plus(far[half:], behind)])
            elif k:
                ahead, behind = plus(block(k), ahead), plus(block(8 - k), behind)
        yield block(0).astype(f32) + ahead.astype(f32) + behind.astype(f32)

    def reduce_products(self, pairs):
        parts = [dot(left, right, ((0,), (0,))).astype(bf16) for left, right in pairs]
        widths = [part.shape[1] for part in parts]
        edges = [sum(widths[:i]) for i in range(len(widths) + 1)]
        slab = parts[0].shape[0] // self.size

        def split(rows):
            return [rows[:, low:high] for low, high in zip(edges, edges[1:])]

        if not self.ring:
            for _ in range(4):
                yield ()
            rows = jnp.concatenate(parts, 1)
            rows = lax.psum_scatter(rows, "seq", scatter_dimension=0, tiled=True)
            yield split(rows.astype(f32))
            return

        ring = self.reduce(
            lambda k: jnp.concatenate([part[k * slab : (k + 1) * slab] for part in parts], axis=1)
        )
        held = yield next(ring)
        for _ in range(3):
            held = yield ring.send(held)
        yield split(ring.send(held))


def once(value, *others):
    return lax.optimization_barrier((value, *others))[0]


def butterfly(value, axis, size):
    step = 1
    while step < size:
        value = value + lax.ppermute(value, axis, [(i, i ^ step) for i in range(size)])
        step *= 2
    return value


def gather_tp(value, axis):
    tp = lax.axis_index("tp")

    def join(second, mine, other):
        low = jnp.where(second, other, mine)
        high = jnp.where(second, mine, other)
        return jnp.concatenate([low, high], axis)

    pair = join(tp % 2 == 1, value, lax.ppermute(value, "tp", CORE_SWAP))
    return join(tp >= 2, pair, lax.ppermute(pair, "tp", Y_SWAP))


def psum_tp(halves):
    mine, other = halves
    mine = (mine.astype(f32) + lax.ppermute(other, "tp", CORE_SWAP).astype(f32)).astype(bf16)
    mine = (mine.astype(f32) + lax.ppermute(mine, "tp", Y_SWAP).astype(f32)).astype(bf16)
    return (mine, lax.ppermute(mine, "tp", CORE_SWAP))


def exact_dot(a, b):
    return lax.dot_general(
        a, b, (((1,), (0,)), ((), ())), precision=highest, preferred_element_type=f32
    )


def anywhere():
    return pl.BlockSpec(memory_space=pl.ANY)


def whole(shape):
    return pl.BlockSpec(
        shape, lambda i, *_: (0,) * len(shape), pipeline_mode=pl.Buffered(1)
    )


def rows_block(block, width):
    return pl.BlockSpec((block, width), lambda i, *_: (i, 0))


def lanes_block(rows, block):
    return pl.BlockSpec((rows, block), lambda i, *_: (0, i))


def shape_of(shape, dtype):
    return jax.ShapeDtypeStruct(shape, dtype)


def call(kernel, name, grid, scalars, ins, outs, scratch=(), flops=0, moved=0, exps=0):
    return pl.pallas_call(
        kernel,
        out_shape=tuple(shape_of(shape, dtype) for shape, dtype, _ in outs),
        grid_spec=pltpu.PrefetchScalarGridSpec(
            num_scalar_prefetch=len(scalars),
            grid=(grid,),
            in_specs=[spec for _, spec in ins],
            out_specs=tuple(spec for _, _, spec in outs),
            scratch_shapes=list(scratch),
        ),
        cost_estimate=pl.CostEstimate(flops=flops, bytes_accessed=moved, transcendentals=exps),
        name=name,
    )(*scalars, *[array for array, _ in ins])


def starts_of(chunks):
    at = 0
    for chunk in chunks:
        yield at
        at += chunk.shape[0]


def chunk_copies(chunks, low, high, held, sems):
    return [
        pltpu.make_async_copy(
            chunk.at[:, low:high], held.at[start : start + chunk.shape[0], :], sems.at[j]
        )
        for j, (chunk, start) in enumerate(zip(chunks, starts_of(chunks)))
    ]


def relative_store(ring_size, ring, place, out_ref, value):
    slab = value.shape[1] // ring_size
    if not ring:
        out_ref[...] = value
        return
    for p in range(ring_size):

        @pl.when(place == p)
        def _(p=p):
            for k in range(ring_size):
                s = CYCLE[(p + k) % ring_size]
                out_ref[:, k * slab : (k + 1) * slab] = value[:, s * slab : (s + 1) * slab]


def absolute_store(ring_size, ring, place, out_ref, value):
    slab = value.shape[1] // ring_size
    if not ring:
        out_ref[...] = value
        return
    for p in range(ring_size):

        @pl.when(place == p)
        def _(p=p):
            for k in range(ring_size):
                s = CYCLE[(p + k) % ring_size]
                out_ref[:, s * slab : (s + 1) * slab] = value[:, k * slab : (k + 1) * slab]


def onehot_rows(segment_col):
    items = lax.broadcasted_iota(jnp.int32, (segment_col.shape[0], ITEMS), 1)
    return (segment_col == items).astype(f32)


def onehot_cols(segment_row):
    items = lax.broadcasted_iota(jnp.int32, (ITEMS, segment_row.shape[1]), 0)
    return (segment_row == items).astype(f32)


def modulate(onehot, mod_ref, block):
    return exact_dot(onehot, mod_ref[block * ITEMS : (block + 1) * ITEMS, :])


def enter_kernel(scal, x_ref, g_ref, mod_ref, gain_ref, sc_ref,
                 xr_ref, gr_ref, modr_ref, gainr_ref, hidden_ref, *, size, ring):
    place = scal[0]

    @pl.when(pl.program_id(0) == 0)
    def _():
        relative_store(size, ring, place, modr_ref, mod_ref[...])
        relative_store(size, ring, place, gainr_ref, gain_ref[...])

    relative_store(size, ring, place, xr_ref, x_ref[...])
    relative_store(size, ring, place, gr_ref, g_ref[...])
    x = xr_ref[...].astype(f32)
    normed, _ = rms_parts(x)
    onehot = onehot_rows(sc_ref[...])
    scale = modulate(onehot, modr_ref, 1)
    shift = modulate(onehot, modr_ref, 0)
    hidden_ref[...] = (normed * gainr_ref[0:1, :] * (1.0 + scale) + shift).astype(bf16)


def project_kernel(hidden_ref, *refs, heads, first_owner, count):
    chunks, (slab_ref, held, sems) = refs[:count], refs[count:]
    width = heads * HD
    copies = chunk_copies(chunks, 0, 3 * width, held, sems)
    for one in copies:
        one.start()
    for s in range(slab_ref.shape[0]):
        if not first_owner <= s < first_owner + heads:
            slab_ref[s] = jnp.zeros(slab_ref.shape[1:], bf16)
    for one in copies:
        one.wait()
    hidden = hidden_ref[...]
    for j in range(3):
        part = dot(hidden, held[:, j * width : (j + 1) * width], ((1,), (0,))).astype(bf16)
        if j == 0:
            part = part * jnp.asarray(score_scale, bf16)
        for h in range(heads):
            slab_ref[first_owner + h, :, j * HD : (j + 1) * HD] = part[:, h * HD : (h + 1) * HD]


def split_halves(core, full_ref, mine_ref, other_ref):
    half = mine_ref.shape[0]
    mine_ref[...] = full_ref[pl.ds(pl.multiple_of(core * half, half), half), :]
    other_ref[...] = full_ref[pl.ds(pl.multiple_of((1 - core) * half, half), half), :]


def join_halves(core, mine_ref, other_ref, full_ref):
    half = mine_ref.shape[0]
    full_ref[pl.ds(pl.multiple_of(core * half, half), half), :] = mine_ref[...]
    full_ref[pl.ds(pl.multiple_of((1 - core) * half, half), half), :] = other_ref[...]


def times_turned(value_ref, held, full_ref):
    tiles = held.shape[0] // WIDE

    def one(i, _):
        at = pl.ds(pl.multiple_of(i * WIDE, WIDE), WIDE)
        full_ref[:, at] = dot(value_ref[...], held[at, :], ((1,), (1,))).astype(bf16)
        return 0

    lax.fori_loop(0, tiles, one, 0)


def out_kernel(scal, slab_ref, *refs, heads, first_owner, count, low, high):
    chunks, (mixed_ref, mine_ref, other_ref, held, full, sems) = refs[:count], refs[count:]
    copies = chunk_copies(chunks, low, high, held, sems)
    for one in copies:
        one.start()
    for h in range(heads):
        mixed_ref[:, h * HD : (h + 1) * HD] = slab_ref[first_owner + h]
    for one in copies:
        one.wait()
    times_turned(mixed_ref, held, full)
    split_halves(scal[1], full, mine_ref, other_ref)


def qkv_back_kernel(scal, slab_ref, *refs, heads, first_owner, count):
    chunks, (grads_ref, mine_ref, other_ref, held, full, sems) = refs[:count], refs[count:]
    width = heads * HD
    copies = chunk_copies(chunks, 0, 3 * width, held, sems)
    for one in copies:
        one.start()
    for j in range(3):
        for h in range(heads):
            at = j * width + h * HD
            grads_ref[:, at : at + HD] = slab_ref[first_owner + h, :, j * HD : (j + 1) * HD]
    for one in copies:
        one.wait()
    times_turned(grads_ref, held, full)
    split_halves(scal[1], full, mine_ref, other_ref)


def ffn_kernel(scal, x_ref, g_ref, am_ref, ao_ref, modr_ref, gainr_ref, sc_ref, *refs,
               count, units):
    chunks = refs[:count]
    (mid_ref, hidden_ref, fgrad_ref, inner_ref, both_ref, hm_ref, ho_ref, fm_ref, fo_ref,
     held, attn, full, sems) = refs[count:]
    core = scal[1]
    copies = chunk_copies(chunks, 0, held.shape[1], held, sems)
    for one in copies:
        one.start()
    join_halves(core, am_ref, ao_ref, attn)

    def prepare(i, _):
        at = pl.ds(pl.multiple_of(i * ROWS, ROWS), ROWS)
        onehot = onehot_rows(sc_ref[at, :])
        x_mid = x_ref[at, :].astype(f32) + jnp.tanh(modulate(onehot, modr_ref, 2)) * attn[
            at, :
        ].astype(f32)
        mid_ref[at, :] = x_mid
        normed, _ = rms_parts(x_mid)
        scale = modulate(onehot, modr_ref, 4)
        shift = modulate(onehot, modr_ref, 3)
        hidden_ref[at, :] = (normed * gainr_ref[1:2, :] * (1.0 + scale) + shift).astype(bf16)
        tanh_ffn = jnp.tanh(modulate(onehot, modr_ref, 5))
        fgrad_ref[at, :] = (g_ref[at, :].astype(f32) * tanh_ffn).astype(bf16)
        return 0

    lax.fori_loop(0, x_ref.shape[0] // ROWS, prepare, 0)
    for one in copies:
        one.wait()

    def tile(i, _):
        def at(base):
            return pl.ds(pl.multiple_of(base + i * WIDE, WIDE), WIDE)

        gate_pre = dot(hidden_ref[...], held[:, at(0)], ((1,), (0,)))
        up_pre = dot(hidden_ref[...], held[:, at(units)], ((1,), (0,)))
        inner_grad = dot(fgrad_ref[...], held[:, at(2 * units)], ((1,), (0,)))
        sigmoid = jax.nn.sigmoid(gate_pre)
        silu = gate_pre * sigmoid
        inner_ref[:, at(0)] = (silu * up_pre).astype(bf16)
        both_ref[:, at(0)] = (
            inner_grad * up_pre * sigmoid * (1.0 + gate_pre * (1.0 - sigmoid))
        ).astype(bf16)
        both_ref[:, at(units)] = (inner_grad * silu).astype(bf16)
        return 0

    lax.fori_loop(0, units // WIDE, tile, 0)
    times_turned(both_ref, held.at[:, 0 : 2 * units], full)
    split_halves(core, full, hm_ref, ho_ref)
    times_turned(inner_ref, held.at[:, 2 * units : 3 * units], full)
    split_halves(core, full, fm_ref, fo_ref)


def mid_kernel(scal, mid_ref, g_ref, hm_ref, ho_ref, modr_ref, gainr_ref, sc_ref, *refs,
               heads, first_owner, count, low, high):
    chunks = refs[:count]
    grad_ref, agrad_ref, slab_ref, held, hgrad, sems = refs[count:]
    copies = chunk_copies(chunks, low, high, held, sems)
    for one in copies:
        one.start()
    join_halves(scal[1], hm_ref, ho_ref, hgrad)
    for s in range(slab_ref.shape[0]):
        if not first_owner <= s < first_owner + heads:
            slab_ref[s] = jnp.zeros(slab_ref.shape[1:], bf16)

    def prepare(i, _):
        at = pl.ds(pl.multiple_of(i * ROWS, ROWS), ROWS)
        onehot = onehot_rows(sc_ref[at, :])
        normed, inverse = rms_parts(mid_ref[at, :])
        scale = modulate(onehot, modr_ref, 4)
        normed_grad = hgrad[at, :].astype(f32) * gainr_ref[1:2, :] * (1.0 + scale)
        grad = g_ref[at, :].astype(f32) + rms_back(normed, inverse, normed_grad)
        grad_ref[at, :] = grad
        agrad_ref[at, :] = (grad * jnp.tanh(modulate(onehot, modr_ref, 2))).astype(bf16)
        return 0

    lax.fori_loop(0, mid_ref.shape[0] // ROWS, prepare, 0)
    for one in copies:
        one.wait()
    mixed = dot(agrad_ref[...], held[...], ((1,), (0,))).astype(bf16)
    for h in range(heads):
        slab_ref[first_owner + h] = mixed[:, h * HD : (h + 1) * HD]


def own_rows(core, mine_ref, other_ref):
    first = pl.program_id(0) < pl.num_programs(0) // 2
    mine = jnp.logical_xor(first, core == 1)
    return jnp.where(mine, mine_ref[...].astype(f32), other_ref[...].astype(f32))


def side_kernel(scal, mid_ref, grad_ref, g_ref, am_ref, ao_ref, fm_ref, fo_ref, hm_ref, ho_ref,
                modr_ref, gainr_ref, sc_ref, sr_ref,
                block_ref, sums_ref, gain_ref, *, size, ring):
    place, core = scal[0], scal[1]

    @pl.when(pl.program_id(0) == 0)
    def _():
        sums_ref[...] = jnp.zeros_like(sums_ref)
        gain_ref[...] = jnp.zeros_like(gain_ref)

    attn = own_rows(core, am_ref, ao_ref)
    ffn_out = own_rows(core, fm_ref, fo_ref)
    hgrad = own_rows(core, hm_ref, ho_ref)
    onehot = onehot_rows(sc_ref[...])
    by_item = onehot_cols(sr_ref[0])
    tanh_attn = jnp.tanh(modulate(onehot, modr_ref, 2))
    tanh_ffn = jnp.tanh(modulate(onehot, modr_ref, 5))
    scale = modulate(onehot, modr_ref, 4)
    x_mid = mid_ref[...]
    absolute_store(size, ring, place, block_ref, x_mid + tanh_ffn * ffn_out)
    normed, _ = rms_parts(x_mid)

    def add(block, value):
        sums_ref[block * ITEMS : (block + 1) * ITEMS, :] += exact_dot(by_item, value)

    add(0, grad_ref[...] * attn * (1.0 - tanh_attn * tanh_attn))
    add(1, hgrad)
    add(2, hgrad * normed * gainr_ref[1:2, :])
    add(3, g_ref[...].astype(f32) * ffn_out * (1.0 - tanh_ffn * tanh_ffn))
    gain_ref[0:1, :] += jnp.sum(hgrad * normed * (1.0 + scale), axis=0, keepdims=True)


def leave_kernel(scal, x_ref, grad_ref, hm_ref, ho_ref, modr_ref, gainr_ref, sc_ref, sr_ref,
                 early_ref, egain_ref, input_ref, sums_ref, gain_ref, total, turned, *, size, ring):
    place, core = scal[0], scal[1]

    @pl.when(pl.program_id(0) == 0)
    def _():
        total[...] = jnp.zeros_like(total)
        total[2 * ITEMS : 6 * ITEMS, :] = early_ref[...]
        total[6 * ITEMS + 1 : 6 * ITEMS + 2, :] = egain_ref[0:1, :]

    hgrad = own_rows(core, hm_ref, ho_ref)
    onehot = onehot_rows(sc_ref[...])
    by_item = onehot_cols(sr_ref[0])
    scale = modulate(onehot, modr_ref, 1)
    normed, inverse = rms_parts(x_ref[...].astype(f32))
    normed_grad = hgrad * gainr_ref[0:1, :] * (1.0 + scale)
    absolute_store(
        size, ring, place, input_ref, grad_ref[...] + rms_back(normed, inverse, normed_grad)
    )
    total[0:ITEMS, :] += exact_dot(by_item, hgrad)
    total[ITEMS : 2 * ITEMS, :] += exact_dot(by_item, hgrad * normed * gainr_ref[0:1, :])
    total[6 * ITEMS : 6 * ITEMS + 1, :] += jnp.sum(
        hgrad * normed * (1.0 + scale), axis=0, keepdims=True
    )

    @pl.when(pl.program_id(0) == pl.num_programs(0) - 1)
    def _():
        absolute_store(size, ring, place, turned, total[...])
        quarter = sums_ref.shape[1]
        at = pl.ds(pl.multiple_of(scal[2] * quarter, quarter), quarter)
        sums_ref[...] = turned[0 : 6 * ITEMS, at]
        gain_ref[...] = turned[6 * ITEMS : 6 * ITEMS + 8, :]


def text_heads_kernel(head_of, w_ref, out_ref, by_head):
    for h in range(by_head.shape[0]):
        for j in range(2):
            by_head[h, :, j * HD : (j + 1) * HD] = w_ref[j, :, h * HD : (h + 1) * HD].astype(bf16)
    for k in range(out_ref.shape[1] // (2 * HD)):
        out_ref[:, 2 * k * HD : 2 * (k + 1) * HD] = by_head[head_of[k]]


def text_grad_kernel(slab_at, cap_ref, *refs):
    chunks, (out_ref, held, sems) = refs[:-3], refs[-3:]
    copies = chunk_copies(chunks, 0, 2 * HD, held, sems)
    for one in copies:
        one.start()
    for one in copies:
        one.wait()
    rows = cap_ref.shape[1]
    for h in range(out_ref.shape[2] // HD):
        at = pl.ds(pl.multiple_of(slab_at[h] * rows, rows), rows)
        part = dot(cap_ref[...], held[at, :], ((1,), (0,)))
        out_ref[0, :, h * HD : (h + 1) * HD] = part[:, :HD]
        out_ref[1, :, h * HD : (h + 1) * HD] = part[:, HD:]


def mod_kernel(scal, embed_ref, w_ref, out_ref):
    out_ref[...] = dot(embed_ref[...], w_ref[...].astype(bf16), ((1,), (0,)))


def turned_copy(source_ref, low, out_ref, block):
    def one(j, _):
        at = pl.ds(pl.multiple_of(j * block, block), block)
        out_ref[:, at] = jnp.transpose(source_ref[at, low : low + HD].astype(f32)).astype(bf16)
        return 0

    lax.fori_loop(0, source_ref.shape[0] // block, one, 0)


def self_kernel(table, q_ref, all_ref, sq_ref, sk_ref, out_ref, stat_ref, k_ref, vt_ref, *, block_k):
    i = pl.program_id(0)

    @pl.when(i == 0)
    def _():
        k_ref[...] = all_ref[:, HD : 2 * HD]
        turned_copy(all_ref, 2 * HD, vt_ref, block_k)

    q = q_ref[:, :HD]
    item_of_q = sq_ref[...]
    width = q.shape[0]

    def step(j, carry):
        top, total, out = carry
        at = pl.ds(pl.multiple_of(j * block_k, block_k), block_k)
        scores = dot(k_ref[at, :], q, ((1,), (1,)))
        scores = jnp.where(sk_ref[at, :] == item_of_q, scores, masked_score)
        new_top = jnp.maximum(top, jnp.max(scores, axis=0, keepdims=True))
        weights = jnp.exp(scores - new_top)
        shrink = jnp.exp(top - new_top)
        total = total * shrink + jnp.sum(weights, axis=0, keepdims=True)
        out = out * shrink + dot(vt_ref[:, at], weights.astype(bf16), ((1,), (0,)))
        return (new_top, total, out)

    start = (
        jnp.full((1, width), lowest_max, f32),
        jnp.zeros((1, width), f32),
        jnp.zeros((HD, width), f32),
    )
    top, total, out = lax.fori_loop(table[0, i], table[1, i], step, start)
    out_ref[...] = out / total
    stat_ref[...] = top + jnp.log(total)


def text_kernel(table, gate, q_ref, kv_ref, self_ref, sq_ref,
                mixed_ref, out_ref, stat_ref, k_ref, vt_ref):
    i = pl.program_id(0)

    @pl.when(i == 0)
    def _():
        k_ref[...] = kv_ref[:, :HD]
        turned_copy(kv_ref, HD, vt_ref, TEXT)

    q = q_ref[:, :HD]
    item_of_q = sq_ref[...]

    def step(item, carry):
        out, stat = carry
        at = pl.ds(pl.multiple_of(item * TEXT, TEXT), TEXT)
        scores = dot(k_ref[at, :], q, ((1,), (1,)))
        top = jnp.max(scores, axis=0, keepdims=True)
        weights = jnp.exp(scores - top)
        total = jnp.sum(weights, axis=0, keepdims=True)
        probs = (weights / total).astype(bf16)
        part = dot(vt_ref[:, at], probs, ((1,), (0,)))
        here = item_of_q == item
        return (jnp.where(here, part, out), jnp.where(here, top + jnp.log(total), stat))

    start = (jnp.zeros((HD, q.shape[0]), f32), jnp.zeros((1, q.shape[0]), f32))
    text_out, stat = lax.fori_loop(table[2, i], table[3, i], step, start)
    out_ref[...] = text_out
    stat_ref[...] = stat
    mixed_ref[...] = jnp.transpose(self_ref[...] + gate[0] * text_out).astype(bf16)


def text_back_kernel(table, gate, q_ref, g_ref, kv_ref, text_ref, stat_ref, sq_ref,
                     dkv_ref, dq_ref, cross_ref, k_ref, v_ref, kt_ref, dk_sum, dv_sum):
    i = pl.program_id(0)

    @pl.when(i == 0)
    def _():
        k_ref[...] = kv_ref[:, :HD]
        v_ref[...] = kv_ref[:, HD:]
        turned_copy(kv_ref, 0, kt_ref, TEXT)
        dk_sum[...] = jnp.zeros_like(dk_sum)
        dv_sum[...] = jnp.zeros_like(dv_sum)

    q = q_ref[:, :HD]
    item_of_q = sq_ref[...]
    g_value = g_ref[...].astype(f32)
    g = (g_value * gate[0]).astype(bf16)
    text_out = text_ref[...]
    cross_ref[...] = jnp.sum(jnp.transpose(g_value) * text_out, axis=0, keepdims=True)
    delta = jnp.sum(jnp.transpose(g.astype(f32)) * text_out, axis=0, keepdims=True)
    stat = stat_ref[...]

    def step(item, total):
        at = pl.ds(pl.multiple_of(item * TEXT, TEXT), TEXT)
        scores = dot(k_ref[at, :], q, ((1,), (1,)))
        probs = jnp.exp(jnp.where(item_of_q == item, scores - stat, masked_score))
        prob_grad = dot(v_ref[at, :], g, ((1,), (1,)))
        score_grad = (probs * (prob_grad - delta)).astype(bf16)
        dk_sum[at, :] += dot(score_grad, q, ((1,), (0,)))
        dv_sum[at, :] += dot(probs.astype(bf16), g, ((1,), (0,)))
        return total + dot(kt_ref[:, at], score_grad, ((1,), (0,)))

    start = jnp.zeros((HD, q.shape[0]), f32)
    dq_ref[...] = lax.fori_loop(table[2, i], table[3, i], step, start)

    @pl.when(i == pl.num_programs(0) - 1)
    def _():
        dkv_ref[:, :HD] = dk_sum[...].astype(bf16)
        dkv_ref[:, HD:] = dv_sum[...].astype(bf16)


def self_back_kernel(table, q_ref, g_ref, all_ref, self_ref, stat_ref, start_ref, sq_ref, sk_ref,
                     dqkv_ref, k_ref, v_ref, kt_ref, dk_sum, dv_sum, *, block_k):
    i = pl.program_id(0)

    @pl.when(i == 0)
    def _():
        k_ref[...] = all_ref[:, HD : 2 * HD]
        v_ref[...] = all_ref[:, 2 * HD :]
        turned_copy(all_ref, HD, kt_ref, block_k)
        dk_sum[...] = jnp.zeros_like(dk_sum)
        dv_sum[...] = jnp.zeros_like(dv_sum)

    q = q_ref[:, :HD]
    g = g_ref[...]
    item_of_q = sq_ref[...]
    delta = jnp.sum(jnp.transpose(g.astype(f32)) * self_ref[...], axis=0, keepdims=True)
    stat = stat_ref[...]

    def step(j, total):
        at = pl.ds(pl.multiple_of(j * block_k, block_k), block_k)
        scores = dot(k_ref[at, :], q, ((1,), (1,)))
        allowed = sk_ref[at, :] == item_of_q
        probs = jnp.exp(jnp.where(allowed, scores - stat, masked_score))
        prob_grad = dot(v_ref[at, :], g, ((1,), (1,)))
        score_grad = (probs * (prob_grad - delta)).astype(bf16)
        dk_sum[at, :] += dot(score_grad, q, ((1,), (0,)))
        dv_sum[at, :] += dot(probs.astype(bf16), g, ((1,), (0,)))
        return total + dot(kt_ref[:, at], score_grad, ((1,), (0,)))

    total = lax.fori_loop(table[0, i], table[1, i], step, start_ref[...])
    rows = q.shape[0]
    dqkv_ref[pl.ds(pl.multiple_of(i * rows, rows), rows), :HD] = jnp.transpose(
        total * score_scale
    ).astype(bf16)

    @pl.when(i == pl.num_programs(0) - 1)
    def _():
        dqkv_ref[:, HD : 2 * HD] = dk_sum[...].astype(bf16)
        dqkv_ref[:, 2 * HD :] = dv_sum[...].astype(bf16)


def attention_table(segments, block_q, block_k):
    by_block = segments.reshape(-1, block_q)
    low_item, high_item = by_block[:, 0], by_block[:, -1]
    first_key = jnp.sum(segments[None, :] < low_item[:, None], axis=1)
    end_key = jnp.sum(segments[None, :] <= high_item[:, None], axis=1)
    return jnp.stack(
        [first_key // block_k, (end_key + block_k - 1) // block_k, low_item, high_item + 1]
    ).astype(jnp.int32)


def per_device(
    x_tokens, caption, timesteps, segment_ids, out_grad,
    mod_weight, mod_first, mod_second,
    norm_gains, gains_first, gains_second,
    qkv_weight, qkv_first, qkv_second,
    out_weight, out_first, out_second,
    text_weight, text_first, text_second,
    cross_gates, cross_first, cross_second,
    updown_weight, updown_first, updown_second,
    down_weight, down_first, down_second,
    *, seq_size, tp_size,
):
    seq_index = lax.axis_index("seq")
    tp_index = lax.axis_index("tp")
    ring = Ring(seq_size)
    here, width = x_tokens.shape
    heads = cross_gates.shape[0]
    local_width = heads * HD
    count = here * seq_size
    units = down_weight.shape[0]
    quarter = width // tp_size
    first_owner = 1 if seq_size >= heads + 2 else 0
    owners = range(first_owner, first_owner + heads)
    seqs = jnp.full((seq_size,), seq_index)
    place = jnp.where(seqs % 2 == 0, seqs // 2, (15 - seqs) // 2)
    places = (place + jnp.arange(seq_size)) % seq_size
    slab_owner = jnp.where(places < 4, 2 * places, 15 - 2 * places).astype(jnp.int32)
    slab_head = jnp.clip(slab_owner - first_owner, 0, heads - 1)
    my_head = jnp.clip(seq_index - first_owner, 0, heads - 1)
    is_owner = (seq_index >= first_owner) & (seq_index < first_owner + heads)
    tps = jnp.full((1,), tp_index)
    scal = jnp.concatenate([place[:1], tps % 2, tps]).astype(jnp.int32)
    which = {"size": seq_size, "ring": ring.ring}

    def exchange(slabs):
        return lax.all_to_all(slabs, "seq", 0, 0, tiled=True)

    cap_rows = caption.shape[0]
    cap_cols = caption.shape[1] // seq_size
    cap_part = cap_cols // tp_size
    text_rows = cap_rows * seq_size
    if cap_part % 128 == 0:
        cap_own = call(
            lambda scal, in_ref, out_ref: out_ref.__setitem__(0, in_ref[...]),
            "caption_slabs", seq_size, [scal],
            [(caption, pl.BlockSpec((cap_rows, cap_part), lambda i, s: (0, i * tp_size + s[2])))],
            [
                (
                    (seq_size, cap_rows, cap_part), bf16,
                    pl.BlockSpec((1, cap_rows, cap_part), lambda i, s: (i, 0, 0)),
                )
            ],
            moved=2 * cap_rows * cap_cols * 4,
        )[0]
    else:
        cap_own = lax.dynamic_index_in_dim(
            caption.reshape(cap_rows, seq_size, tp_size, cap_part), tp_index, 2, keepdims=False
        )
        cap_own = jnp.transpose(cap_own, (1, 0, 2))
    silu_embed = jax.nn.silu(time_embed(timesteps)).astype(bf16)
    mod_rows = mod_weight.shape[0]
    silu_embed = once(silu_embed, cap_own)
    embed_rows = lax.dynamic_slice_in_dim(silu_embed, seq_index * mod_rows, mod_rows, 1)
    mod_part = call(
        mod_kernel, "modulation", 6, [scal],
        [
            (embed_rows, whole((ITEMS, mod_rows))),
            (mod_weight, pl.BlockSpec((mod_rows, quarter), lambda i, s: (0, i * tp_size + s[2]))),
        ],
        [((6 * ITEMS, quarter), f32, rows_block(ITEMS, quarter))],
        moved=mod_rows * 6 * quarter * 4, flops=2 * ITEMS * mod_rows * 6 * quarter,
    )[0]
    is_here = jnp.arange(seq_size) == seq_index
    slots = jnp.where(is_here[:, None], segment_ids.astype(f32)[None, :], 0.0).reshape(-1)
    gain_cols = norm_gains.shape[1]
    gain_slots = jnp.where(is_here[None, :, None], norm_gains[:, None, :], 0.0).reshape(-1)
    spare = -(slots.size + gain_slots.size) % (8 * quarter)
    packed = jnp.concatenate([slots, gain_slots, jnp.zeros((spare,), f32)]).reshape(-1, quarter)
    packed = butterfly(jnp.concatenate([mod_part, packed]), "seq", seq_size)
    modulation = gather_tp(packed[: 6 * ITEMS], 1)
    packed = packed[6 * ITEMS :].reshape(-1)
    segments = packed[:count].astype(jnp.int32)
    gains_value = packed[count : count + 2 * width].reshape(2, width).astype(bf16).astype(f32)
    gains_value = jnp.concatenate([gains_value] * 4)

    def turned(shard):
        return jnp.transpose(shard.astype(bf16), (1, 0, 2)).reshape(shard.shape[1], -1)

    attn_chunks = ring.gather(
        jnp.concatenate([turned(qkv_weight), out_weight.astype(bf16).T], axis=1)
    )
    pieces = len(attn_chunks)
    piece_sems = pltpu.SemaphoreType.DMA((pieces,))
    attn_ins = [(chunk, anywhere()) for chunk in attn_chunks]
    qkv_width = 3 * local_width

    def hop(chunks, k):
        return (chunks[k], chunks[-k]) if ring.ring else ()

    cap_own = once(exchange(cap_own), *hop(attn_chunks, 1))
    caption_cols = gather_tp(cap_own.reshape(text_rows, cap_part), 1)
    ffn_shard = jnp.concatenate([turned(updown_weight), down_weight.astype(bf16).T], axis=1)
    ffn_chunks = ring.gather(once(ffn_shard, packed))
    ffn_ins = [(chunk, anywhere()) for chunk in ffn_chunks]
    modulation = once(modulation, *hop(attn_chunks, 3), *hop(ffn_chunks, 1))
    segment_col = segment_ids[:, None]
    steps = here // ROWS
    segment_row = segment_ids.reshape(steps, 1, ROWS)
    row_ins = [
        (segment_col, rows_block(ROWS, 1)),
        (segment_row, pl.BlockSpec((1, 1, ROWS), lambda i, *_: (i, 0, 0))),
    ]
    block = rows_block(ROWS, width)
    mod_shape, gain_shape = modulation.shape, gains_value.shape
    x_rel, g_rel, mod_rel, gain_rel, hidden_attn = call(
        functools.partial(enter_kernel, **which), "enter", steps, [scal],
        [
            (x_tokens, block), (out_grad, block), (modulation, whole(mod_shape)),
            (gains_value, whole(gain_shape)), row_ins[0],
        ],
        [
            ((here, width), bf16, block), ((here, width), bf16, block),
            (mod_shape, f32, whole(mod_shape)), (gain_shape, f32, whole(gain_shape)),
            ((here, width), bf16, block),
        ],
        moved=here * width * 10,
    )
    mod_ins = [(mod_rel, whole(mod_shape)), (gain_rel, whole(gain_shape))]
    full_ins = mod_ins + [(segment_col, whole((here, 1)))]
    slab_shape = (seq_size, here, 3 * HD)
    slabs = call(
        functools.partial(
            project_kernel, heads=heads, first_owner=first_owner, count=pieces
        ),
        "project", 1, [],
        [(hidden_attn, whole((here, width)))] + attn_ins,
        [(slab_shape, bf16, whole(slab_shape))],
        [pltpu.VMEM((width, qkv_width), bf16), piece_sems],
        moved=width * qkv_width * 2, flops=2 * here * width * qkv_width,
    )[0]
    if ring.ring:
        text_slabs = call(
            text_heads_kernel, "text_heads", 1, [slab_head],
            [(text_weight, whole(text_weight.shape))],
            [((cap_cols, seq_size * 2 * HD), bf16, whole((cap_cols, seq_size * 2 * HD)))],
            [pltpu.VMEM((heads, cap_cols, 2 * HD), bf16)],
            moved=text_weight.size * 6,
        )[0]
        text_parts = dot(caption_cols, text_slabs, ((1,), (0,))).astype(bf16)

        text_sum = ring.reduce(
            lambda k: text_parts[:, 2 * k * HD : 2 * (k + 1) * HD], owners
        )
        next(text_sum)
        for held in ((slabs,), (), (), ()):
            text_kv = text_sum.send(held)
        text_kv = text_kv.astype(bf16)
    else:
        parts = jnp.einsum(
            "rc,jchd->hrjd", caption_cols,
            text_weight.astype(bf16).reshape(2, cap_cols, heads, HD), preferred_element_type=f32,
        ).reshape(heads, text_rows, 2 * HD)
        after = seq_size - heads - first_owner
        parts = jnp.pad(parts.astype(bf16), ((first_owner, after), (0, 0), (0, 0)))
        text_kv = lax.psum_scatter(parts, "seq", scatter_dimension=0, tiled=False)

    qkv_head = once(exchange(slabs), *hop(ffn_chunks, 2)).reshape(count, 3 * HD)

    block_q = math.gcd(count, 512)
    block_k = math.gcd(count, 512)
    table = attention_table(segments, block_q, block_k)
    tanh_cross = jnp.tanh(cross_gates)
    my_gate = jnp.sum(jnp.where(jnp.arange(heads) == my_head, tanh_cross, 0.0)).reshape(1)
    blocks = count // block_q
    q_ins = [(qkv_head, rows_block(block_q, 3 * HD))]
    seg_row = (segments[None, :], lanes_block(1, block_q))
    seg_col = (segments[:, None], whole((count, 1)))
    turned_out = ((HD, count), f32, lanes_block(HD, block_q))
    stat_out = ((1, count), f32, lanes_block(1, block_q))
    area = count * count * HD
    self_out, stat = call(
        functools.partial(self_kernel, block_k=block_k), "attend", blocks, [table],
        q_ins + [(qkv_head, whole(qkv_head.shape)), seg_row, seg_col],
        [turned_out, stat_out],
        [pltpu.VMEM((count, HD), bf16), pltpu.VMEM((HD, count), bf16)],
        flops=4 * area, moved=count * HD * 20, exps=count * count,
    )
    mixed_head, text_out, text_stat = call(
        text_kernel, "attend_text", blocks, [table, my_gate],
        q_ins
        + [(text_kv, whole(text_kv.shape)), (self_out, lanes_block(HD, block_q)), seg_row],
        [((count, HD), bf16, rows_block(block_q, HD)), turned_out, stat_out],
        [pltpu.VMEM((text_rows, HD), bf16), pltpu.VMEM((HD, text_rows), bf16)],
        flops=4 * count * TEXT * HD, moved=count * HD * 20, exps=count * TEXT,
    )
    mixed_head = once(mixed_head, *hop(ffn_chunks, 3))
    mixed_slabs = exchange(mixed_head.reshape(seq_size, here, HD))
    mixed_slabs = once(mixed_slabs, *(ffn_chunks[4:6] if ring.ring else ()))
    low, high = qkv_width, qkv_width + local_width
    head_args = {"heads": heads, "first_owner": first_owner, "count": pieces}
    half_shape = (here // 2, width)
    half_out = (half_shape, bf16, whole(half_shape))
    slab64 = (seq_size, here, HD)
    held_out = [pltpu.VMEM((width, local_width), bf16)]
    full_sum = [pltpu.VMEM((here, width), bf16), piece_sems]
    mixed, *attn = call(
        functools.partial(out_kernel, low=low, high=high, **head_args), "out", 1, [scal],
        [(mixed_slabs, whole(slab64))] + attn_ins,
        [((here, local_width), bf16, whole((here, local_width))), half_out, half_out],
        held_out + full_sum,
        moved=width * local_width * 2, flops=2 * here * width * local_width,
    )
    attn = psum_tp(attn)

    def halves(pair, spec=None):
        return [(one, spec or whole(half_shape)) for one in pair]

    tokens = (here, width)
    x_mid, hidden_ffn, ffn_grad, inner, both_grads, hm, ho, fm, fo = call(
        functools.partial(ffn_kernel, count=pieces, units=units), "ffn", 1, [scal],
        [(x_rel, whole(tokens)), (g_rel, whole(tokens))] + halves(attn) + full_ins + ffn_ins,
        [
            (tokens, f32, whole(tokens)), (tokens, bf16, whole(tokens)),
            (tokens, bf16, whole(tokens)), ((here, units), bf16, whole((here, units))),
            ((here, 2 * units), bf16, whole((here, 2 * units))),
            half_out, half_out, half_out, half_out,
        ],
        [pltpu.VMEM((width, 3 * units), bf16), pltpu.VMEM(tokens, bf16)] + full_sum,
        moved=width * 3 * units * 2, flops=12 * here * width * units,
    )
    hgrad = psum_tp((hm, ho))
    ffn_out = psum_tp(lax.optimization_barrier((fm, fo, *hgrad))[:2])
    mid_grad, attn_grad, grad_slabs = call(
        functools.partial(mid_kernel, low=low, high=high, **head_args), "mid", 1, [scal],
        [(x_mid, whole(tokens)), (g_rel, whole(tokens))] + halves(hgrad) + full_ins + attn_ins,
        [(tokens, f32, whole(tokens)), (tokens, bf16, whole(tokens)), (slab64, bf16, whole(slab64))],
        held_out + full_sum,
        moved=width * local_width * 2, flops=2 * here * width * local_width,
    )
    head_grad = exchange(grad_slabs).reshape(count, HD)
    ffn_sum = ring.reduce_products([(hidden_ffn, both_grads), (ffn_grad, inner)])
    next(ffn_sum)
    ffn_sum.send((grad_slabs,))
    head_grad = once(head_grad, *ffn_sum.send((head_grad,)))
    half_block = pl.BlockSpec((ROWS, width), lambda i, *_: (i % (steps // 2), 0))
    sums_shape, one_gain = (4 * ITEMS, width), (8, width)
    block_out, early_sums, early_gain = call(
        functools.partial(side_kernel, **which), "side", steps, [scal],
        [(x_mid, block), (mid_grad, block), (g_rel, block)]
        + halves(attn, half_block) + halves(ffn_out, half_block) + halves(hgrad, half_block)
        + mod_ins + row_ins,
        [(tokens, f32, block), (sums_shape, f32, whole(sums_shape)), (one_gain, f32, whole(one_gain))],
        moved=here * width * 24,
    )

    g_ins = [(head_grad, rows_block(block_q, HD))]
    kv64 = pltpu.VMEM((text_rows, HD), bf16)
    text_dkv, text_dq, cross_rows = call(
        text_back_kernel, "attend_text_back", blocks, [table, my_gate],
        q_ins + g_ins
        + [
            (text_kv, whole(text_kv.shape)), (text_out, lanes_block(HD, block_q)),
            (text_stat, lanes_block(1, block_q)), seg_row,
        ],
        [((text_rows, 2 * HD), bf16, whole((text_rows, 2 * HD))), turned_out, stat_out],
        [kv64, kv64, pltpu.VMEM((HD, text_rows), bf16)] + [pltpu.VMEM((text_rows, HD), f32)] * 2,
        flops=10 * count * TEXT * HD, moved=count * HD * 20, exps=count * TEXT,
    )
    head64 = pltpu.VMEM((count, HD), bf16)
    dqkv = call(
        functools.partial(self_back_kernel, block_k=block_k), "attend_back", blocks, [table],
        q_ins + g_ins
        + [
            (qkv_head, whole(qkv_head.shape)), (self_out, lanes_block(HD, block_q)),
            (stat, lanes_block(1, block_q)), (text_dq, lanes_block(HD, block_q)), seg_row, seg_col,
        ],
        [(qkv_head.shape, bf16, whole(qkv_head.shape))],
        [head64, head64, pltpu.VMEM((HD, count), bf16)] + [pltpu.VMEM((count, HD), f32)] * 2,
        flops=10 * area, moved=count * HD * 20, exps=count * count,
    )[0]

    back_slabs = exchange(dqkv.reshape(slab_shape))
    qkv_grads, *hidden_grad = call(
        functools.partial(qkv_back_kernel, **head_args), "qkv_back", 1, [scal],
        [(back_slabs, whole(slab_shape))] + attn_ins,
        [((here, qkv_width), bf16, whole((here, qkv_width))), half_out, half_out],
        [pltpu.VMEM((width, qkv_width), bf16)] + full_sum,
        moved=width * qkv_width * 2, flops=2 * here * width * qkv_width,
    )
    text_grads = ring.gather(text_dkv)
    if ring.ring:
        slab_at = jnp.argmax(
            slab_owner[None, :] == jnp.arange(first_owner, first_owner + heads)[:, None], axis=1
        ).astype(jnp.int32)
        text_owned = call(
            text_grad_kernel, "text_grad", 1, [slab_at],
            [(caption_cols.T, whole((cap_cols, text_rows)))]
            + [(one, anywhere()) for one in text_grads],
            [(text_weight.shape, f32, whole(text_weight.shape))],
            [
                pltpu.VMEM((seq_size * text_rows, 2 * HD), bf16),
                pltpu.SemaphoreType.DMA((len(text_grads),)),
            ],
            flops=4 * text_rows * cap_cols * local_width, moved=text_rows * cap_cols * 4,
        )[0]
    else:
        text_grads = text_grads[0].reshape(seq_size, text_rows, 2, HD)
        text_owned = jnp.einsum(
            "rc,hrjd->jchd", caption_cols, text_grads[first_owner : first_owner + heads],
            preferred_element_type=f32,
        ).reshape(text_weight.shape)

    attn_sum = ring.reduce_products([(hidden_attn, qkv_grads), (attn_grad, mixed)])
    next(attn_sum)
    ffn_sum.send((dqkv,))
    updown_rows, down_owned = ffn_sum.send(())
    for _ in range(4):
        attn_grads = attn_sum.send(())
    qkv_rows, out_owned = attn_grads
    hidden_grad = psum_tp(hidden_grad)
    all_sums = (6 * ITEMS, quarter)
    input_grad, item_sums, gain_sums = call(
        functools.partial(leave_kernel, **which), "leave", steps, [scal],
        [(x_rel, block), (mid_grad, block)] + halves(hidden_grad, half_block) + mod_ins + row_ins
        + [(early_sums, whole(sums_shape)), (early_gain, whole(one_gain))],
        [(tokens, f32, block), (all_sums, f32, whole(all_sums)), (one_gain, f32, whole(one_gain))],
        [pltpu.VMEM((6 * ITEMS + 8, width), f32)] * 2,
        moved=here * width * 16,
    )

    cross_here = jnp.where(
        is_owner & (jnp.arange(quarter) == my_head), jnp.sum(cross_rows), 0.0
    )
    packed = jnp.concatenate(
        [
            item_sums, gain_sums[:2].reshape(-1, quarter), cross_here[None],
            jnp.zeros((-(2 * tp_size + 1) % 8, quarter), f32),
        ]
    )
    packed = butterfly(packed, "seq", seq_size)
    item_mod_low = packed[: 6 * ITEMS].astype(bf16)
    gain_grads = packed[6 * ITEMS : 6 * ITEMS + 2 * tp_size].reshape(2, seq_size, gain_cols)
    gains_owned = jnp.sum(jnp.where(is_here[None, :, None], gain_grads, 0.0), axis=1)
    cross_total = packed[6 * ITEMS + 2 * tp_size, :heads] * (1.0 - tanh_cross * tanh_cross)

    def by_block(sums):
        return jnp.transpose(sums.reshape(6, ITEMS, -1), (1, 0, 2)).reshape(ITEMS, -1)

    mod_weight_grad = dot(embed_rows, by_block(gather_tp(item_mod_low, 1)), ((0,), (0,)))
    mod_quarter_grad = dot(embed_rows, by_block(item_mod_low), ((0,), (0,)))

    owned_square = (
        square_sum(qkv_rows)
        + square_sum(out_owned)
        + square_sum(text_owned)
        + square_sum(updown_rows)
        + square_sum(down_owned)
        + square_sum(mod_quarter_grad)
    )
    owned_square = owned_square + jnp.where(tp_index == 0, square_sum(gains_owned), 0.0)
    owned_square = owned_square + jnp.where(seq_index == 0, square_sum(cross_total), 0.0)
    total_square = jnp.full((8, 128), owned_square)
    total_square = butterfly(butterfly(total_square, "tp", tp_size), "seq", seq_size)[0, 0]
    grad_norm = jnp.sqrt(total_square)
    clip = jnp.minimum(1.0, clip_limit / (grad_norm + 1e-06))

    def unturned(rows, blocks):
        return jnp.transpose(rows.reshape(rows.shape[0], blocks, -1), (1, 0, 2))

    matrix = functools.partial(adam_update, clip=clip, rate=rate_matrix, decay=decay_matrix)
    small = functools.partial(adam_update, clip=clip, rate=rate_small, decay=0.0)
    return (
        block_out,
        input_grad,
        grad_norm,
        *matrix(mod_weight, mod_first, mod_second, mod_weight_grad),
        *small(norm_gains, gains_first, gains_second, gains_owned),
        *matrix(qkv_weight, qkv_first, qkv_second, unturned(qkv_rows, 3)),
        *matrix(out_weight, out_first, out_second, out_owned.T),
        *matrix(text_weight, text_first, text_second, text_owned),
        *small(cross_gates, cross_first, cross_second, cross_total),
        *matrix(updown_weight, updown_first, updown_second, unturned(updown_rows, 2)),
        *matrix(down_weight, down_first, down_second, down_owned.T),
    )


def solution(mesh):
    rows = P("seq", None)
    cols = P(None, "seq")
    split = P(None, "seq", "tp")
    turned = P("tp", "seq")
    heads = P("tp")
    weights = (rows,) * 3 + (cols,) * 3 + (split,) * 3 + (turned,) * 3 + (split,) * 3
    weights = weights + (heads,) * 3 + (split,) * 3 + (turned,) * 3
    return jax.shard_map(
        functools.partial(per_device, seq_size=mesh.shape["seq"], tp_size=mesh.shape["tp"]),
        mesh=mesh,
        in_specs=(rows, rows, P(), P("seq"), rows) + weights,
        out_specs=(rows, rows, P()) + weights,
        check_vma=False,
    )
```

```python
import functools
import math

import jax
import jax.numpy as jnp
from jax import lax
from jax.experimental import pallas as pl
from jax.experimental.pallas import tpu as pltpu
from jax.sharding import PartitionSpec as P

HD = 64
TE = 1024
TEXT = 256
ITEMS = 8
ADAM_STEP = 10

bf16 = jnp.bfloat16
f32 = jnp.float32
highest = lax.Precision.HIGHEST
eps_norm = 1e-06
masked_score = -1e30
lowest_max = -1e20
clip_limit = 1.0
beta_first = 0.9
beta_second = 0.95
adam_eps = 1e-08
rate_matrix = 0.05
rate_small = 0.5
decay_matrix = 0.1
score_scale = HD ** (-0.5)

WIDE = 256
ROWS = 64

CORE_SWAP = [(0, 1), (1, 0), (2, 3), (3, 2)]
Y_SWAP = [(0, 2), (2, 0), (1, 3), (3, 1)]
CYCLE = (0, 2, 4, 6, 7, 5, 3, 1)


def time_embed(timesteps):
    half_width = TE // 2
    frequency = jnp.exp(-math.log(10000.0) * jnp.arange(half_width, dtype=f32) / half_width)
    angles = 1000.0 * timesteps[:, None] * frequency[None, :]
    return jnp.concatenate([jnp.cos(angles), jnp.sin(angles)], axis=1)


def rms_parts(values):
    inverse = lax.rsqrt(jnp.mean(values * values, axis=-1, keepdims=True) + eps_norm)
    return (values * inverse, inverse)


def rms_back(normed, inverse, normed_grad):
    return inverse * (normed_grad - normed * jnp.mean(normed_grad * normed, axis=-1, keepdims=True))


def adam_update(weight, first, second, grad, clip, rate, decay):
    clipped = grad * clip
    first_new = beta_first * first + (1.0 - beta_first) * clipped
    second_new = beta_second * second + (1.0 - beta_second) * clipped * clipped
    first_hat = first_new / (1.0 - beta_first**ADAM_STEP)
    second_hat = second_new / (1.0 - beta_second**ADAM_STEP)
    weight_new = weight - rate * (first_hat / (jnp.sqrt(second_hat) + adam_eps) + decay * weight)
    return (weight_new, first_new, second_new)


def square_sum(values):
    return jnp.sum(values * values)


def dot(a, b, dims):
    return lax.dot_general(a, b, (dims, ((), ())), preferred_element_type=f32)


class Ring:
    def __init__(self, size):
        self.size = size
        self.ring = size == len(CYCLE)

    def hop(self, value, step, sends=None):
        n = self.size
        pairs = [(CYCLE[p], CYCLE[(p + step) % n]) for p in range(n) if sends is None or sends(p)]
        return lax.ppermute(value, "seq", pairs)

    def gather(self, own, held=((), (), ())):
        if not self.ring:
            return [lax.all_gather(own, "seq", axis=0, tiled=True)]
        half = own.shape[0] // 2
        ahead, behind = [own], [own]
        for i in range(3):
            ahead.append(self.hop(ahead[-1], 1))
            behind.append(self.hop(behind[-1], -1))
            if held[i]:
                ahead[-1], behind[-1] = lax.optimization_barrier(
                    (ahead[-1], behind[-1], *held[i])
                )[:2]
        far = [self.hop(behind[-1][:half], -1), self.hop(ahead[-1][half:], 1)]
        return behind + far + ahead[:0:-1]

    def reduce(self, block, active=None):
        rows = block(0).shape[0]
        half = rows // 2

        def sends(k):
            if active is None:
                return None
            return lambda p: CYCLE[(p + k) % self.size] in active

        def wait(held, *values):
            return lax.optimization_barrier((*values, *held))[: len(values)] if held else values

        def plus(part, moved):
            return (part.astype(f32) + moved.astype(f32)).astype(bf16)

        ahead, behind = block(4)[:half], block(4)[half:]
        for k in (3, 2, 1, 0):
            sent = (ahead, behind)
            ahead = self.hop(ahead, 1, sends(k + 1))
            behind = self.hop(behind, -1, sends(-k - 1))
            ahead, behind = wait((yield sent), ahead, behind)
            if k == 3:
                near, far = block(3), block(5)
                ahead = jnp.concatenate([plus(near[:half], ahead), near[half:]])
                behind = jnp.concatenate([far[:half], plus(far[half:], behind)])
            elif k:
                ahead, behind = plus(block(k), ahead), plus(block(8 - k), behind)
        yield block(0).astype(f32) + ahead.astype(f32) + behind.astype(f32)

    def reduce_products(self, pairs):
        parts = [dot(left, right, ((0,), (0,))).astype(bf16) for left, right in pairs]
        widths = [part.shape[1] for part in parts]
        edges = [sum(widths[:i]) for i in range(len(widths) + 1)]
        slab = parts[0].shape[0] // self.size

        def split(rows):
            return [rows[:, low:high] for low, high in zip(edges, edges[1:])]

        if not self.ring:
            for _ in range(4):
                yield ()
            rows = jnp.concatenate(parts, 1)
            rows = lax.psum_scatter(rows, "seq", scatter_dimension=0, tiled=True)
            yield split(rows.astype(f32))
            return

        ring = self.reduce(
            lambda k: jnp.concatenate([part[k * slab : (k + 1) * slab] for part in parts], axis=1)
        )
        held = yield next(ring)
        for _ in range(3):
            held = yield ring.send(held)
        yield split(ring.send(held))


def once(value, *others):
    return lax.optimization_barrier((value, *others))[0]


def butterfly(value, axis, size):
    step = 1
    while step < size:
        value = value + lax.ppermute(value, axis, [(i, i ^ step) for i in range(size)])
        step *= 2
    return value


def gather_tp(value, axis):
    tp = lax.axis_index("tp")

    def join(second, mine, other):
        low = jnp.where(second, other, mine)
        high = jnp.where(second, mine, other)
        return jnp.concatenate([low, high], axis)

    pair = join(tp % 2 == 1, value, lax.ppermute(value, "tp", CORE_SWAP))
    return join(tp >= 2, pair, lax.ppermute(pair, "tp", Y_SWAP))


def psum_tp(halves, held=()):
    mine, other = halves
    mine = (mine.astype(f32) + lax.ppermute(other, "tp", CORE_SWAP).astype(f32)).astype(bf16)
    mine = once(mine, *held)
    mine = (mine.astype(f32) + lax.ppermute(mine, "tp", Y_SWAP).astype(f32)).astype(bf16)
    return (mine, lax.ppermute(mine, "tp", CORE_SWAP))


def exact_dot(a, b):
    return lax.dot_general(
        a, b, (((1,), (0,)), ((), ())), precision=highest, preferred_element_type=f32
    )


def anywhere():
    return pl.BlockSpec(memory_space=pl.ANY)


def whole(shape):
    return pl.BlockSpec(
        shape, lambda i, *_: (0,) * len(shape), pipeline_mode=pl.Buffered(1)
    )


def rows_block(block, width):
    return pl.BlockSpec((block, width), lambda i, *_: (i, 0))


def lanes_block(rows, block):
    return pl.BlockSpec((rows, block), lambda i, *_: (0, i))


def shape_of(shape, dtype):
    return jax.ShapeDtypeStruct(shape, dtype)


def call(kernel, name, grid, scalars, ins, outs, scratch=(), flops=0, moved=0, exps=0):
    return pl.pallas_call(
        kernel,
        out_shape=tuple(shape_of(shape, dtype) for shape, dtype, _ in outs),
        grid_spec=pltpu.PrefetchScalarGridSpec(
            num_scalar_prefetch=len(scalars),
            grid=(grid,),
            in_specs=[spec for _, spec in ins],
            out_specs=tuple(spec for _, _, spec in outs),
            scratch_shapes=list(scratch),
        ),
        cost_estimate=pl.CostEstimate(flops=flops, bytes_accessed=moved, transcendentals=exps),
        name=name,
    )(*scalars, *[array for array, _ in ins])


def starts_of(chunks):
    at = 0
    for chunk in chunks:
        yield at
        at += chunk.shape[0]


def chunk_copies(chunks, low, high, held, sems):
    return [
        pltpu.make_async_copy(
            chunk.at[:, low:high], held.at[start : start + chunk.shape[0], :], sems.at[j]
        )
        for j, (chunk, start) in enumerate(zip(chunks, starts_of(chunks)))
    ]


def relative_store(ring_size, ring, place, out_ref, value):
    slab = value.shape[1] // ring_size
    if not ring:
        out_ref[...] = value
        return
    for p in range(ring_size):

        @pl.when(place == p)
        def _(p=p):
            for k in range(ring_size):
                s = CYCLE[(p + k) % ring_size]
                out_ref[:, k * slab : (k + 1) * slab] = value[:, s * slab : (s + 1) * slab]


def absolute_store(ring_size, ring, place, out_ref, value):
    slab = value.shape[1] // ring_size
    if not ring:
        out_ref[...] = value
        return
    for p in range(ring_size):

        @pl.when(place == p)
        def _(p=p):
            for k in range(ring_size):
                s = CYCLE[(p + k) % ring_size]
                out_ref[:, s * slab : (s + 1) * slab] = value[:, k * slab : (k + 1) * slab]


def onehot_rows(segment_col):
    items = lax.broadcasted_iota(jnp.int32, (segment_col.shape[0], ITEMS), 1)
    return (segment_col == items).astype(f32)


def onehot_cols(segment_row):
    items = lax.broadcasted_iota(jnp.int32, (ITEMS, segment_row.shape[1]), 0)
    return (segment_row == items).astype(f32)


def modulate(onehot, mod_ref, block):
    return exact_dot(onehot, mod_ref[block * ITEMS : (block + 1) * ITEMS, :])


def enter_kernel(scal, x_ref, g_ref, mod_ref, gain_ref, sc_ref,
                 xr_ref, gr_ref, modr_ref, gainr_ref, hidden_ref, *, size, ring):
    place = scal[0]

    @pl.when(pl.program_id(0) == 0)
    def _():
        relative_store(size, ring, place, modr_ref, mod_ref[...])
        relative_store(size, ring, place, gainr_ref, gain_ref[...])

    relative_store(size, ring, place, xr_ref, x_ref[...])
    relative_store(size, ring, place, gr_ref, g_ref[...])
    x = xr_ref[...].astype(f32)
    normed, _ = rms_parts(x)
    onehot = onehot_rows(sc_ref[...])
    scale = modulate(onehot, modr_ref, 1)
    shift = modulate(onehot, modr_ref, 0)
    hidden_ref[...] = (normed * gainr_ref[0:1, :] * (1.0 + scale) + shift).astype(bf16)


def project_kernel(hidden_ref, *refs, heads, first_owner, count):
    chunks, (slab_ref, held, sems) = refs[:count], refs[count:]
    width = heads * HD
    copies = chunk_copies(chunks, 0, 3 * width, held, sems)
    for one in copies:
        one.start()
    for s in range(slab_ref.shape[0]):
        if not first_owner <= s < first_owner + heads:
            slab_ref[s] = jnp.zeros(slab_ref.shape[1:], bf16)
    for one in copies:
        one.wait()
    hidden = hidden_ref[...]
    for j in range(3):
        part = dot(hidden, held[:, j * width : (j + 1) * width], ((1,), (0,))).astype(bf16)
        if j == 0:
            part = part * jnp.asarray(score_scale, bf16)
        for h in range(heads):
            slab_ref[first_owner + h, :, j * HD : (j + 1) * HD] = part[:, h * HD : (h + 1) * HD]


def split_halves(core, full_ref, mine_ref, other_ref):
    half = mine_ref.shape[0]
    mine_ref[...] = full_ref[pl.ds(pl.multiple_of(core * half, half), half), :]
    other_ref[...] = full_ref[pl.ds(pl.multiple_of((1 - core) * half, half), half), :]


def join_halves(core, mine_ref, other_ref, full_ref):
    half = mine_ref.shape[0]
    full_ref[pl.ds(pl.multiple_of(core * half, half), half), :] = mine_ref[...]
    full_ref[pl.ds(pl.multiple_of((1 - core) * half, half), half), :] = other_ref[...]


def times_turned(value_ref, held, full_ref):
    tiles = held.shape[0] // WIDE

    def one(i, _):
        at = pl.ds(pl.multiple_of(i * WIDE, WIDE), WIDE)
        full_ref[:, at] = dot(value_ref[...], held[at, :], ((1,), (1,))).astype(bf16)
        return 0

    lax.fori_loop(0, tiles, one, 0)


def out_kernel(scal, slab_ref, *refs, heads, first_owner, count, low, high):
    chunks, (mixed_ref, mine_ref, other_ref, held, full, sems) = refs[:count], refs[count:]
    copies = chunk_copies(chunks, low, high, held, sems)
    for one in copies:
        one.start()
    for h in range(heads):
        mixed_ref[:, h * HD : (h + 1) * HD] = slab_ref[first_owner + h]
    for one in copies:
        one.wait()
    times_turned(mixed_ref, held, full)
    split_halves(scal[1], full, mine_ref, other_ref)


def qkv_back_kernel(scal, slab_ref, *refs, heads, first_owner, count):
    chunks, (grads_ref, mine_ref, other_ref, held, full, sems) = refs[:count], refs[count:]
    width = heads * HD
    copies = chunk_copies(chunks, 0, 3 * width, held, sems)
    for one in copies:
        one.start()
    for j in range(3):
        for h in range(heads):
            at = j * width + h * HD
            grads_ref[:, at : at + HD] = slab_ref[first_owner + h, :, j * HD : (j + 1) * HD]
    for one in copies:
        one.wait()
    times_turned(grads_ref, held, full)
    split_halves(scal[1], full, mine_ref, other_ref)


def ffn_kernel(scal, x_ref, g_ref, am_ref, ao_ref, modr_ref, gainr_ref, sc_ref, *refs,
               count, units):
    chunks = refs[:count]
    (mid_ref, hidden_ref, fgrad_ref, inner_ref, both_ref, hm_ref, ho_ref, fm_ref, fo_ref,
     held, attn, full, sems) = refs[count:]
    core = scal[1]
    copies = chunk_copies(chunks, 0, held.shape[1], held, sems)
    for one in copies:
        one.start()
    join_halves(core, am_ref, ao_ref, attn)

    def prepare(i, _):
        at = pl.ds(pl.multiple_of(i * ROWS, ROWS), ROWS)
        onehot = onehot_rows(sc_ref[at, :])
        x_mid = x_ref[at, :].astype(f32) + jnp.tanh(modulate(onehot, modr_ref, 2)) * attn[
            at, :
        ].astype(f32)
        mid_ref[at, :] = x_mid
        normed, _ = rms_parts(x_mid)
        scale = modulate(onehot, modr_ref, 4)
        shift = modulate(onehot, modr_ref, 3)
        hidden_ref[at, :] = (normed * gainr_ref[1:2, :] * (1.0 + scale) + shift).astype(bf16)
        tanh_ffn = jnp.tanh(modulate(onehot, modr_ref, 5))
        fgrad_ref[at, :] = (g_ref[at, :].astype(f32) * tanh_ffn).astype(bf16)
        return 0

    lax.fori_loop(0, x_ref.shape[0] // ROWS, prepare, 0)
    for one in copies:
        one.wait()

    def tile(i, _):
        def at(base):
            return pl.ds(pl.multiple_of(base + i * WIDE, WIDE), WIDE)

        gate_pre = dot(hidden_ref[...], held[:, at(0)], ((1,), (0,)))
        up_pre = dot(hidden_ref[...], held[:, at(units)], ((1,), (0,)))
        inner_grad = dot(fgrad_ref[...], held[:, at(2 * units)], ((1,), (0,)))
        sigmoid = jax.nn.sigmoid(gate_pre)
        silu = gate_pre * sigmoid
        inner_ref[:, at(0)] = (silu * up_pre).astype(bf16)
        both_ref[:, at(0)] = (
            inner_grad * up_pre * sigmoid * (1.0 + gate_pre * (1.0 - sigmoid))
        ).astype(bf16)
        both_ref[:, at(units)] = (inner_grad * silu).astype(bf16)
        return 0

    lax.fori_loop(0, units // WIDE, tile, 0)
    times_turned(both_ref, held.at[:, 0 : 2 * units], full)
    split_halves(core, full, hm_ref, ho_ref)
    times_turned(inner_ref, held.at[:, 2 * units : 3 * units], full)
    split_halves(core, full, fm_ref, fo_ref)


def mid_kernel(scal, mid_ref, g_ref, hm_ref, ho_ref, modr_ref, gainr_ref, sc_ref, *refs,
               heads, first_owner, count, low, high):
    chunks = refs[:count]
    grad_ref, agrad_ref, slab_ref, held, hgrad, sems = refs[count:]
    copies = chunk_copies(chunks, low, high, held, sems)
    for one in copies:
        one.start()
    join_halves(scal[1], hm_ref, ho_ref, hgrad)
    for s in range(slab_ref.shape[0]):
        if not first_owner <= s < first_owner + heads:
            slab_ref[s] = jnp.zeros(slab_ref.shape[1:], bf16)

    def prepare(i, _):
        at = pl.ds(pl.multiple_of(i * ROWS, ROWS), ROWS)
        onehot = onehot_rows(sc_ref[at, :])
        normed, inverse = rms_parts(mid_ref[at, :])
        scale = modulate(onehot, modr_ref, 4)
        normed_grad = hgrad[at, :].astype(f32) * gainr_ref[1:2, :] * (1.0 + scale)
        grad = g_ref[at, :].astype(f32) + rms_back(normed, inverse, normed_grad)
        grad_ref[at, :] = grad
        agrad_ref[at, :] = (grad * jnp.tanh(modulate(onehot, modr_ref, 2))).astype(bf16)
        return 0

    lax.fori_loop(0, mid_ref.shape[0] // ROWS, prepare, 0)
    for one in copies:
        one.wait()
    mixed = dot(agrad_ref[...], held[...], ((1,), (0,))).astype(bf16)
    for h in range(heads):
        slab_ref[first_owner + h] = mixed[:, h * HD : (h + 1) * HD]


def own_rows(core, mine_ref, other_ref):
    first = pl.program_id(0) < pl.num_programs(0) // 2
    mine = jnp.logical_xor(first, core == 1)
    return jnp.where(mine, mine_ref[...].astype(f32), other_ref[...].astype(f32))


def side_kernel(scal, mid_ref, grad_ref, g_ref, am_ref, ao_ref, fm_ref, fo_ref, hm_ref, ho_ref,
                modr_ref, gainr_ref, sc_ref, sr_ref,
                block_ref, sums_ref, gain_ref, *, size, ring):
    place, core = scal[0], scal[1]

    @pl.when(pl.program_id(0) == 0)
    def _():
        sums_ref[...] = jnp.zeros_like(sums_ref)
        gain_ref[...] = jnp.zeros_like(gain_ref)

    attn = own_rows(core, am_ref, ao_ref)
    ffn_out = own_rows(core, fm_ref, fo_ref)
    hgrad = own_rows(core, hm_ref, ho_ref)
    onehot = onehot_rows(sc_ref[...])
    by_item = onehot_cols(sr_ref[0])
    tanh_attn = jnp.tanh(modulate(onehot, modr_ref, 2))
    tanh_ffn = jnp.tanh(modulate(onehot, modr_ref, 5))
    scale = modulate(onehot, modr_ref, 4)
    x_mid = mid_ref[...]
    absolute_store(size, ring, place, block_ref, x_mid + tanh_ffn * ffn_out)
    normed, _ = rms_parts(x_mid)

    def add(block, value):
        sums_ref[block * ITEMS : (block + 1) * ITEMS, :] += exact_dot(by_item, value)

    add(0, grad_ref[...] * attn * (1.0 - tanh_attn * tanh_attn))
    add(1, hgrad)
    add(2, hgrad * normed * gainr_ref[1:2, :])
    add(3, g_ref[...].astype(f32) * ffn_out * (1.0 - tanh_ffn * tanh_ffn))
    gain_ref[0:1, :] += jnp.sum(hgrad * normed * (1.0 + scale), axis=0, keepdims=True)


def leave_kernel(scal, x_ref, grad_ref, hm_ref, ho_ref, modr_ref, gainr_ref, sc_ref, sr_ref,
                 early_ref, egain_ref, input_ref, sums_ref, gain_ref, total, turned, *, size, ring):
    place, core = scal[0], scal[1]

    @pl.when(pl.program_id(0) == 0)
    def _():
        total[...] = jnp.zeros_like(total)
        total[2 * ITEMS : 6 * ITEMS, :] = early_ref[...]
        total[6 * ITEMS + 1 : 6 * ITEMS + 2, :] = egain_ref[0:1, :]

    hgrad = own_rows(core, hm_ref, ho_ref)
    onehot = onehot_rows(sc_ref[...])
    by_item = onehot_cols(sr_ref[0])
    scale = modulate(onehot, modr_ref, 1)
    normed, inverse = rms_parts(x_ref[...].astype(f32))
    normed_grad = hgrad * gainr_ref[0:1, :] * (1.0 + scale)
    absolute_store(
        size, ring, place, input_ref, grad_ref[...] + rms_back(normed, inverse, normed_grad)
    )
    total[0:ITEMS, :] += exact_dot(by_item, hgrad)
    total[ITEMS : 2 * ITEMS, :] += exact_dot(by_item, hgrad * normed * gainr_ref[0:1, :])
    total[6 * ITEMS : 6 * ITEMS + 1, :] += jnp.sum(
        hgrad * normed * (1.0 + scale), axis=0, keepdims=True
    )

    @pl.when(pl.program_id(0) == pl.num_programs(0) - 1)
    def _():
        absolute_store(size, ring, place, turned, total[...])
        quarter = sums_ref.shape[1]
        at = pl.ds(pl.multiple_of(scal[2] * quarter, quarter), quarter)
        sums_ref[...] = turned[0 : 6 * ITEMS, at]
        gain_ref[...] = turned[6 * ITEMS : 6 * ITEMS + 8, :]


def text_heads_kernel(head_of, w_ref, out_ref, by_head):
    for h in range(by_head.shape[0]):
        for j in range(2):
            by_head[h, :, j * HD : (j + 1) * HD] = w_ref[j, :, h * HD : (h + 1) * HD].astype(bf16)
    for k in range(out_ref.shape[1] // (2 * HD)):
        out_ref[:, 2 * k * HD : 2 * (k + 1) * HD] = by_head[head_of[k]]


def text_grad_kernel(slab_at, cap_ref, *refs):
    chunks, (out_ref, held, sems) = refs[:-3], refs[-3:]
    copies = chunk_copies(chunks, 0, 2 * HD, held, sems)
    for one in copies:
        one.start()
    for one in copies:
        one.wait()
    rows = cap_ref.shape[1]
    for h in range(out_ref.shape[2] // HD):
        at = pl.ds(pl.multiple_of(slab_at[h] * rows, rows), rows)
        part = dot(cap_ref[...], held[at, :], ((1,), (0,)))
        out_ref[0, :, h * HD : (h + 1) * HD] = part[:, :HD]
        out_ref[1, :, h * HD : (h + 1) * HD] = part[:, HD:]


def mod_kernel(scal, embed_ref, w_ref, out_ref):
    out_ref[...] = dot(embed_ref[...], w_ref[...].astype(bf16), ((1,), (0,)))


def turned_copy(source_ref, low, out_ref, block):
    def one(j, _):
        at = pl.ds(pl.multiple_of(j * block, block), block)
        out_ref[:, at] = jnp.transpose(source_ref[at, low : low + HD].astype(f32)).astype(bf16)
        return 0

    lax.fori_loop(0, source_ref.shape[0] // block, one, 0)


def self_kernel(table, q_ref, all_ref, sq_ref, sk_ref, out_ref, stat_ref, k_ref, vt_ref, *, block_k):
    i = pl.program_id(0)

    @pl.when(i == 0)
    def _():
        k_ref[...] = all_ref[:, HD : 2 * HD]
        turned_copy(all_ref, 2 * HD, vt_ref, block_k)

    q = q_ref[:, :HD]
    item_of_q = sq_ref[...]
    width = q.shape[0]

    def step(j, carry):
        top, total, out = carry
        at = pl.ds(pl.multiple_of(j * block_k, block_k), block_k)
        scores = dot(k_ref[at, :], q, ((1,), (1,)))
        scores = jnp.where(sk_ref[at, :] == item_of_q, scores, masked_score)
        new_top = jnp.maximum(top, jnp.max(scores, axis=0, keepdims=True))
        weights = jnp.exp(scores - new_top)
        shrink = jnp.exp(top - new_top)
        total = total * shrink + jnp.sum(weights, axis=0, keepdims=True)
        out = out * shrink + dot(vt_ref[:, at], weights.astype(bf16), ((1,), (0,)))
        return (new_top, total, out)

    start = (
        jnp.full((1, width), lowest_max, f32),
        jnp.zeros((1, width), f32),
        jnp.zeros((HD, width), f32),
    )
    top, total, out = lax.fori_loop(table[0, i], table[1, i], step, start)
    out_ref[...] = out / total
    stat_ref[...] = top + jnp.log(total)


def text_kernel(table, gate, q_ref, kv_ref, self_ref, sq_ref,
                mixed_ref, out_ref, stat_ref, k_ref, vt_ref):
    i = pl.program_id(0)

    @pl.when(i == 0)
    def _():
        k_ref[...] = kv_ref[:, :HD]
        turned_copy(kv_ref, HD, vt_ref, TEXT)

    q = q_ref[:, :HD]
    item_of_q = sq_ref[...]

    def step(item, carry):
        out, stat = carry
        at = pl.ds(pl.multiple_of(item * TEXT, TEXT), TEXT)
        scores = dot(k_ref[at, :], q, ((1,), (1,)))
        top = jnp.max(scores, axis=0, keepdims=True)
        weights = jnp.exp(scores - top)
        total = jnp.sum(weights, axis=0, keepdims=True)
        probs = (weights / total).astype(bf16)
        part = dot(vt_ref[:, at], probs, ((1,), (0,)))
        here = item_of_q == item
        return (jnp.where(here, part, out), jnp.where(here, top + jnp.log(total), stat))

    start = (jnp.zeros((HD, q.shape[0]), f32), jnp.zeros((1, q.shape[0]), f32))
    text_out, stat = lax.fori_loop(table[2, i], table[3, i], step, start)
    out_ref[...] = text_out
    stat_ref[...] = stat
    mixed_ref[...] = jnp.transpose(self_ref[...] + gate[0] * text_out).astype(bf16)


def text_back_kernel(table, gate, q_ref, g_ref, kv_ref, text_ref, stat_ref, sq_ref,
                     dkv_ref, dq_ref, cross_ref, k_ref, v_ref, kt_ref, dk_sum, dv_sum):
    i = pl.program_id(0)

    @pl.when(i == 0)
    def _():
        k_ref[...] = kv_ref[:, :HD]
        v_ref[...] = kv_ref[:, HD:]
        turned_copy(kv_ref, 0, kt_ref, TEXT)
        dk_sum[...] = jnp.zeros_like(dk_sum)
        dv_sum[...] = jnp.zeros_like(dv_sum)

    q = q_ref[:, :HD]
    item_of_q = sq_ref[...]
    g_value = g_ref[...].astype(f32)
    g = (g_value * gate[0]).astype(bf16)
    text_out = text_ref[...]
    cross_ref[...] = jnp.sum(jnp.transpose(g_value) * text_out, axis=0, keepdims=True)
    delta = jnp.sum(jnp.transpose(g.astype(f32)) * text_out, axis=0, keepdims=True)
    stat = stat_ref[...]

    def step(item, total):
        at = pl.ds(pl.multiple_of(item * TEXT, TEXT), TEXT)
        scores = dot(k_ref[at, :], q, ((1,), (1,)))
        probs = jnp.exp(jnp.where(item_of_q == item, scores - stat, masked_score))
        prob_grad = dot(v_ref[at, :], g, ((1,), (1,)))
        score_grad = (probs * (prob_grad - delta)).astype(bf16)
        dk_sum[at, :] += dot(score_grad, q, ((1,), (0,)))
        dv_sum[at, :] += dot(probs.astype(bf16), g, ((1,), (0,)))
        return total + dot(kt_ref[:, at], score_grad, ((1,), (0,)))

    start = jnp.zeros((HD, q.shape[0]), f32)
    dq_ref[...] = lax.fori_loop(table[2, i], table[3, i], step, start)

    @pl.when(i == pl.num_programs(0) - 1)
    def _():
        dkv_ref[:, :HD] = dk_sum[...].astype(bf16)
        dkv_ref[:, HD:] = dv_sum[...].astype(bf16)


def self_back_kernel(table, q_ref, g_ref, all_ref, self_ref, stat_ref, start_ref, sq_ref, sk_ref,
                     dqkv_ref, k_ref, v_ref, kt_ref, dk_sum, dv_sum, *, block_k):
    i = pl.program_id(0)

    @pl.when(i == 0)
    def _():
        k_ref[...] = all_ref[:, HD : 2 * HD]
        v_ref[...] = all_ref[:, 2 * HD :]
        turned_copy(all_ref, HD, kt_ref, block_k)
        dk_sum[...] = jnp.zeros_like(dk_sum)
        dv_sum[...] = jnp.zeros_like(dv_sum)

    q = q_ref[:, :HD]
    g = g_ref[...]
    item_of_q = sq_ref[...]
    delta = jnp.sum(jnp.transpose(g.astype(f32)) * self_ref[...], axis=0, keepdims=True)
    stat = stat_ref[...]

    def step(j, total):
        at = pl.ds(pl.multiple_of(j * block_k, block_k), block_k)
        scores = dot(k_ref[at, :], q, ((1,), (1,)))
        allowed = sk_ref[at, :] == item_of_q
        probs = jnp.exp(jnp.where(allowed, scores - stat, masked_score))
        prob_grad = dot(v_ref[at, :], g, ((1,), (1,)))
        score_grad = (probs * (prob_grad - delta)).astype(bf16)
        dk_sum[at, :] += dot(score_grad, q, ((1,), (0,)))
        dv_sum[at, :] += dot(probs.astype(bf16), g, ((1,), (0,)))
        return total + dot(kt_ref[:, at], score_grad, ((1,), (0,)))

    total = lax.fori_loop(table[0, i], table[1, i], step, start_ref[...])
    rows = q.shape[0]
    dqkv_ref[pl.ds(pl.multiple_of(i * rows, rows), rows), :HD] = jnp.transpose(
        total * score_scale
    ).astype(bf16)

    @pl.when(i == pl.num_programs(0) - 1)
    def _():
        dqkv_ref[:, HD : 2 * HD] = dk_sum[...].astype(bf16)
        dqkv_ref[:, 2 * HD :] = dv_sum[...].astype(bf16)


def attention_table(segments, block_q, block_k):
    by_block = segments.reshape(-1, block_q)
    low_item, high_item = by_block[:, 0], by_block[:, -1]
    first_key = jnp.sum(segments[None, :] < low_item[:, None], axis=1)
    end_key = jnp.sum(segments[None, :] <= high_item[:, None], axis=1)
    return jnp.stack(
        [first_key // block_k, (end_key + block_k - 1) // block_k, low_item, high_item + 1]
    ).astype(jnp.int32)


def per_device(
    x_tokens, caption, timesteps, segment_ids, out_grad,
    mod_weight, mod_first, mod_second,
    norm_gains, gains_first, gains_second,
    qkv_weight, qkv_first, qkv_second,
    out_weight, out_first, out_second,
    text_weight, text_first, text_second,
    cross_gates, cross_first, cross_second,
    updown_weight, updown_first, updown_second,
    down_weight, down_first, down_second,
    *, seq_size, tp_size,
):
    seq_index = lax.axis_index("seq")
    tp_index = lax.axis_index("tp")
    ring = Ring(seq_size)
    here, width = x_tokens.shape
    heads = cross_gates.shape[0]
    local_width = heads * HD
    count = here * seq_size
    units = down_weight.shape[0]
    quarter = width // tp_size
    first_owner = 1 if seq_size >= heads + 2 else 0
    owners = range(first_owner, first_owner + heads)
    seqs = jnp.full((seq_size,), seq_index)
    place = jnp.where(seqs % 2 == 0, seqs // 2, (15 - seqs) // 2)
    places = (place + jnp.arange(seq_size)) % seq_size
    slab_owner = jnp.where(places < 4, 2 * places, 15 - 2 * places).astype(jnp.int32)
    slab_head = jnp.clip(slab_owner - first_owner, 0, heads - 1)
    my_head = jnp.clip(seq_index - first_owner, 0, heads - 1)
    is_owner = (seq_index >= first_owner) & (seq_index < first_owner + heads)
    tps = jnp.full((1,), tp_index)
    scal = jnp.concatenate([place[:1], tps % 2, tps]).astype(jnp.int32)
    which = {"size": seq_size, "ring": ring.ring}

    def exchange(slabs):
        return lax.all_to_all(slabs, "seq", 0, 0, tiled=True)

    cap_rows = caption.shape[0]
    cap_cols = caption.shape[1] // seq_size
    cap_part = cap_cols // tp_size
    text_rows = cap_rows * seq_size
    if cap_part % 128 == 0:
        cap_own = call(
            lambda scal, in_ref, out_ref: out_ref.__setitem__(0, in_ref[...]),
            "caption_slabs", seq_size, [scal],
            [(caption, pl.BlockSpec((cap_rows, cap_part), lambda i, s: (0, i * tp_size + s[2])))],
            [
                (
                    (seq_size, cap_rows, cap_part), bf16,
                    pl.BlockSpec((1, cap_rows, cap_part), lambda i, s: (i, 0, 0)),
                )
            ],
            moved=2 * cap_rows * cap_cols * 4,
        )[0]
    else:
        cap_own = lax.dynamic_index_in_dim(
            caption.reshape(cap_rows, seq_size, tp_size, cap_part), tp_index, 2, keepdims=False
        )
        cap_own = jnp.transpose(cap_own, (1, 0, 2))
    silu_embed = jax.nn.silu(time_embed(timesteps)).astype(bf16)
    mod_rows = mod_weight.shape[0]
    silu_embed = once(silu_embed, cap_own)
    embed_rows = lax.dynamic_slice_in_dim(silu_embed, seq_index * mod_rows, mod_rows, 1)
    mod_part = call(
        mod_kernel, "modulation", 6, [scal],
        [
            (embed_rows, whole((ITEMS, mod_rows))),
            (mod_weight, pl.BlockSpec((mod_rows, quarter), lambda i, s: (0, i * tp_size + s[2]))),
        ],
        [((6 * ITEMS, quarter), f32, rows_block(ITEMS, quarter))],
        moved=mod_rows * 6 * quarter * 4, flops=2 * ITEMS * mod_rows * 6 * quarter,
    )[0]
    is_here = jnp.arange(seq_size) == seq_index
    slots = jnp.where(is_here[:, None], segment_ids.astype(f32)[None, :], 0.0).reshape(-1)
    gain_cols = norm_gains.shape[1]
    gain_slots = jnp.where(is_here[None, :, None], norm_gains[:, None, :], 0.0).reshape(-1)
    spare = -(slots.size + gain_slots.size) % (8 * quarter)
    packed = jnp.concatenate([slots, gain_slots, jnp.zeros((spare,), f32)]).reshape(-1, quarter)
    packed = butterfly(jnp.concatenate([mod_part, packed]), "seq", seq_size)
    modulation = gather_tp(packed[: 6 * ITEMS], 1)
    packed = packed[6 * ITEMS :].reshape(-1)
    segments = packed[:count].astype(jnp.int32)
    gains_value = packed[count : count + 2 * width].reshape(2, width).astype(bf16).astype(f32)
    gains_value = jnp.concatenate([gains_value] * 4)

    def turned(shard):
        return jnp.transpose(shard.astype(bf16), (1, 0, 2)).reshape(shard.shape[1], -1)

    attn_chunks = ring.gather(
        jnp.concatenate([turned(qkv_weight), out_weight.astype(bf16).T], axis=1)
    )
    pieces = len(attn_chunks)
    piece_sems = pltpu.SemaphoreType.DMA((pieces,))
    attn_ins = [(chunk, anywhere()) for chunk in attn_chunks]
    qkv_width = 3 * local_width

    def hop(chunks, k):
        return (chunks[k], chunks[-k]) if ring.ring else ()

    cap_own = once(exchange(cap_own), *hop(attn_chunks, 1))
    caption_cols = gather_tp(cap_own.reshape(text_rows, cap_part), 1)
    if ring.ring:
        text_slabs = call(
            text_heads_kernel, "text_heads", 1, [slab_head],
            [(text_weight, whole(text_weight.shape))],
            [((cap_cols, seq_size * 2 * HD), bf16, whole((cap_cols, seq_size * 2 * HD)))],
            [pltpu.VMEM((heads, cap_cols, 2 * HD), bf16)],
            moved=text_weight.size * 6,
        )[0]
        text_parts = dot(caption_cols, text_slabs, ((1,), (0,))).astype(bf16)

        text_sum = ring.reduce(
            lambda k: text_parts[:, 2 * k * HD : 2 * (k + 1) * HD], owners
        )
        next(text_sum)
    else:
        parts = jnp.einsum(
            "rc,jchd->hrjd", caption_cols,
            text_weight.astype(bf16).reshape(2, cap_cols, heads, HD), preferred_element_type=f32,
        ).reshape(heads, text_rows, 2 * HD)
        after = seq_size - heads - first_owner
        parts = jnp.pad(parts.astype(bf16), ((first_owner, after), (0, 0), (0, 0)))
        text_kv = lax.psum_scatter(parts, "seq", scatter_dimension=0, tiled=False)

    ffn_shard = jnp.concatenate([turned(updown_weight), down_weight.astype(bf16).T], axis=1)
    ffn_chunks = ring.gather(once(ffn_shard, packed, *([text_parts] if ring.ring else [])))
    ffn_ins = [(chunk, anywhere()) for chunk in ffn_chunks]
    text_sent = text_sum.send(()) if ring.ring else ()
    modulation = once(modulation, *hop(attn_chunks, 3), *hop(ffn_chunks, 1), *text_sent)
    segment_col = segment_ids[:, None]
    steps = here // ROWS
    segment_row = segment_ids.reshape(steps, 1, ROWS)
    row_ins = [
        (segment_col, rows_block(ROWS, 1)),
        (segment_row, pl.BlockSpec((1, 1, ROWS), lambda i, *_: (i, 0, 0))),
    ]
    block = rows_block(ROWS, width)
    mod_shape, gain_shape = modulation.shape, gains_value.shape
    x_rel, g_rel, mod_rel, gain_rel, hidden_attn = call(
        functools.partial(enter_kernel, **which), "enter", steps, [scal],
        [
            (x_tokens, block), (out_grad, block), (modulation, whole(mod_shape)),
            (gains_value, whole(gain_shape)), row_ins[0],
        ],
        [
            ((here, width), bf16, block), ((here, width), bf16, block),
            (mod_shape, f32, whole(mod_shape)), (gain_shape, f32, whole(gain_shape)),
            ((here, width), bf16, block),
        ],
        moved=here * width * 10,
    )
    mod_ins = [(mod_rel, whole(mod_shape)), (gain_rel, whole(gain_shape))]
    full_ins = mod_ins + [(segment_col, whole((here, 1)))]
    slab_shape = (seq_size, here, 3 * HD)
    slabs = call(
        functools.partial(
            project_kernel, heads=heads, first_owner=first_owner, count=pieces
        ),
        "project", 1, [],
        [(hidden_attn, whole((here, width)))] + attn_ins,
        [(slab_shape, bf16, whole(slab_shape))],
        [pltpu.VMEM((width, qkv_width), bf16), piece_sems],
        moved=width * qkv_width * 2, flops=2 * here * width * qkv_width,
    )[0]
    qkv_head = exchange(slabs).reshape(count, 3 * HD)

    block_q = math.gcd(count, 512)
    block_k = math.gcd(count, 512)
    table = attention_table(segments, block_q, block_k)
    tanh_cross = jnp.tanh(cross_gates)
    my_gate = jnp.sum(jnp.where(jnp.arange(heads) == my_head, tanh_cross, 0.0)).reshape(1)
    blocks = count // block_q
    q_ins = [(qkv_head, rows_block(block_q, 3 * HD))]
    seg_row = (segments[None, :], lanes_block(1, block_q))
    seg_col = (segments[:, None], whole((count, 1)))
    turned_out = ((HD, count), f32, lanes_block(HD, block_q))
    stat_out = ((1, count), f32, lanes_block(1, block_q))
    area = count * count * HD
    self_out, stat = call(
        functools.partial(self_kernel, block_k=block_k), "attend", blocks, [table],
        q_ins + [(qkv_head, whole(qkv_head.shape)), seg_row, seg_col],
        [turned_out, stat_out],
        [pltpu.VMEM((count, HD), bf16), pltpu.VMEM((HD, count), bf16)],
        flops=4 * area, moved=count * HD * 20, exps=count * count,
    )
    self_out = once(self_out, *hop(ffn_chunks, 2))
    if ring.ring:
        for held in ((slabs,), (qkv_head,), ()):
            text_kv = text_sum.send(held)
        text_kv = text_kv.astype(bf16)
    mixed_head, text_out, text_stat = call(
        text_kernel, "attend_text", blocks, [table, my_gate],
        q_ins
        + [(text_kv, whole(text_kv.shape)), (self_out, lanes_block(HD, block_q)), seg_row],
        [((count, HD), bf16, rows_block(block_q, HD)), turned_out, stat_out],
        [pltpu.VMEM((text_rows, HD), bf16), pltpu.VMEM((HD, text_rows), bf16)],
        flops=4 * count * TEXT * HD, moved=count * HD * 20, exps=count * TEXT,
    )
    mixed_head = once(mixed_head, *hop(ffn_chunks, 3))
    mixed_slabs = exchange(mixed_head.reshape(seq_size, here, HD))
    mixed_slabs = once(mixed_slabs, *(ffn_chunks[4:6] if ring.ring else ()))
    low, high = qkv_width, qkv_width + local_width
    head_args = {"heads": heads, "first_owner": first_owner, "count": pieces}
    half_shape = (here // 2, width)
    half_out = (half_shape, bf16, whole(half_shape))
    slab64 = (seq_size, here, HD)
    held_out = [pltpu.VMEM((width, local_width), bf16)]
    full_sum = [pltpu.VMEM((here, width), bf16), piece_sems]
    mixed, *attn = call(
        functools.partial(out_kernel, low=low, high=high, **head_args), "out", 1, [scal],
        [(mixed_slabs, whole(slab64))] + attn_ins,
        [((here, local_width), bf16, whole((here, local_width))), half_out, half_out],
        held_out + full_sum,
        moved=width * local_width * 2, flops=2 * here * width * local_width,
    )
    attn = psum_tp(attn)

    def halves(pair, spec=None):
        return [(one, spec or whole(half_shape)) for one in pair]

    tokens = (here, width)
    x_mid, hidden_ffn, ffn_grad, inner, both_grads, hm, ho, fm, fo = call(
        functools.partial(ffn_kernel, count=pieces, units=units), "ffn", 1, [scal],
        [(x_rel, whole(tokens)), (g_rel, whole(tokens))] + halves(attn) + full_ins + ffn_ins,
        [
            (tokens, f32, whole(tokens)), (tokens, bf16, whole(tokens)),
            (tokens, bf16, whole(tokens)), ((here, units), bf16, whole((here, units))),
            ((here, 2 * units), bf16, whole((here, 2 * units))),
            half_out, half_out, half_out, half_out,
        ],
        [pltpu.VMEM((width, 3 * units), bf16), pltpu.VMEM(tokens, bf16)] + full_sum,
        moved=width * 3 * units * 2, flops=12 * here * width * units,
    )
    hgrad = psum_tp((hm, ho))
    ffn_out = psum_tp(lax.optimization_barrier((fm, fo, *hgrad))[:2])
    mid_grad, attn_grad, grad_slabs = call(
        functools.partial(mid_kernel, low=low, high=high, **head_args), "mid", 1, [scal],
        [(x_mid, whole(tokens)), (g_rel, whole(tokens))] + halves(hgrad) + full_ins + attn_ins,
        [(tokens, f32, whole(tokens)), (tokens, bf16, whole(tokens)), (slab64, bf16, whole(slab64))],
        held_out + full_sum,
        moved=width * local_width * 2, flops=2 * here * width * local_width,
    )
    head_grad = exchange(grad_slabs).reshape(count, HD)
    ffn_sum = ring.reduce_products([(hidden_ffn, both_grads), (ffn_grad, inner)])
    next(ffn_sum)
    ffn_sum.send((grad_slabs,))
    head_grad = once(head_grad, *ffn_sum.send((head_grad,)))
    half_block = pl.BlockSpec((ROWS, width), lambda i, *_: (i % (steps // 2), 0))
    sums_shape, one_gain = (4 * ITEMS, width), (8, width)
    block_out, early_sums, early_gain = call(
        functools.partial(side_kernel, **which), "side", steps, [scal],
        [(x_mid, block), (mid_grad, block), (g_rel, block)]
        + halves(attn, half_block) + halves(ffn_out, half_block) + halves(hgrad, half_block)
        + mod_ins + row_ins,
        [(tokens, f32, block), (sums_shape, f32, whole(sums_shape)), (one_gain, f32, whole(one_gain))],
        moved=here * width * 24,
    )

    g_ins = [(head_grad, rows_block(block_q, HD))]
    kv64 = pltpu.VMEM((text_rows, HD), bf16)
    text_dkv, text_dq, cross_rows = call(
        text_back_kernel, "attend_text_back", blocks, [table, my_gate],
        q_ins + g_ins
        + [
            (text_kv, whole(text_kv.shape)), (text_out, lanes_block(HD, block_q)),
            (text_stat, lanes_block(1, block_q)), seg_row,
        ],
        [((text_rows, 2 * HD), bf16, whole((text_rows, 2 * HD))), turned_out, stat_out],
        [kv64, kv64, pltpu.VMEM((HD, text_rows), bf16)] + [pltpu.VMEM((text_rows, HD), f32)] * 2,
        flops=10 * count * TEXT * HD, moved=count * HD * 20, exps=count * TEXT,
    )
    head64 = pltpu.VMEM((count, HD), bf16)
    dqkv = call(
        functools.partial(self_back_kernel, block_k=block_k), "attend_back", blocks, [table],
        q_ins + g_ins
        + [
            (qkv_head, whole(qkv_head.shape)), (self_out, lanes_block(HD, block_q)),
            (stat, lanes_block(1, block_q)), (text_dq, lanes_block(HD, block_q)), seg_row, seg_col,
        ],
        [(qkv_head.shape, bf16, whole(qkv_head.shape))],
        [head64, head64, pltpu.VMEM((HD, count), bf16)] + [pltpu.VMEM((count, HD), f32)] * 2,
        flops=10 * area, moved=count * HD * 20, exps=count * count,
    )[0]

    back_slabs = exchange(dqkv.reshape(slab_shape))
    qkv_grads, *hidden_grad = call(
        functools.partial(qkv_back_kernel, **head_args), "qkv_back", 1, [scal],
        [(back_slabs, whole(slab_shape))] + attn_ins,
        [((here, qkv_width), bf16, whole((here, qkv_width))), half_out, half_out],
        [pltpu.VMEM((width, qkv_width), bf16)] + full_sum,
        moved=width * qkv_width * 2, flops=2 * here * width * qkv_width,
    )
    text_grads = ring.gather(text_dkv)
    if ring.ring:
        slab_at = jnp.argmax(
            slab_owner[None, :] == jnp.arange(first_owner, first_owner + heads)[:, None], axis=1
        ).astype(jnp.int32)
        text_owned = call(
            text_grad_kernel, "text_grad", 1, [slab_at],
            [(caption_cols.T, whole((cap_cols, text_rows)))]
            + [(one, anywhere()) for one in text_grads],
            [(text_weight.shape, f32, whole(text_weight.shape))],
            [
                pltpu.VMEM((seq_size * text_rows, 2 * HD), bf16),
                pltpu.SemaphoreType.DMA((len(text_grads),)),
            ],
            flops=4 * text_rows * cap_cols * local_width, moved=text_rows * cap_cols * 4,
        )[0]
    else:
        text_grads = text_grads[0].reshape(seq_size, text_rows, 2, HD)
        text_owned = jnp.einsum(
            "rc,hrjd->jchd", caption_cols, text_grads[first_owner : first_owner + heads],
            preferred_element_type=f32,
        ).reshape(text_weight.shape)

    attn_sum = ring.reduce_products([(hidden_attn, qkv_grads), (attn_grad, mixed)])
    next(attn_sum)
    ffn_sum.send((dqkv,))
    updown_rows, down_owned = ffn_sum.send(())
    for _ in range(4):
        attn_grads = attn_sum.send(())
    qkv_rows, out_owned = attn_grads
    hidden_grad = psum_tp(hidden_grad)
    all_sums = (6 * ITEMS, quarter)
    input_grad, item_sums, gain_sums = call(
        functools.partial(leave_kernel, **which), "leave", steps, [scal],
        [(x_rel, block), (mid_grad, block)] + halves(hidden_grad, half_block) + mod_ins + row_ins
        + [(early_sums, whole(sums_shape)), (early_gain, whole(one_gain))],
        [(tokens, f32, block), (all_sums, f32, whole(all_sums)), (one_gain, f32, whole(one_gain))],
        [pltpu.VMEM((6 * ITEMS + 8, width), f32)] * 2,
        moved=here * width * 16,
    )

    cross_here = jnp.where(
        is_owner & (jnp.arange(quarter) == my_head), jnp.sum(cross_rows), 0.0
    )
    packed = jnp.concatenate(
        [
            item_sums, gain_sums[:2].reshape(-1, quarter), cross_here[None],
            jnp.zeros((-(2 * tp_size + 1) % 8, quarter), f32),
        ]
    )
    packed = butterfly(packed, "seq", seq_size)
    item_mod_low = packed[: 6 * ITEMS].astype(bf16)
    gain_grads = packed[6 * ITEMS : 6 * ITEMS + 2 * tp_size].reshape(2, seq_size, gain_cols)
    gains_owned = jnp.sum(jnp.where(is_here[None, :, None], gain_grads, 0.0), axis=1)
    cross_total = packed[6 * ITEMS + 2 * tp_size, :heads] * (1.0 - tanh_cross * tanh_cross)

    def by_block(sums):
        return jnp.transpose(sums.reshape(6, ITEMS, -1), (1, 0, 2)).reshape(ITEMS, -1)

    mod_weight_grad = dot(embed_rows, by_block(gather_tp(item_mod_low, 1)), ((0,), (0,)))
    mod_quarter_grad = dot(embed_rows, by_block(item_mod_low), ((0,), (0,)))

    owned_square = (
        square_sum(qkv_rows)
        + square_sum(out_owned)
        + square_sum(text_owned)
        + square_sum(updown_rows)
        + square_sum(down_owned)
        + square_sum(mod_quarter_grad)
    )
    owned_square = owned_square + jnp.where(tp_index == 0, square_sum(gains_owned), 0.0)
    owned_square = owned_square + jnp.where(seq_index == 0, square_sum(cross_total), 0.0)
    total_square = jnp.full((8, 128), owned_square)
    total_square = butterfly(butterfly(total_square, "tp", tp_size), "seq", seq_size)[0, 0]
    grad_norm = jnp.sqrt(total_square)
    clip = jnp.minimum(1.0, clip_limit / (grad_norm + 1e-06))

    def unturned(rows, blocks):
        return jnp.transpose(rows.reshape(rows.shape[0], blocks, -1), (1, 0, 2))

    matrix = functools.partial(adam_update, clip=clip, rate=rate_matrix, decay=decay_matrix)
    small = functools.partial(adam_update, clip=clip, rate=rate_small, decay=0.0)
    return (
        block_out,
        input_grad,
        grad_norm,
        *matrix(mod_weight, mod_first, mod_second, mod_weight_grad),
        *small(norm_gains, gains_first, gains_second, gains_owned),
        *matrix(qkv_weight, qkv_first, qkv_second, unturned(qkv_rows, 3)),
        *matrix(out_weight, out_first, out_second, out_owned.T),
        *matrix(text_weight, text_first, text_second, text_owned),
        *small(cross_gates, cross_first, cross_second, cross_total),
        *matrix(updown_weight, updown_first, updown_second, unturned(updown_rows, 2)),
        *matrix(down_weight, down_first, down_second, down_owned.T),
    )


def solution(mesh):
    rows = P("seq", None)
    cols = P(None, "seq")
    split = P(None, "seq", "tp")
    turned = P("tp", "seq")
    heads = P("tp")
    weights = (rows,) * 3 + (cols,) * 3 + (split,) * 3 + (turned,) * 3 + (split,) * 3
    weights = weights + (heads,) * 3 + (split,) * 3 + (turned,) * 3
    return jax.shard_map(
        functools.partial(per_device, seq_size=mesh.shape["seq"], tp_size=mesh.shape["tp"]),
        mesh=mesh,
        in_specs=(rows, rows, P(), P("seq"), rows) + weights,
        out_specs=(rows, rows, P()) + weights,
        check_vma=False,
    )
```

```python
import functools
import math

import jax
import jax.numpy as jnp
from jax import lax
from jax.experimental import pallas as pl
from jax.experimental.pallas import tpu as pltpu
from jax.sharding import PartitionSpec as P

HD = 64
TE = 1024
TEXT = 256
ITEMS = 8
ADAM_STEP = 10

bf16 = jnp.bfloat16
f32 = jnp.float32
highest = lax.Precision.HIGHEST
eps_norm = 1e-06
masked_score = -1e30
lowest_max = -1e20
clip_limit = 1.0
beta_first = 0.9
beta_second = 0.95
adam_eps = 1e-08
rate_matrix = 0.05
rate_small = 0.5
decay_matrix = 0.1
score_scale = HD ** (-0.5)

WIDE = 256
ROWS = 128

CORE_SWAP = [(0, 1), (1, 0), (2, 3), (3, 2)]
Y_SWAP = [(0, 2), (2, 0), (1, 3), (3, 1)]
CYCLE = (0, 2, 4, 6, 7, 5, 3, 1)


def time_embed(timesteps):
    half_width = TE // 2
    frequency = jnp.exp(-math.log(10000.0) * jnp.arange(half_width, dtype=f32) / half_width)
    angles = 1000.0 * timesteps[:, None] * frequency[None, :]
    return jnp.concatenate([jnp.cos(angles), jnp.sin(angles)], axis=1)


def rms_parts(values):
    inverse = lax.rsqrt(jnp.mean(values * values, axis=-1, keepdims=True) + eps_norm)
    return (values * inverse, inverse)


def rms_back(normed, inverse, normed_grad):
    return inverse * (normed_grad - normed * jnp.mean(normed_grad * normed, axis=-1, keepdims=True))


def adam_update(weight, first, second, grad, clip, rate, decay):
    clipped = grad * clip
    first_new = beta_first * first + (1.0 - beta_first) * clipped
    second_new = beta_second * second + (1.0 - beta_second) * clipped * clipped
    first_hat = first_new / (1.0 - beta_first**ADAM_STEP)
    second_hat = second_new / (1.0 - beta_second**ADAM_STEP)
    weight_new = weight - rate * (first_hat / (jnp.sqrt(second_hat) + adam_eps) + decay * weight)
    return (weight_new, first_new, second_new)


def square_sum(values):
    return jnp.sum(values * values)


def dot(a, b, dims):
    return lax.dot_general(a, b, (dims, ((), ())), preferred_element_type=f32)


class Ring:
    def __init__(self, size):
        self.size = size
        self.ring = size == len(CYCLE)

    def hop(self, value, step, sends=None):
        n = self.size
        pairs = [(CYCLE[p], CYCLE[(p + step) % n]) for p in range(n) if sends is None or sends(p)]
        return lax.ppermute(value, "seq", pairs)

    def gather(self, own, held=((), (), ())):
        if not self.ring:
            return [lax.all_gather(own, "seq", axis=0, tiled=True)]
        half = own.shape[0] // 2
        ahead, behind = [own], [own]
        for i in range(3):
            ahead.append(self.hop(ahead[-1], 1))
            behind.append(self.hop(behind[-1], -1))
            if held[i]:
                ahead[-1], behind[-1] = lax.optimization_barrier(
                    (ahead[-1], behind[-1], *held[i])
                )[:2]
        far = [self.hop(behind[-1][:half], -1), self.hop(ahead[-1][half:], 1)]
        return behind + far + ahead[:0:-1]

    def reduce(self, block, active=None):
        rows = block(0).shape[0]
        half = rows // 2

        def sends(k):
            if active is None:
                return None
            return lambda p: CYCLE[(p + k) % self.size] in active

        def wait(held, *values):
            return lax.optimization_barrier((*values, *held))[: len(values)] if held else values

        def plus(part, moved):
            return (part.astype(f32) + moved.astype(f32)).astype(bf16)

        ahead, behind = block(4)[:half], block(4)[half:]
        for k in (3, 2, 1, 0):
            sent = (ahead, behind)
            ahead = self.hop(ahead, 1, sends(k + 1))
            behind = self.hop(behind, -1, sends(-k - 1))
            ahead, behind = wait((yield sent), ahead, behind)
            if k == 3:
                near, far = block(3), block(5)
                ahead = jnp.concatenate([plus(near[:half], ahead), near[half:]])
                behind = jnp.concatenate([far[:half], plus(far[half:], behind)])
            elif k:
                ahead, behind = plus(block(k), ahead), plus(block(8 - k), behind)
        yield block(0).astype(f32) + ahead.astype(f32) + behind.astype(f32)

    def reduce_products(self, pairs):
        parts = [dot(left, right, ((0,), (0,))).astype(bf16) for left, right in pairs]
        widths = [part.shape[1] for part in parts]
        edges = [sum(widths[:i]) for i in range(len(widths) + 1)]
        slab = parts[0].shape[0] // self.size

        def split(rows):
            return [rows[:, low:high] for low, high in zip(edges, edges[1:])]

        if not self.ring:
            for _ in range(4):
                yield ()
            rows = jnp.concatenate(parts, 1)
            rows = lax.psum_scatter(rows, "seq", scatter_dimension=0, tiled=True)
            yield split(rows.astype(f32))
            return

        ring = self.reduce(
            lambda k: jnp.concatenate([part[k * slab : (k + 1) * slab] for part in parts], axis=1)
        )
        held = yield next(ring)
        for _ in range(3):
            held = yield ring.send(held)
        yield split(ring.send(held))


def once(value, *others):
    return lax.optimization_barrier((value, *others))[0]


def butterfly(value, axis, size):
    step = 1
    while step < size:
        value = value + lax.ppermute(value, axis, [(i, i ^ step) for i in range(size)])
        step *= 2
    return value


def gather_tp(value, axis):
    tp = lax.axis_index("tp")

    def join(second, mine, other):
        low = jnp.where(second, other, mine)
        high = jnp.where(second, mine, other)
        return jnp.concatenate([low, high], axis)

    pair = join(tp % 2 == 1, value, lax.ppermute(value, "tp", CORE_SWAP))
    return join(tp >= 2, pair, lax.ppermute(pair, "tp", Y_SWAP))


def psum_tp(halves, held=()):
    mine, other = halves
    mine = (mine.astype(f32) + lax.ppermute(other, "tp", CORE_SWAP).astype(f32)).astype(bf16)
    mine = once(mine, *held)
    mine = (mine.astype(f32) + lax.ppermute(mine, "tp", Y_SWAP).astype(f32)).astype(bf16)
    return (mine, lax.ppermute(mine, "tp", CORE_SWAP))


def thirds(value):
    high = value.astype(bf16).astype(f32)
    rest = value - high
    middle = rest.astype(bf16).astype(f32)
    return jnp.concatenate([high, middle, rest - middle], axis=0).astype(bf16)


def item_sum(by_item, value):
    return dot(jnp.concatenate([by_item] * 3, axis=1).astype(bf16), thirds(value), ((1,), (0,)))


def anywhere():
    return pl.BlockSpec(memory_space=pl.ANY)


def whole(shape):
    return pl.BlockSpec(
        shape, lambda i, *_: (0,) * len(shape), pipeline_mode=pl.Buffered(1)
    )


def rows_block(block, width):
    return pl.BlockSpec((block, width), lambda i, *_: (i, 0))


def lanes_block(rows, block):
    return pl.BlockSpec((rows, block), lambda i, *_: (0, i))


def shape_of(shape, dtype):
    return jax.ShapeDtypeStruct(shape, dtype)


def call(kernel, name, grid, scalars, ins, outs, scratch=(), flops=0, moved=0, exps=0):
    return pl.pallas_call(
        kernel,
        out_shape=tuple(shape_of(shape, dtype) for shape, dtype, _ in outs),
        grid_spec=pltpu.PrefetchScalarGridSpec(
            num_scalar_prefetch=len(scalars),
            grid=(grid,),
            in_specs=[spec for _, spec in ins],
            out_specs=tuple(spec for _, _, spec in outs),
            scratch_shapes=list(scratch),
        ),
        cost_estimate=pl.CostEstimate(flops=flops, bytes_accessed=moved, transcendentals=exps),
        name=name,
    )(*scalars, *[array for array, _ in ins])


def starts_of(chunks):
    at = 0
    for chunk in chunks:
        yield at
        at += chunk.shape[0]


def chunk_copies(chunks, low, high, held, sems):
    return [
        pltpu.make_async_copy(
            chunk.at[:, low:high], held.at[start : start + chunk.shape[0], :], sems.at[j]
        )
        for j, (chunk, start) in enumerate(zip(chunks, starts_of(chunks)))
    ]


def relative_store(ring_size, ring, place, out_ref, value):
    slab = value.shape[1] // ring_size
    if not ring:
        out_ref[...] = value
        return
    for p in range(ring_size):

        @pl.when(place == p)
        def _(p=p):
            for k in range(ring_size):
                s = CYCLE[(p + k) % ring_size]
                out_ref[:, k * slab : (k + 1) * slab] = value[:, s * slab : (s + 1) * slab]


def absolute_store(ring_size, ring, place, out_ref, value):
    slab = value.shape[1] // ring_size
    if not ring:
        out_ref[...] = value
        return
    for p in range(ring_size):

        @pl.when(place == p)
        def _(p=p):
            for k in range(ring_size):
                s = CYCLE[(p + k) % ring_size]
                out_ref[:, s * slab : (s + 1) * slab] = value[:, k * slab : (k + 1) * slab]


def onehot_rows(segment_col):
    items = lax.broadcasted_iota(jnp.int32, (segment_col.shape[0], 3 * ITEMS), 1) % ITEMS
    return (segment_col == items).astype(f32).astype(bf16)


def onehot_cols(segment_row):
    items = lax.broadcasted_iota(jnp.int32, (ITEMS, segment_row.shape[1]), 0)
    return (segment_row == items).astype(f32)


def modulate(onehot, mod_ref, block):
    return dot(onehot, thirds(mod_ref[block * ITEMS : (block + 1) * ITEMS, :]), ((1,), (0,)))


def enter_kernel(scal, x_ref, g_ref, mod_ref, gain_ref, sc_ref,
                 xr_ref, gr_ref, modr_ref, gainr_ref, hidden_ref, *, size, ring):
    place = scal[0]

    @pl.when(pl.program_id(0) == 0)
    def _():
        relative_store(size, ring, place, modr_ref, mod_ref[...])
        relative_store(size, ring, place, gainr_ref, gain_ref[...])

    relative_store(size, ring, place, xr_ref, x_ref[...])
    relative_store(size, ring, place, gr_ref, g_ref[...])
    x = xr_ref[...].astype(f32)
    normed, _ = rms_parts(x)
    onehot = onehot_rows(sc_ref[...])
    scale = modulate(onehot, modr_ref, 1)
    shift = modulate(onehot, modr_ref, 0)
    hidden_ref[...] = (normed * gainr_ref[0:1, :] * (1.0 + scale) + shift).astype(bf16)


def project_kernel(hidden_ref, *refs, heads, first_owner, count):
    chunks, (slab_ref, held, sems) = refs[:count], refs[count:]
    width = heads * HD
    copies = chunk_copies(chunks, 0, 3 * width, held, sems)
    for one in copies:
        one.start()
    for s in range(slab_ref.shape[0]):
        if not first_owner <= s < first_owner + heads:
            slab_ref[s] = jnp.zeros(slab_ref.shape[1:], bf16)
    for one in copies:
        one.wait()
    hidden = hidden_ref[...]
    for j in range(3):
        part = dot(hidden, held[:, j * width : (j + 1) * width], ((1,), (0,))).astype(bf16)
        if j == 0:
            part = part * jnp.asarray(score_scale, bf16)
        for h in range(heads):
            slab_ref[first_owner + h, :, j * HD : (j + 1) * HD] = part[:, h * HD : (h + 1) * HD]


def split_halves(core, full_ref, mine_ref, other_ref):
    half = mine_ref.shape[0]
    mine_ref[...] = full_ref[pl.ds(pl.multiple_of(core * half, half), half), :]
    other_ref[...] = full_ref[pl.ds(pl.multiple_of((1 - core) * half, half), half), :]


def join_halves(core, mine_ref, other_ref, full_ref):
    half = mine_ref.shape[0]
    full_ref[pl.ds(pl.multiple_of(core * half, half), half), :] = mine_ref[...]
    full_ref[pl.ds(pl.multiple_of((1 - core) * half, half), half), :] = other_ref[...]


def times_turned(value_ref, held, full_ref):
    tiles = held.shape[0] // WIDE

    def one(i, _):
        at = pl.ds(pl.multiple_of(i * WIDE, WIDE), WIDE)
        full_ref[:, at] = dot(value_ref[...], held[at, :], ((1,), (1,))).astype(bf16)
        return 0

    lax.fori_loop(0, tiles, one, 0, unroll=True)


def out_kernel(scal, slab_ref, *refs, heads, first_owner, count, low, high):
    chunks, (mixed_ref, mine_ref, other_ref, held, full, sems) = refs[:count], refs[count:]
    copies = chunk_copies(chunks, low, high, held, sems)
    for one in copies:
        one.start()
    for h in range(heads):
        mixed_ref[:, h * HD : (h + 1) * HD] = slab_ref[first_owner + h]
    for one in copies:
        one.wait()
    times_turned(mixed_ref, held, full)
    split_halves(scal[1], full, mine_ref, other_ref)


def qkv_back_kernel(scal, slab_ref, *refs, heads, first_owner, count):
    chunks, (grads_ref, mine_ref, other_ref, held, full, sems) = refs[:count], refs[count:]
    width = heads * HD
    copies = chunk_copies(chunks, 0, 3 * width, held, sems)
    for one in copies:
        one.start()
    for j in range(3):
        for h in range(heads):
            at = j * width + h * HD
            grads_ref[:, at : at + HD] = slab_ref[first_owner + h, :, j * HD : (j + 1) * HD]
    for one in copies:
        one.wait()
    times_turned(grads_ref, held, full)
    split_halves(scal[1], full, mine_ref, other_ref)


def ffn_kernel(scal, x_ref, g_ref, am_ref, ao_ref, modr_ref, gainr_ref, sc_ref, *refs,
               count, units):
    chunks = refs[:count]
    (mid_ref, hidden_ref, fgrad_ref, inner_ref, both_ref, hm_ref, ho_ref, fm_ref, fo_ref,
     held, attn, full, sems) = refs[count:]
    core = scal[1]
    copies = chunk_copies(chunks, 0, held.shape[1], held, sems)
    for one in copies:
        one.start()
    join_halves(core, am_ref, ao_ref, attn)

    def prepare(i, _):
        at = pl.ds(pl.multiple_of(i * ROWS, ROWS), ROWS)
        onehot = onehot_rows(sc_ref[at, :])
        x_mid = x_ref[at, :].astype(f32) + jnp.tanh(modulate(onehot, modr_ref, 2)) * attn[
            at, :
        ].astype(f32)
        mid_ref[at, :] = x_mid
        normed, _ = rms_parts(x_mid)
        scale = modulate(onehot, modr_ref, 4)
        shift = modulate(onehot, modr_ref, 3)
        hidden_ref[at, :] = (normed * gainr_ref[1:2, :] * (1.0 + scale) + shift).astype(bf16)
        tanh_ffn = jnp.tanh(modulate(onehot, modr_ref, 5))
        fgrad_ref[at, :] = (g_ref[at, :].astype(f32) * tanh_ffn).astype(bf16)
        return 0

    lax.fori_loop(0, x_ref.shape[0] // ROWS, prepare, 0)
    for one in copies:
        one.wait()

    def tile(i, _):
        def at(base):
            return pl.ds(pl.multiple_of(base + i * WIDE, WIDE), WIDE)

        gate_pre = dot(hidden_ref[...], held[:, at(0)], ((1,), (0,)))
        up_pre = dot(hidden_ref[...], held[:, at(units)], ((1,), (0,)))
        inner_grad = dot(fgrad_ref[...], held[:, at(2 * units)], ((1,), (0,)))
        sigmoid = jax.nn.sigmoid(gate_pre)
        silu = gate_pre * sigmoid
        inner_ref[:, at(0)] = (silu * up_pre).astype(bf16)
        both_ref[:, at(0)] = (
            inner_grad * up_pre * sigmoid * (1.0 + gate_pre * (1.0 - sigmoid))
        ).astype(bf16)
        both_ref[:, at(units)] = (inner_grad * silu).astype(bf16)
        return 0

    lax.fori_loop(0, units // WIDE, tile, 0, unroll=True)
    times_turned(both_ref, held.at[:, 0 : 2 * units], full)
    split_halves(core, full, hm_ref, ho_ref)
    times_turned(inner_ref, held.at[:, 2 * units : 3 * units], full)
    split_halves(core, full, fm_ref, fo_ref)


def mid_kernel(scal, mid_ref, g_ref, hm_ref, ho_ref, modr_ref, gainr_ref, sc_ref, *refs,
               heads, first_owner, count, low, high):
    chunks = refs[:count]
    grad_ref, agrad_ref, slab_ref, held, hgrad, sems = refs[count:]
    copies = chunk_copies(chunks, low, high, held, sems)
    for one in copies:
        one.start()
    join_halves(scal[1], hm_ref, ho_ref, hgrad)
    for s in range(slab_ref.shape[0]):
        if not first_owner <= s < first_owner + heads:
            slab_ref[s] = jnp.zeros(slab_ref.shape[1:], bf16)

    def prepare(i, _):
        at = pl.ds(pl.multiple_of(i * ROWS, ROWS), ROWS)
        onehot = onehot_rows(sc_ref[at, :])
        normed, inverse = rms_parts(mid_ref[at, :])
        scale = modulate(onehot, modr_ref, 4)
        normed_grad = hgrad[at, :].astype(f32) * gainr_ref[1:2, :] * (1.0 + scale)
        grad = g_ref[at, :].astype(f32) + rms_back(normed, inverse, normed_grad)
        grad_ref[at, :] = grad
        agrad_ref[at, :] = (grad * jnp.tanh(modulate(onehot, modr_ref, 2))).astype(bf16)
        return 0

    lax.fori_loop(0, mid_ref.shape[0] // ROWS, prepare, 0)
    for one in copies:
        one.wait()
    mixed = dot(agrad_ref[...], held[...], ((1,), (0,))).astype(bf16)
    for h in range(heads):
        slab_ref[first_owner + h] = mixed[:, h * HD : (h + 1) * HD]


def own_rows(core, mine_ref, other_ref):
    first = pl.program_id(0) < pl.num_programs(0) // 2
    mine = jnp.logical_xor(first, core == 1)
    return jnp.where(mine, mine_ref[...].astype(f32), other_ref[...].astype(f32))


def side_kernel(scal, mid_ref, grad_ref, g_ref, am_ref, ao_ref, fm_ref, fo_ref, hm_ref, ho_ref,
                modr_ref, gainr_ref, sc_ref, sr_ref,
                block_ref, sums_ref, gain_ref, *, size, ring):
    place, core = scal[0], scal[1]

    @pl.when(pl.program_id(0) == 0)
    def _():
        sums_ref[...] = jnp.zeros_like(sums_ref)
        gain_ref[...] = jnp.zeros_like(gain_ref)

    attn = own_rows(core, am_ref, ao_ref)
    ffn_out = own_rows(core, fm_ref, fo_ref)
    hgrad = own_rows(core, hm_ref, ho_ref)
    onehot = onehot_rows(sc_ref[...])
    by_item = onehot_cols(sr_ref[0])
    tanh_attn = jnp.tanh(modulate(onehot, modr_ref, 2))
    tanh_ffn = jnp.tanh(modulate(onehot, modr_ref, 5))
    scale = modulate(onehot, modr_ref, 4)
    x_mid = mid_ref[...]
    absolute_store(size, ring, place, block_ref, x_mid + tanh_ffn * ffn_out)
    normed, _ = rms_parts(x_mid)

    def add(block, value):
        sums_ref[block * ITEMS : (block + 1) * ITEMS, :] += item_sum(by_item, value)

    add(0, grad_ref[...] * attn * (1.0 - tanh_attn * tanh_attn))
    add(1, hgrad)
    add(2, hgrad * normed * gainr_ref[1:2, :])
    add(3, g_ref[...].astype(f32) * ffn_out * (1.0 - tanh_ffn * tanh_ffn))
    gain_ref[0:1, :] += jnp.sum(hgrad * normed * (1.0 + scale), axis=0, keepdims=True)


def leave_kernel(scal, x_ref, grad_ref, hm_ref, ho_ref, modr_ref, gainr_ref, sc_ref, sr_ref,
                 early_ref, egain_ref, input_ref, sums_ref, gain_ref, total, turned, *, size, ring):
    place, core = scal[0], scal[1]

    @pl.when(pl.program_id(0) == 0)
    def _():
        total[...] = jnp.zeros_like(total)
        total[2 * ITEMS : 6 * ITEMS, :] = early_ref[...]
        total[6 * ITEMS + 1 : 6 * ITEMS + 2, :] = egain_ref[0:1, :]

    hgrad = own_rows(core, hm_ref, ho_ref)
    onehot = onehot_rows(sc_ref[...])
    by_item = onehot_cols(sr_ref[0])
    scale = modulate(onehot, modr_ref, 1)
    normed, inverse = rms_parts(x_ref[...].astype(f32))
    normed_grad = hgrad * gainr_ref[0:1, :] * (1.0 + scale)
    absolute_store(
        size, ring, place, input_ref, grad_ref[...] + rms_back(normed, inverse, normed_grad)
    )
    total[0:ITEMS, :] += item_sum(by_item, hgrad)
    total[ITEMS : 2 * ITEMS, :] += item_sum(by_item, hgrad * normed * gainr_ref[0:1, :])
    total[6 * ITEMS : 6 * ITEMS + 1, :] += jnp.sum(
        hgrad * normed * (1.0 + scale), axis=0, keepdims=True
    )

    @pl.when(pl.program_id(0) == pl.num_programs(0) - 1)
    def _():
        absolute_store(size, ring, place, turned, total[...])
        quarter = sums_ref.shape[1]
        at = pl.ds(pl.multiple_of(scal[2] * quarter, quarter), quarter)
        sums_ref[...] = turned[0 : 6 * ITEMS, at]
        gain_ref[...] = turned[6 * ITEMS : 6 * ITEMS + 8, :]


def text_heads_kernel(head_of, w_ref, out_ref, by_head):
    for h in range(by_head.shape[0]):
        for j in range(2):
            by_head[h, :, j * HD : (j + 1) * HD] = w_ref[j, :, h * HD : (h + 1) * HD].astype(bf16)
    for k in range(out_ref.shape[1] // (2 * HD)):
        out_ref[:, 2 * k * HD : 2 * (k + 1) * HD] = by_head[head_of[k]]


def text_grad_kernel(slab_at, cap_ref, *refs):
    chunks, (out_ref, held, sems) = refs[:-3], refs[-3:]
    copies = chunk_copies(chunks, 0, 2 * HD, held, sems)
    for one in copies:
        one.start()
    for one in copies:
        one.wait()
    rows = cap_ref.shape[1]
    for h in range(out_ref.shape[2] // HD):
        at = pl.ds(pl.multiple_of(slab_at[h] * rows, rows), rows)
        part = dot(cap_ref[...], held[at, :], ((1,), (0,)))
        out_ref[0, :, h * HD : (h + 1) * HD] = part[:, :HD]
        out_ref[1, :, h * HD : (h + 1) * HD] = part[:, HD:]


def mod_kernel(scal, embed_ref, w_ref, out_ref):
    out_ref[...] = dot(embed_ref[...], w_ref[...].astype(bf16), ((1,), (0,)))


def turned_copy(source_ref, low, out_ref, block):
    def one(j, _):
        at = pl.ds(pl.multiple_of(j * block, block), block)
        out_ref[:, at] = jnp.transpose(source_ref[at, low : low + HD].astype(f32)).astype(bf16)
        return 0

    lax.fori_loop(0, source_ref.shape[0] // block, one, 0)


def self_kernel(table, q_ref, all_ref, sq_ref, sk_ref, out_ref, stat_ref, k_ref, vt_ref, *, block_k):
    i = pl.program_id(0)

    @pl.when(i == 0)
    def _():
        k_ref[...] = all_ref[:, HD : 2 * HD]
        turned_copy(all_ref, 2 * HD, vt_ref, block_k)

    q = q_ref[:, :HD]
    item_of_q = sq_ref[...]
    width = q.shape[0]

    def step(j, carry):
        top, total, out = carry
        at = pl.ds(pl.multiple_of(j * block_k, block_k), block_k)
        scores = dot(k_ref[at, :], q, ((1,), (1,)))
        scores = jnp.where(sk_ref[at, :] == item_of_q, scores, masked_score)
        new_top = jnp.maximum(top, jnp.max(scores, axis=0, keepdims=True))
        weights = jnp.exp(scores - new_top)
        shrink = jnp.exp(top - new_top)
        total = total * shrink + jnp.sum(weights, axis=0, keepdims=True)
        out = out * shrink + dot(vt_ref[:, at], weights.astype(bf16), ((1,), (0,)))
        return (new_top, total, out)

    start = (
        jnp.full((1, width), lowest_max, f32),
        jnp.zeros((1, width), f32),
        jnp.zeros((HD, width), f32),
    )
    top, total, out = lax.fori_loop(table[0, i], table[1, i], step, start)
    out_ref[...] = out / total
    stat_ref[...] = top + jnp.log(total)


def text_kernel(table, gate, q_ref, kv_ref, self_ref, sq_ref,
                mixed_ref, out_ref, stat_ref, k_ref, vt_ref):
    i = pl.program_id(0)

    @pl.when(i == 0)
    def _():
        k_ref[...] = kv_ref[:, :HD]
        turned_copy(kv_ref, HD, vt_ref, TEXT)

    q = q_ref[:, :HD]
    item_of_q = sq_ref[...]

    def step(item, carry):
        out, stat = carry
        at = pl.ds(pl.multiple_of(item * TEXT, TEXT), TEXT)
        scores = dot(k_ref[at, :], q, ((1,), (1,)))
        top = jnp.max(scores, axis=0, keepdims=True)
        weights = jnp.exp(scores - top)
        total = jnp.sum(weights, axis=0, keepdims=True)
        probs = (weights / total).astype(bf16)
        part = dot(vt_ref[:, at], probs, ((1,), (0,)))
        here = item_of_q == item
        return (jnp.where(here, part, out), jnp.where(here, top + jnp.log(total), stat))

    start = (jnp.zeros((HD, q.shape[0]), f32), jnp.zeros((1, q.shape[0]), f32))
    text_out, stat = lax.fori_loop(table[2, i], table[3, i], step, start)
    out_ref[...] = text_out
    stat_ref[...] = stat
    mixed_ref[...] = jnp.transpose(self_ref[...] + gate[0] * text_out).astype(bf16)


def text_back_kernel(table, gate, q_ref, g_ref, kv_ref, text_ref, stat_ref, sq_ref,
                     dkv_ref, dq_ref, cross_ref, k_ref, v_ref, kt_ref, dk_sum, dv_sum):
    i = pl.program_id(0)

    @pl.when(i == 0)
    def _():
        k_ref[...] = kv_ref[:, :HD]
        v_ref[...] = kv_ref[:, HD:]
        turned_copy(kv_ref, 0, kt_ref, TEXT)
        dk_sum[...] = jnp.zeros_like(dk_sum)
        dv_sum[...] = jnp.zeros_like(dv_sum)

    q = q_ref[:, :HD]
    item_of_q = sq_ref[...]
    g_value = g_ref[...].astype(f32)
    g = (g_value * gate[0]).astype(bf16)
    text_out = text_ref[...]
    cross_ref[...] = jnp.sum(jnp.transpose(g_value) * text_out, axis=0, keepdims=True)
    delta = jnp.sum(jnp.transpose(g.astype(f32)) * text_out, axis=0, keepdims=True)
    stat = stat_ref[...]

    def step(item, total):
        at = pl.ds(pl.multiple_of(item * TEXT, TEXT), TEXT)
        scores = dot(k_ref[at, :], q, ((1,), (1,)))
        probs = jnp.exp(jnp.where(item_of_q == item, scores - stat, masked_score))
        prob_grad = dot(v_ref[at, :], g, ((1,), (1,)))
        score_grad = (probs * (prob_grad - delta)).astype(bf16)
        dk_sum[at, :] += dot(score_grad, q, ((1,), (0,)))
        dv_sum[at, :] += dot(probs.astype(bf16), g, ((1,), (0,)))
        return total + dot(kt_ref[:, at], score_grad, ((1,), (0,)))

    start = jnp.zeros((HD, q.shape[0]), f32)
    dq_ref[...] = lax.fori_loop(table[2, i], table[3, i], step, start)

    @pl.when(i == pl.num_programs(0) - 1)
    def _():
        dkv_ref[:, :HD] = dk_sum[...].astype(bf16)
        dkv_ref[:, HD:] = dv_sum[...].astype(bf16)


def self_back_kernel(table, q_ref, g_ref, all_ref, self_ref, stat_ref, start_ref, sq_ref, sk_ref,
                     dqkv_ref, k_ref, v_ref, kt_ref, dk_sum, dv_sum, *, block_k):
    i = pl.program_id(0)

    @pl.when(i == 0)
    def _():
        k_ref[...] = all_ref[:, HD : 2 * HD]
        v_ref[...] = all_ref[:, 2 * HD :]
        turned_copy(all_ref, HD, kt_ref, block_k)
        dk_sum[...] = jnp.zeros_like(dk_sum)
        dv_sum[...] = jnp.zeros_like(dv_sum)

    q = q_ref[:, :HD]
    g = g_ref[...]
    item_of_q = sq_ref[...]
    delta = jnp.sum(jnp.transpose(g.astype(f32)) * self_ref[...], axis=0, keepdims=True)
    stat = stat_ref[...]

    def step(j, total):
        at = pl.ds(pl.multiple_of(j * block_k, block_k), block_k)
        scores = dot(k_ref[at, :], q, ((1,), (1,)))
        allowed = sk_ref[at, :] == item_of_q
        probs = jnp.exp(jnp.where(allowed, scores - stat, masked_score))
        prob_grad = dot(v_ref[at, :], g, ((1,), (1,)))
        score_grad = (probs * (prob_grad - delta)).astype(bf16)
        dk_sum[at, :] += dot(score_grad, q, ((1,), (0,)))
        dv_sum[at, :] += dot(probs.astype(bf16), g, ((1,), (0,)))
        return total + dot(kt_ref[:, at], score_grad, ((1,), (0,)))

    total = lax.fori_loop(table[0, i], table[1, i], step, start_ref[...])
    rows = q.shape[0]
    dqkv_ref[pl.ds(pl.multiple_of(i * rows, rows), rows), :HD] = jnp.transpose(
        total * score_scale
    ).astype(bf16)

    @pl.when(i == pl.num_programs(0) - 1)
    def _():
        dqkv_ref[:, HD : 2 * HD] = dk_sum[...].astype(bf16)
        dqkv_ref[:, 2 * HD :] = dv_sum[...].astype(bf16)


def attention_table(segments, block_q, block_k):
    by_block = segments.reshape(-1, block_q)
    low_item, high_item = by_block[:, 0], by_block[:, -1]
    first_key = jnp.sum(segments[None, :] < low_item[:, None], axis=1)
    end_key = jnp.sum(segments[None, :] <= high_item[:, None], axis=1)
    return jnp.stack(
        [first_key // block_k, (end_key + block_k - 1) // block_k, low_item, high_item + 1]
    ).astype(jnp.int32)


def per_device(
    x_tokens, caption, timesteps, segment_ids, out_grad,
    mod_weight, mod_first, mod_second,
    norm_gains, gains_first, gains_second,
    qkv_weight, qkv_first, qkv_second,
    out_weight, out_first, out_second,
    text_weight, text_first, text_second,
    cross_gates, cross_first, cross_second,
    updown_weight, updown_first, updown_second,
    down_weight, down_first, down_second,
    *, seq_size, tp_size,
):
    seq_index = lax.axis_index("seq")
    tp_index = lax.axis_index("tp")
    ring = Ring(seq_size)
    here, width = x_tokens.shape
    heads = cross_gates.shape[0]
    local_width = heads * HD
    count = here * seq_size
    units = down_weight.shape[0]
    quarter = width // tp_size
    first_owner = 1 if seq_size >= heads + 2 else 0
    owners = range(first_owner, first_owner + heads)
    seqs = jnp.full((seq_size,), seq_index)
    place = jnp.where(seqs % 2 == 0, seqs // 2, (15 - seqs) // 2)
    places = (place + jnp.arange(seq_size)) % seq_size
    slab_owner = jnp.where(places < 4, 2 * places, 15 - 2 * places).astype(jnp.int32)
    slab_head = jnp.clip(slab_owner - first_owner, 0, heads - 1)
    my_head = jnp.clip(seq_index - first_owner, 0, heads - 1)
    is_owner = (seq_index >= first_owner) & (seq_index < first_owner + heads)
    tps = jnp.full((1,), tp_index)
    scal = jnp.concatenate([place[:1], tps % 2, tps]).astype(jnp.int32)
    which = {"size": seq_size, "ring": ring.ring}

    def exchange(slabs):
        return lax.all_to_all(slabs, "seq", 0, 0, tiled=True)

    cap_rows = caption.shape[0]
    cap_cols = caption.shape[1] // seq_size
    cap_part = cap_cols // tp_size
    text_rows = cap_rows * seq_size
    if cap_part % 128 == 0:
        cap_own = call(
            lambda scal, in_ref, out_ref: out_ref.__setitem__(0, in_ref[...]),
            "caption_slabs", seq_size, [scal],
            [(caption, pl.BlockSpec((cap_rows, cap_part), lambda i, s: (0, i * tp_size + s[2])))],
            [
                (
                    (seq_size, cap_rows, cap_part), bf16,
                    pl.BlockSpec((1, cap_rows, cap_part), lambda i, s: (i, 0, 0)),
                )
            ],
            moved=2 * cap_rows * cap_cols * 4,
        )[0]
    else:
        cap_own = lax.dynamic_index_in_dim(
            caption.reshape(cap_rows, seq_size, tp_size, cap_part), tp_index, 2, keepdims=False
        )
        cap_own = jnp.transpose(cap_own, (1, 0, 2))
    silu_embed = jax.nn.silu(time_embed(timesteps)).astype(bf16)
    mod_rows = mod_weight.shape[0]
    silu_embed = once(silu_embed, cap_own)
    embed_rows = lax.dynamic_slice_in_dim(silu_embed, seq_index * mod_rows, mod_rows, 1)
    mod_part = call(
        mod_kernel, "modulation", 6, [scal],
        [
            (embed_rows, whole((ITEMS, mod_rows))),
            (mod_weight, pl.BlockSpec((mod_rows, quarter), lambda i, s: (0, i * tp_size + s[2]))),
        ],
        [((6 * ITEMS, quarter), f32, rows_block(ITEMS, quarter))],
        moved=mod_rows * 6 * quarter * 4, flops=2 * ITEMS * mod_rows * 6 * quarter,
    )[0]
    is_here = jnp.arange(seq_size) == seq_index
    slots = jnp.where(is_here[:, None], segment_ids.astype(f32)[None, :], 0.0).reshape(-1)
    gain_cols = norm_gains.shape[1]
    gain_slots = jnp.where(is_here[None, :, None], norm_gains[:, None, :], 0.0).reshape(-1)
    spare = -(slots.size + gain_slots.size) % (8 * quarter)
    packed = jnp.concatenate([slots, gain_slots, jnp.zeros((spare,), f32)]).reshape(-1, quarter)
    packed = butterfly(jnp.concatenate([mod_part, packed]), "seq", seq_size)
    modulation = gather_tp(packed[: 6 * ITEMS], 1)
    packed = packed[6 * ITEMS :].reshape(-1)
    segments = packed[:count].astype(jnp.int32)
    gains_value = packed[count : count + 2 * width].reshape(2, width).astype(bf16).astype(f32)
    gains_value = jnp.concatenate([gains_value] * 4)

    def turned(shard):
        return jnp.transpose(shard.astype(bf16), (1, 0, 2)).reshape(shard.shape[1], -1)

    attn_chunks = ring.gather(
        jnp.concatenate([turned(qkv_weight), out_weight.astype(bf16).T], axis=1)
    )
    pieces = len(attn_chunks)
    piece_sems = pltpu.SemaphoreType.DMA((pieces,))
    attn_ins = [(chunk, anywhere()) for chunk in attn_chunks]
    qkv_width = 3 * local_width

    def hop(chunks, k):
        return (chunks[k], chunks[-k]) if ring.ring else ()

    cap_own = once(exchange(cap_own), *hop(attn_chunks, 1))
    caption_cols = gather_tp(cap_own.reshape(text_rows, cap_part), 1)
    if ring.ring:
        text_slabs = call(
            text_heads_kernel, "text_heads", 1, [slab_head],
            [(text_weight, whole(text_weight.shape))],
            [((cap_cols, seq_size * 2 * HD), bf16, whole((cap_cols, seq_size * 2 * HD)))],
            [pltpu.VMEM((heads, cap_cols, 2 * HD), bf16)],
            moved=text_weight.size * 6,
        )[0]
        text_parts = dot(caption_cols, text_slabs, ((1,), (0,))).astype(bf16)

        text_sum = ring.reduce(
            lambda k: text_parts[:, 2 * k * HD : 2 * (k + 1) * HD], owners
        )
        next(text_sum)
    else:
        parts = jnp.einsum(
            "rc,jchd->hrjd", caption_cols,
            text_weight.astype(bf16).reshape(2, cap_cols, heads, HD), preferred_element_type=f32,
        ).reshape(heads, text_rows, 2 * HD)
        after = seq_size - heads - first_owner
        parts = jnp.pad(parts.astype(bf16), ((first_owner, after), (0, 0), (0, 0)))
        text_kv = lax.psum_scatter(parts, "seq", scatter_dimension=0, tiled=False)

    ffn_shard = jnp.concatenate([turned(updown_weight), down_weight.astype(bf16).T], axis=1)
    ffn_chunks = ring.gather(once(ffn_shard, packed, *([text_parts] if ring.ring else [])))
    ffn_ins = [(chunk, anywhere()) for chunk in ffn_chunks]
    text_sent = text_sum.send(()) if ring.ring else ()
    modulation = once(modulation, *hop(attn_chunks, 3), *hop(ffn_chunks, 1), *text_sent)
    segment_col = segment_ids[:, None]
    steps = here // ROWS
    segment_row = segment_ids.reshape(steps, 1, ROWS)
    row_ins = [
        (segment_col, rows_block(ROWS, 1)),
        (segment_row, pl.BlockSpec((1, 1, ROWS), lambda i, *_: (i, 0, 0))),
    ]
    block = rows_block(ROWS, width)
    mod_shape, gain_shape = modulation.shape, gains_value.shape
    x_rel, g_rel, mod_rel, gain_rel, hidden_attn = call(
        functools.partial(enter_kernel, **which), "enter", steps, [scal],
        [
            (x_tokens, block), (out_grad, block), (modulation, whole(mod_shape)),
            (gains_value, whole(gain_shape)), row_ins[0],
        ],
        [
            ((here, width), bf16, block), ((here, width), bf16, block),
            (mod_shape, f32, whole(mod_shape)), (gain_shape, f32, whole(gain_shape)),
            ((here, width), bf16, block),
        ],
        moved=here * width * 10,
    )
    mod_ins = [(mod_rel, whole(mod_shape)), (gain_rel, whole(gain_shape))]
    full_ins = mod_ins + [(segment_col, whole((here, 1)))]
    slab_shape = (seq_size, here, 3 * HD)
    slabs = call(
        functools.partial(
            project_kernel, heads=heads, first_owner=first_owner, count=pieces
        ),
        "project", 1, [],
        [(hidden_attn, whole((here, width)))] + attn_ins,
        [(slab_shape, bf16, whole(slab_shape))],
        [pltpu.VMEM((width, qkv_width), bf16), piece_sems],
        moved=width * qkv_width * 2, flops=2 * here * width * qkv_width,
    )[0]
    qkv_head = exchange(slabs).reshape(count, 3 * HD)

    block_q = math.gcd(count, 512)
    block_k = math.gcd(count, 512)
    table = attention_table(segments, block_q, block_k)
    tanh_cross = jnp.tanh(cross_gates)
    my_gate = jnp.sum(jnp.where(jnp.arange(heads) == my_head, tanh_cross, 0.0)).reshape(1)
    blocks = count // block_q
    q_ins = [(qkv_head, rows_block(block_q, 3 * HD))]
    seg_row = (segments[None, :], lanes_block(1, block_q))
    seg_col = (segments[:, None], whole((count, 1)))
    turned_out = ((HD, count), f32, lanes_block(HD, block_q))
    stat_out = ((1, count), f32, lanes_block(1, block_q))
    area = count * count * HD
    self_out, stat = call(
        functools.partial(self_kernel, block_k=block_k), "attend", blocks, [table],
        q_ins + [(qkv_head, whole(qkv_head.shape)), seg_row, seg_col],
        [turned_out, stat_out],
        [pltpu.VMEM((count, HD), bf16), pltpu.VMEM((HD, count), bf16)],
        flops=4 * area, moved=count * HD * 20, exps=count * count,
    )
    self_out = once(self_out, *hop(ffn_chunks, 2))
    if ring.ring:
        for held in ((slabs,), (qkv_head,), ()):
            text_kv = text_sum.send(held)
        text_kv = text_kv.astype(bf16)
    mixed_head, text_out, text_stat = call(
        text_kernel, "attend_text", blocks, [table, my_gate],
        q_ins
        + [(text_kv, whole(text_kv.shape)), (self_out, lanes_block(HD, block_q)), seg_row],
        [((count, HD), bf16, rows_block(block_q, HD)), turned_out, stat_out],
        [pltpu.VMEM((text_rows, HD), bf16), pltpu.VMEM((HD, text_rows), bf16)],
        flops=4 * count * TEXT * HD, moved=count * HD * 20, exps=count * TEXT,
    )
    mixed_head = once(mixed_head, *hop(ffn_chunks, 3))
    mixed_slabs = exchange(mixed_head.reshape(seq_size, here, HD))
    mixed_slabs = once(mixed_slabs, *(ffn_chunks[4:6] if ring.ring else ()))
    low, high = qkv_width, qkv_width + local_width
    head_args = {"heads": heads, "first_owner": first_owner, "count": pieces}
    half_shape = (here // 2, width)
    half_out = (half_shape, bf16, whole(half_shape))
    slab64 = (seq_size, here, HD)
    held_out = [pltpu.VMEM((width, local_width), bf16)]
    full_sum = [pltpu.VMEM((here, width), bf16), piece_sems]
    mixed, *attn = call(
        functools.partial(out_kernel, low=low, high=high, **head_args), "out", 1, [scal],
        [(mixed_slabs, whole(slab64))] + attn_ins,
        [((here, local_width), bf16, whole((here, local_width))), half_out, half_out],
        held_out + full_sum,
        moved=width * local_width * 2, flops=2 * here * width * local_width,
    )
    attn = psum_tp(attn)

    def halves(pair, spec=None):
        return [(one, spec or whole(half_shape)) for one in pair]

    tokens = (here, width)
    x_mid, hidden_ffn, ffn_grad, inner, both_grads, hm, ho, fm, fo = call(
        functools.partial(ffn_kernel, count=pieces, units=units), "ffn", 1, [scal],
        [(x_rel, whole(tokens)), (g_rel, whole(tokens))] + halves(attn) + full_ins + ffn_ins,
        [
            (tokens, f32, whole(tokens)), (tokens, bf16, whole(tokens)),
            (tokens, bf16, whole(tokens)), ((here, units), bf16, whole((here, units))),
            ((here, 2 * units), bf16, whole((here, 2 * units))),
            half_out, half_out, half_out, half_out,
        ],
        [pltpu.VMEM((width, 3 * units), bf16), pltpu.VMEM(tokens, bf16)] + full_sum,
        moved=width * 3 * units * 2, flops=12 * here * width * units,
    )
    hgrad = psum_tp((hm, ho))
    ffn_out = psum_tp(lax.optimization_barrier((fm, fo, *hgrad))[:2])
    mid_grad, attn_grad, grad_slabs = call(
        functools.partial(mid_kernel, low=low, high=high, **head_args), "mid", 1, [scal],
        [(x_mid, whole(tokens)), (g_rel, whole(tokens))] + halves(hgrad) + full_ins + attn_ins,
        [(tokens, f32, whole(tokens)), (tokens, bf16, whole(tokens)), (slab64, bf16, whole(slab64))],
        held_out + full_sum,
        moved=width * local_width * 2, flops=2 * here * width * local_width,
    )
    head_grad = exchange(grad_slabs).reshape(count, HD)
    ffn_sum = ring.reduce_products([(hidden_ffn, both_grads), (ffn_grad, inner)])
    next(ffn_sum)
    ffn_sum.send((grad_slabs,))
    head_grad = once(head_grad, *ffn_sum.send((head_grad,)))
    half_block = pl.BlockSpec((ROWS, width), lambda i, *_: (i % (steps // 2), 0))
    sums_shape, one_gain = (4 * ITEMS, width), (8, width)

    g_ins = [(head_grad, rows_block(block_q, HD))]
    kv64 = pltpu.VMEM((text_rows, HD), bf16)
    text_dkv, text_dq, cross_rows = call(
        text_back_kernel, "attend_text_back", blocks, [table, my_gate],
        q_ins + g_ins
        + [
            (text_kv, whole(text_kv.shape)), (text_out, lanes_block(HD, block_q)),
            (text_stat, lanes_block(1, block_q)), seg_row,
        ],
        [((text_rows, 2 * HD), bf16, whole((text_rows, 2 * HD))), turned_out, stat_out],
        [kv64, kv64, pltpu.VMEM((HD, text_rows), bf16)] + [pltpu.VMEM((text_rows, HD), f32)] * 2,
        flops=10 * count * TEXT * HD, moved=count * HD * 20, exps=count * TEXT,
    )
    head64 = pltpu.VMEM((count, HD), bf16)
    dqkv = call(
        functools.partial(self_back_kernel, block_k=block_k), "attend_back", blocks, [table],
        q_ins + g_ins
        + [
            (qkv_head, whole(qkv_head.shape)), (self_out, lanes_block(HD, block_q)),
            (stat, lanes_block(1, block_q)), (text_dq, lanes_block(HD, block_q)), seg_row, seg_col,
        ],
        [(qkv_head.shape, bf16, whole(qkv_head.shape))],
        [head64, head64, pltpu.VMEM((HD, count), bf16)] + [pltpu.VMEM((count, HD), f32)] * 2,
        flops=10 * area, moved=count * HD * 20, exps=count * count,
    )[0]

    back_slabs = exchange(dqkv.reshape(slab_shape))
    qkv_grads, *hidden_grad = call(
        functools.partial(qkv_back_kernel, **head_args), "qkv_back", 1, [scal],
        [(back_slabs, whole(slab_shape))] + attn_ins,
        [((here, qkv_width), bf16, whole((here, qkv_width))), half_out, half_out],
        [pltpu.VMEM((width, qkv_width), bf16)] + full_sum,
        moved=width * qkv_width * 2, flops=2 * here * width * qkv_width,
    )
    text_grads = ring.gather(text_dkv)
    if ring.ring:
        slab_at = jnp.argmax(
            slab_owner[None, :] == jnp.arange(first_owner, first_owner + heads)[:, None], axis=1
        ).astype(jnp.int32)
        text_owned = call(
            text_grad_kernel, "text_grad", 1, [slab_at],
            [(caption_cols.T, whole((cap_cols, text_rows)))]
            + [(one, anywhere()) for one in text_grads],
            [(text_weight.shape, f32, whole(text_weight.shape))],
            [
                pltpu.VMEM((seq_size * text_rows, 2 * HD), bf16),
                pltpu.SemaphoreType.DMA((len(text_grads),)),
            ],
            flops=4 * text_rows * cap_cols * local_width, moved=text_rows * cap_cols * 4,
        )[0]
    else:
        text_grads = text_grads[0].reshape(seq_size, text_rows, 2, HD)
        text_owned = jnp.einsum(
            "rc,hrjd->jchd", caption_cols, text_grads[first_owner : first_owner + heads],
            preferred_element_type=f32,
        ).reshape(text_weight.shape)

    attn_sum = ring.reduce_products([(hidden_attn, qkv_grads), (attn_grad, mixed)])
    next(attn_sum)
    ffn_sent = ffn_sum.send((dqkv,))
    updown_rows, down_owned = ffn_sum.send(())
    side_mid = once(x_mid, *ffn_sent)
    block_out, early_sums, early_gain = call(
        functools.partial(side_kernel, **which), "side", steps, [scal],
        [(side_mid, block), (mid_grad, block), (g_rel, block)]
        + halves(attn, half_block) + halves(ffn_out, half_block) + halves(hgrad, half_block)
        + mod_ins + row_ins,
        [(tokens, f32, block), (sums_shape, f32, whole(sums_shape)), (one_gain, f32, whole(one_gain))],
        moved=here * width * 24,
    )
    for _ in range(4):
        attn_grads = attn_sum.send(())
    qkv_rows, out_owned = attn_grads
    hidden_grad = psum_tp(hidden_grad)
    all_sums = (6 * ITEMS, quarter)
    input_grad, item_sums, gain_sums = call(
        functools.partial(leave_kernel, **which), "leave", steps, [scal],
        [(x_rel, block), (mid_grad, block)] + halves(hidden_grad, half_block) + mod_ins + row_ins
        + [(early_sums, whole(sums_shape)), (early_gain, whole(one_gain))],
        [(tokens, f32, block), (all_sums, f32, whole(all_sums)), (one_gain, f32, whole(one_gain))],
        [pltpu.VMEM((6 * ITEMS + 8, width), f32)] * 2,
        moved=here * width * 16,
    )

    cross_here = jnp.where(
        is_owner & (jnp.arange(quarter) == my_head), jnp.sum(cross_rows), 0.0
    )
    packed = jnp.concatenate(
        [
            item_sums, gain_sums[:2].reshape(-1, quarter), cross_here[None],
            jnp.zeros((-(2 * tp_size + 1) % 8, quarter), f32),
        ]
    )
    packed = butterfly(packed, "seq", seq_size)
    item_mod_low = packed[: 6 * ITEMS].astype(bf16)
    gain_grads = packed[6 * ITEMS : 6 * ITEMS + 2 * tp_size].reshape(2, seq_size, gain_cols)
    gains_owned = jnp.sum(jnp.where(is_here[None, :, None], gain_grads, 0.0), axis=1)
    cross_total = packed[6 * ITEMS + 2 * tp_size, :heads] * (1.0 - tanh_cross * tanh_cross)

    def by_block(sums):
        return jnp.transpose(sums.reshape(6, ITEMS, -1), (1, 0, 2)).reshape(ITEMS, -1)

    mod_weight_grad = dot(embed_rows, by_block(gather_tp(item_mod_low, 1)), ((0,), (0,)))
    mod_quarter_grad = dot(embed_rows, by_block(item_mod_low), ((0,), (0,)))

    owned_square = (
        square_sum(qkv_rows)
        + square_sum(out_owned)
        + square_sum(text_owned)
        + square_sum(updown_rows)
        + square_sum(down_owned)
        + square_sum(mod_quarter_grad)
    )
    owned_square = owned_square + jnp.where(tp_index == 0, square_sum(gains_owned), 0.0)
    owned_square = owned_square + jnp.where(seq_index == 0, square_sum(cross_total), 0.0)
    total_square = jnp.full((8, 128), owned_square)
    total_square = butterfly(butterfly(total_square, "tp", tp_size), "seq", seq_size)[0, 0]
    grad_norm = jnp.sqrt(total_square)
    clip = jnp.minimum(1.0, clip_limit / (grad_norm + 1e-06))

    def unturned(rows, blocks):
        return jnp.transpose(rows.reshape(rows.shape[0], blocks, -1), (1, 0, 2))

    matrix = functools.partial(adam_update, clip=clip, rate=rate_matrix, decay=decay_matrix)
    small = functools.partial(adam_update, clip=clip, rate=rate_small, decay=0.0)
    return (
        block_out,
        input_grad,
        grad_norm,
        *matrix(mod_weight, mod_first, mod_second, mod_weight_grad),
        *small(norm_gains, gains_first, gains_second, gains_owned),
        *matrix(qkv_weight, qkv_first, qkv_second, unturned(qkv_rows, 3)),
        *matrix(out_weight, out_first, out_second, out_owned.T),
        *matrix(text_weight, text_first, text_second, text_owned),
        *small(cross_gates, cross_first, cross_second, cross_total),
        *matrix(updown_weight, updown_first, updown_second, unturned(updown_rows, 2)),
        *matrix(down_weight, down_first, down_second, down_owned.T),
    )


def solution(mesh):
    rows = P("seq", None)
    cols = P(None, "seq")
    split = P(None, "seq", "tp")
    turned = P("tp", "seq")
    heads = P("tp")
    weights = (rows,) * 3 + (cols,) * 3 + (split,) * 3 + (turned,) * 3 + (split,) * 3
    weights = weights + (heads,) * 3 + (split,) * 3 + (turned,) * 3
    return jax.shard_map(
        functools.partial(per_device, seq_size=mesh.shape["seq"], tp_size=mesh.shape["tp"]),
        mesh=mesh,
        in_specs=(rows, rows, P(), P("seq"), rows) + weights,
        out_specs=(rows, rows, P()) + weights,
        check_vma=False,
    )
```

```python
import functools
import math

import jax
import jax.numpy as jnp
from jax import lax
from jax.experimental import pallas as pl
from jax.experimental.pallas import tpu as pltpu
from jax.sharding import PartitionSpec as P

HD = 64
TE = 1024
TEXT = 256
ITEMS = 8
ADAM_STEP = 10

bf16 = jnp.bfloat16
f32 = jnp.float32
highest = lax.Precision.HIGHEST
eps_norm = 1e-06
masked_score = -1e30
lowest_max = -1e20
clip_limit = 1.0
beta_first = 0.9
beta_second = 0.95
adam_eps = 1e-08
rate_matrix = 0.05
rate_small = 0.5
decay_matrix = 0.1
score_scale = HD ** (-0.5)

WIDE = 256
ROWS = 128

CORE_SWAP = [(0, 1), (1, 0), (2, 3), (3, 2)]
Y_SWAP = [(0, 2), (2, 0), (1, 3), (3, 1)]
CYCLE = (0, 2, 4, 6, 7, 5, 3, 1)


def time_embed(timesteps):
    half_width = TE // 2
    frequency = jnp.exp(-math.log(10000.0) * jnp.arange(half_width, dtype=f32) / half_width)
    angles = 1000.0 * timesteps[:, None] * frequency[None, :]
    return jnp.concatenate([jnp.cos(angles), jnp.sin(angles)], axis=1)


def rms_parts(values):
    inverse = lax.rsqrt(jnp.mean(values * values, axis=-1, keepdims=True) + eps_norm)
    return (values * inverse, inverse)


def rms_back(normed, inverse, normed_grad):
    return inverse * (normed_grad - normed * jnp.mean(normed_grad * normed, axis=-1, keepdims=True))


def adam_update(weight, first, second, grad, clip, rate, decay):
    clipped = grad * clip
    first_new = beta_first * first + (1.0 - beta_first) * clipped
    second_new = beta_second * second + (1.0 - beta_second) * clipped * clipped
    first_hat = first_new / (1.0 - beta_first**ADAM_STEP)
    second_hat = second_new / (1.0 - beta_second**ADAM_STEP)
    weight_new = weight - rate * (first_hat / (jnp.sqrt(second_hat) + adam_eps) + decay * weight)
    return (weight_new, first_new, second_new)


def square_sum(values):
    return jnp.sum(values * values)


def dot(a, b, dims):
    return lax.dot_general(a, b, (dims, ((), ())), preferred_element_type=f32)


class Ring:
    def __init__(self, size):
        self.size = size
        self.ring = size == len(CYCLE)

    def hop(self, value, step, sends=None):
        n = self.size
        pairs = [(CYCLE[p], CYCLE[(p + step) % n]) for p in range(n) if sends is None or sends(p)]
        return lax.ppermute(value, "seq", pairs)

    def gather(self, own, held=((), (), ())):
        if not self.ring:
            return [lax.all_gather(own, "seq", axis=0, tiled=True)]
        half = own.shape[0] // 2
        ahead, behind = [own], [own]
        for i in range(3):
            ahead.append(self.hop(ahead[-1], 1))
            behind.append(self.hop(behind[-1], -1))
            if held[i]:
                ahead[-1], behind[-1] = lax.optimization_barrier(
                    (ahead[-1], behind[-1], *held[i])
                )[:2]
        far = [self.hop(behind[-1][:half], -1), self.hop(ahead[-1][half:], 1)]
        return behind + far + ahead[:0:-1]

    def reduce(self, block, active=None):
        rows = block(0).shape[0]
        half = rows // 2

        def sends(k):
            if active is None:
                return None
            return lambda p: CYCLE[(p + k) % self.size] in active

        def wait(held, *values):
            return lax.optimization_barrier((*values, *held))[: len(values)] if held else values

        def plus(part, moved):
            return (part.astype(f32) + moved.astype(f32)).astype(bf16)

        ahead, behind = block(4)[:half], block(4)[half:]
        for k in (3, 2, 1, 0):
            sent = (ahead, behind)
            ahead = self.hop(ahead, 1, sends(k + 1))
            behind = self.hop(behind, -1, sends(-k - 1))
            ahead, behind = wait((yield sent), ahead, behind)
            if k == 3:
                near, far = block(3), block(5)
                ahead = jnp.concatenate([plus(near[:half], ahead), near[half:]])
                behind = jnp.concatenate([far[:half], plus(far[half:], behind)])
            elif k:
                ahead, behind = plus(block(k), ahead), plus(block(8 - k), behind)
        yield block(0).astype(f32) + ahead.astype(f32) + behind.astype(f32)

    def reduce_products(self, pairs):
        parts = [dot(left, right, ((0,), (0,))).astype(bf16) for left, right in pairs]
        widths = [part.shape[1] for part in parts]
        edges = [sum(widths[:i]) for i in range(len(widths) + 1)]
        slab = parts[0].shape[0] // self.size

        def split(rows):
            return [rows[:, low:high] for low, high in zip(edges, edges[1:])]

        if not self.ring:
            for _ in range(4):
                yield ()
            rows = jnp.concatenate(parts, 1)
            rows = lax.psum_scatter(rows, "seq", scatter_dimension=0, tiled=True)
            yield split(rows.astype(f32))
            return

        ring = self.reduce(
            lambda k: jnp.concatenate([part[k * slab : (k + 1) * slab] for part in parts], axis=1)
        )
        held = yield next(ring)
        for _ in range(3):
            held = yield ring.send(held)
        yield split(ring.send(held))


def once(value, *others):
    return lax.optimization_barrier((value, *others))[0]


def butterfly(value, axis, size):
    step = 1
    while step < size:
        value = value + lax.ppermute(value, axis, [(i, i ^ step) for i in range(size)])
        step *= 2
    return value


def gather_tp(value, axis):
    tp = lax.axis_index("tp")

    def join(second, mine, other):
        low = jnp.where(second, other, mine)
        high = jnp.where(second, mine, other)
        return jnp.concatenate([low, high], axis)

    pair = join(tp % 2 == 1, value, lax.ppermute(value, "tp", CORE_SWAP))
    return join(tp >= 2, pair, lax.ppermute(pair, "tp", Y_SWAP))


def psum_tp(halves, held=()):
    mine, other = halves
    mine = (mine.astype(f32) + lax.ppermute(other, "tp", CORE_SWAP).astype(f32)).astype(bf16)
    mine = once(mine, *held)
    mine = (mine.astype(f32) + lax.ppermute(mine, "tp", Y_SWAP).astype(f32)).astype(bf16)
    return (mine, lax.ppermute(mine, "tp", CORE_SWAP))


def thirds(value):
    high = value.astype(bf16).astype(f32)
    rest = value - high
    middle = rest.astype(bf16).astype(f32)
    return jnp.concatenate([high, middle, rest - middle], axis=0).astype(bf16)


def item_sum(by_item, value):
    return dot(jnp.concatenate([by_item] * 3, axis=1).astype(bf16), thirds(value), ((1,), (0,)))


def anywhere():
    return pl.BlockSpec(memory_space=pl.ANY)


def whole(shape):
    return pl.BlockSpec(
        shape, lambda i, *_: (0,) * len(shape), pipeline_mode=pl.Buffered(1)
    )


def rows_block(block, width):
    return pl.BlockSpec((block, width), lambda i, *_: (i, 0))


def lanes_block(rows, block):
    return pl.BlockSpec((rows, block), lambda i, *_: (0, i))


def shape_of(shape, dtype):
    return jax.ShapeDtypeStruct(shape, dtype)


def call(kernel, name, grid, scalars, ins, outs, scratch=(), flops=0, moved=0, exps=0):
    return pl.pallas_call(
        kernel,
        out_shape=tuple(shape_of(shape, dtype) for shape, dtype, _ in outs),
        grid_spec=pltpu.PrefetchScalarGridSpec(
            num_scalar_prefetch=len(scalars),
            grid=(grid,),
            in_specs=[spec for _, spec in ins],
            out_specs=tuple(spec for _, _, spec in outs),
            scratch_shapes=list(scratch),
        ),
        cost_estimate=pl.CostEstimate(flops=flops, bytes_accessed=moved, transcendentals=exps),
        name=name,
    )(*scalars, *[array for array, _ in ins])


def starts_of(chunks):
    at = 0
    for chunk in chunks:
        yield at
        at += chunk.shape[0]


def chunk_copies(chunks, low, high, held, sems):
    return [
        pltpu.make_async_copy(
            chunk.at[:, low:high], held.at[start : start + chunk.shape[0], :], sems.at[j]
        )
        for j, (chunk, start) in enumerate(zip(chunks, starts_of(chunks)))
    ]


def relative_store(ring_size, ring, place, out_ref, value):
    slab = value.shape[1] // ring_size
    if not ring:
        out_ref[...] = value
        return
    for p in range(ring_size):

        @pl.when(place == p)
        def _(p=p):
            for k in range(ring_size):
                s = CYCLE[(p + k) % ring_size]
                out_ref[:, k * slab : (k + 1) * slab] = value[:, s * slab : (s + 1) * slab]


def absolute_store(ring_size, ring, place, out_ref, value):
    slab = value.shape[1] // ring_size
    if not ring:
        out_ref[...] = value
        return
    for p in range(ring_size):

        @pl.when(place == p)
        def _(p=p):
            for k in range(ring_size):
                s = CYCLE[(p + k) % ring_size]
                out_ref[:, s * slab : (s + 1) * slab] = value[:, k * slab : (k + 1) * slab]


def onehot_rows(segment_col):
    items = lax.broadcasted_iota(jnp.int32, (segment_col.shape[0], 3 * ITEMS), 1) % ITEMS
    return (segment_col == items).astype(f32).astype(bf16)


def onehot_cols(segment_row):
    items = lax.broadcasted_iota(jnp.int32, (ITEMS, segment_row.shape[1]), 0)
    return (segment_row == items).astype(f32)


def modulate(onehot, mod_ref, block):
    return dot(onehot, thirds(mod_ref[block * ITEMS : (block + 1) * ITEMS, :]), ((1,), (0,)))


def enter_kernel(scal, x_ref, g_ref, mod_ref, gain_ref, sc_ref,
                 xr_ref, gr_ref, modr_ref, gainr_ref, hidden_ref, *, size, ring):
    place = scal[0]

    @pl.when(pl.program_id(0) == 0)
    def _():
        relative_store(size, ring, place, modr_ref, mod_ref[...])
        relative_store(size, ring, place, gainr_ref, gain_ref[...])

    relative_store(size, ring, place, xr_ref, x_ref[...])
    relative_store(size, ring, place, gr_ref, g_ref[...])
    x = xr_ref[...].astype(f32)
    normed, _ = rms_parts(x)
    onehot = onehot_rows(sc_ref[...])
    scale = modulate(onehot, modr_ref, 1)
    shift = modulate(onehot, modr_ref, 0)
    hidden_ref[...] = (normed * gainr_ref[0:1, :] * (1.0 + scale) + shift).astype(bf16)


def project_kernel(hidden_ref, *refs, heads, first_owner, count):
    chunks, (slab_ref, held, sems) = refs[:count], refs[count:]
    width = heads * HD
    copies = chunk_copies(chunks, 0, 3 * width, held, sems)
    for one in copies:
        one.start()
    for s in range(slab_ref.shape[0]):
        if not first_owner <= s < first_owner + heads:
            slab_ref[s] = jnp.zeros(slab_ref.shape[1:], bf16)
    for one in copies:
        one.wait()
    hidden = hidden_ref[...]
    for j in range(3):
        part = dot(hidden, held[:, j * width : (j + 1) * width], ((1,), (0,))).astype(bf16)
        if j == 0:
            part = part * jnp.asarray(score_scale, bf16)
        for h in range(heads):
            slab_ref[first_owner + h, :, j * HD : (j + 1) * HD] = part[:, h * HD : (h + 1) * HD]


def split_halves(core, full_ref, mine_ref, other_ref):
    half = mine_ref.shape[0]
    mine_ref[...] = full_ref[pl.ds(pl.multiple_of(core * half, half), half), :]
    other_ref[...] = full_ref[pl.ds(pl.multiple_of((1 - core) * half, half), half), :]


def join_halves(core, mine_ref, other_ref, full_ref):
    half = mine_ref.shape[0]
    full_ref[pl.ds(pl.multiple_of(core * half, half), half), :] = mine_ref[...]
    full_ref[pl.ds(pl.multiple_of((1 - core) * half, half), half), :] = other_ref[...]


def times_turned(value_ref, held, full_ref):
    tiles = held.shape[0] // WIDE

    def one(i, _):
        at = pl.ds(pl.multiple_of(i * WIDE, WIDE), WIDE)
        full_ref[:, at] = dot(value_ref[...], held[at, :], ((1,), (1,))).astype(bf16)
        return 0

    lax.fori_loop(0, tiles, one, 0, unroll=True)


def out_kernel(scal, slab_ref, *refs, heads, first_owner, count, low, high):
    chunks, (mixed_ref, mine_ref, other_ref, held, full, sems) = refs[:count], refs[count:]
    copies = chunk_copies(chunks, low, high, held, sems)
    for one in copies:
        one.start()
    for h in range(heads):
        mixed_ref[:, h * HD : (h + 1) * HD] = slab_ref[first_owner + h]
    for one in copies:
        one.wait()
    times_turned(mixed_ref, held, full)
    split_halves(scal[1], full, mine_ref, other_ref)


def qkv_back_kernel(scal, slab_ref, *refs, heads, first_owner, count):
    chunks, (grads_ref, mine_ref, other_ref, held, full, sems) = refs[:count], refs[count:]
    width = heads * HD
    copies = chunk_copies(chunks, 0, 3 * width, held, sems)
    for one in copies:
        one.start()
    for j in range(3):
        for h in range(heads):
            at = j * width + h * HD
            grads_ref[:, at : at + HD] = slab_ref[first_owner + h, :, j * HD : (j + 1) * HD]
    for one in copies:
        one.wait()
    times_turned(grads_ref, held, full)
    split_halves(scal[1], full, mine_ref, other_ref)


def ffn_kernel(scal, x_ref, g_ref, am_ref, ao_ref, modr_ref, gainr_ref, sc_ref, *refs,
               count, units):
    chunks = refs[:count]
    (mid_ref, hidden_ref, fgrad_ref, inner_ref, both_ref, hm_ref, ho_ref, fm_ref, fo_ref,
     held, attn, full, sems) = refs[count:]
    core = scal[1]
    copies = chunk_copies(chunks, 0, held.shape[1], held, sems)
    for one in copies:
        one.start()
    join_halves(core, am_ref, ao_ref, attn)

    def prepare(i, _):
        at = pl.ds(pl.multiple_of(i * ROWS, ROWS), ROWS)
        onehot = onehot_rows(sc_ref[at, :])
        x_mid = x_ref[at, :].astype(f32) + jnp.tanh(modulate(onehot, modr_ref, 2)) * attn[
            at, :
        ].astype(f32)
        mid_ref[at, :] = x_mid
        normed, _ = rms_parts(x_mid)
        scale = modulate(onehot, modr_ref, 4)
        shift = modulate(onehot, modr_ref, 3)
        hidden_ref[at, :] = (normed * gainr_ref[1:2, :] * (1.0 + scale) + shift).astype(bf16)
        tanh_ffn = jnp.tanh(modulate(onehot, modr_ref, 5))
        fgrad_ref[at, :] = (g_ref[at, :].astype(f32) * tanh_ffn).astype(bf16)
        return 0

    lax.fori_loop(0, x_ref.shape[0] // ROWS, prepare, 0)
    for one in copies:
        one.wait()

    def tile(i, _):
        def at(base):
            return pl.ds(pl.multiple_of(base + i * WIDE, WIDE), WIDE)

        gate_pre = dot(hidden_ref[...], held[:, at(0)], ((1,), (0,)))
        up_pre = dot(hidden_ref[...], held[:, at(units)], ((1,), (0,)))
        inner_grad = dot(fgrad_ref[...], held[:, at(2 * units)], ((1,), (0,)))
        sigmoid = jax.nn.sigmoid(gate_pre)
        silu = gate_pre * sigmoid
        inner_ref[:, at(0)] = (silu * up_pre).astype(bf16)
        both_ref[:, at(0)] = (
            inner_grad * up_pre * sigmoid * (1.0 + gate_pre * (1.0 - sigmoid))
        ).astype(bf16)
        both_ref[:, at(units)] = (inner_grad * silu).astype(bf16)
        return 0

    lax.fori_loop(0, units // WIDE, tile, 0, unroll=True)
    times_turned(both_ref, held.at[:, 0 : 2 * units], full)
    split_halves(core, full, hm_ref, ho_ref)
    times_turned(inner_ref, held.at[:, 2 * units : 3 * units], full)
    split_halves(core, full, fm_ref, fo_ref)


def mid_kernel(scal, mid_ref, g_ref, hm_ref, ho_ref, modr_ref, gainr_ref, sc_ref, *refs,
               heads, first_owner, count, low, high):
    chunks = refs[:count]
    grad_ref, agrad_ref, slab_ref, held, hgrad, sems = refs[count:]
    copies = chunk_copies(chunks, low, high, held, sems)
    for one in copies:
        one.start()
    join_halves(scal[1], hm_ref, ho_ref, hgrad)
    for s in range(slab_ref.shape[0]):
        if not first_owner <= s < first_owner + heads:
            slab_ref[s] = jnp.zeros(slab_ref.shape[1:], bf16)

    def prepare(i, _):
        at = pl.ds(pl.multiple_of(i * ROWS, ROWS), ROWS)
        onehot = onehot_rows(sc_ref[at, :])
        normed, inverse = rms_parts(mid_ref[at, :])
        scale = modulate(onehot, modr_ref, 4)
        normed_grad = hgrad[at, :].astype(f32) * gainr_ref[1:2, :] * (1.0 + scale)
        grad = g_ref[at, :].astype(f32) + rms_back(normed, inverse, normed_grad)
        grad_ref[at, :] = grad
        agrad_ref[at, :] = (grad * jnp.tanh(modulate(onehot, modr_ref, 2))).astype(bf16)
        return 0

    lax.fori_loop(0, mid_ref.shape[0] // ROWS, prepare, 0)
    for one in copies:
        one.wait()
    mixed = dot(agrad_ref[...], held[...], ((1,), (0,))).astype(bf16)
    for h in range(heads):
        slab_ref[first_owner + h] = mixed[:, h * HD : (h + 1) * HD]


def own_rows(core, mine_ref, other_ref):
    first = pl.program_id(0) < pl.num_programs(0) // 2
    mine = jnp.logical_xor(first, core == 1)
    return jnp.where(mine, mine_ref[...].astype(f32), other_ref[...].astype(f32))


def side_kernel(scal, mid_ref, grad_ref, g_ref, am_ref, ao_ref, fm_ref, fo_ref, hm_ref, ho_ref,
                modr_ref, gainr_ref, sc_ref, sr_ref,
                block_ref, sums_ref, gain_ref, *, size, ring):
    place, core = scal[0], scal[1]

    @pl.when(pl.program_id(0) == 0)
    def _():
        sums_ref[...] = jnp.zeros_like(sums_ref)
        gain_ref[...] = jnp.zeros_like(gain_ref)

    attn = own_rows(core, am_ref, ao_ref)
    ffn_out = own_rows(core, fm_ref, fo_ref)
    hgrad = own_rows(core, hm_ref, ho_ref)
    onehot = onehot_rows(sc_ref[...])
    by_item = onehot_cols(sr_ref[0])
    tanh_attn = jnp.tanh(modulate(onehot, modr_ref, 2))
    tanh_ffn = jnp.tanh(modulate(onehot, modr_ref, 5))
    scale = modulate(onehot, modr_ref, 4)
    x_mid = mid_ref[...]
    absolute_store(size, ring, place, block_ref, x_mid + tanh_ffn * ffn_out)
    normed, _ = rms_parts(x_mid)

    def add(block, value):
        sums_ref[block * ITEMS : (block + 1) * ITEMS, :] += item_sum(by_item, value)

    add(0, grad_ref[...] * attn * (1.0 - tanh_attn * tanh_attn))
    add(1, hgrad)
    add(2, hgrad * normed * gainr_ref[1:2, :])
    add(3, g_ref[...].astype(f32) * ffn_out * (1.0 - tanh_ffn * tanh_ffn))
    gain_ref[0:1, :] += jnp.sum(hgrad * normed * (1.0 + scale), axis=0, keepdims=True)


def leave_kernel(scal, x_ref, grad_ref, hm_ref, ho_ref, modr_ref, gainr_ref, sc_ref, sr_ref,
                 early_ref, egain_ref, input_ref, sums_ref, gain_ref, total, turned, *, size, ring):
    place, core = scal[0], scal[1]

    @pl.when(pl.program_id(0) == 0)
    def _():
        total[...] = jnp.zeros_like(total)
        total[2 * ITEMS : 6 * ITEMS, :] = early_ref[...]
        total[6 * ITEMS + 1 : 6 * ITEMS + 2, :] = egain_ref[0:1, :]

    hgrad = own_rows(core, hm_ref, ho_ref)
    onehot = onehot_rows(sc_ref[...])
    by_item = onehot_cols(sr_ref[0])
    scale = modulate(onehot, modr_ref, 1)
    normed, inverse = rms_parts(x_ref[...].astype(f32))
    normed_grad = hgrad * gainr_ref[0:1, :] * (1.0 + scale)
    absolute_store(
        size, ring, place, input_ref, grad_ref[...] + rms_back(normed, inverse, normed_grad)
    )
    total[0:ITEMS, :] += item_sum(by_item, hgrad)
    total[ITEMS : 2 * ITEMS, :] += item_sum(by_item, hgrad * normed * gainr_ref[0:1, :])
    total[6 * ITEMS : 6 * ITEMS + 1, :] += jnp.sum(
        hgrad * normed * (1.0 + scale), axis=0, keepdims=True
    )

    @pl.when(pl.program_id(0) == pl.num_programs(0) - 1)
    def _():
        absolute_store(size, ring, place, turned, total[...])
        quarter = sums_ref.shape[1]
        at = pl.ds(pl.multiple_of(scal[2] * quarter, quarter), quarter)
        sums_ref[...] = turned[0 : 6 * ITEMS, at]
        gain_ref[...] = turned[6 * ITEMS : 6 * ITEMS + 8, :]


def text_heads_kernel(head_of, w_ref, out_ref, by_head):
    for h in range(by_head.shape[0]):
        for j in range(2):
            by_head[h, :, j * HD : (j + 1) * HD] = w_ref[j, :, h * HD : (h + 1) * HD].astype(bf16)
    for k in range(out_ref.shape[1] // (2 * HD)):
        out_ref[:, 2 * k * HD : 2 * (k + 1) * HD] = by_head[head_of[k]]


def text_grad_kernel(slab_at, cap_ref, *refs):
    chunks, (out_ref, held, sems) = refs[:-3], refs[-3:]
    copies = chunk_copies(chunks, 0, 2 * HD, held, sems)
    for one in copies:
        one.start()
    for one in copies:
        one.wait()
    rows = cap_ref.shape[1]
    for h in range(out_ref.shape[2] // HD):
        at = pl.ds(pl.multiple_of(slab_at[h] * rows, rows), rows)
        part = dot(cap_ref[...], held[at, :], ((1,), (0,)))
        out_ref[0, :, h * HD : (h + 1) * HD] = part[:, :HD]
        out_ref[1, :, h * HD : (h + 1) * HD] = part[:, HD:]


def mod_kernel(scal, embed_ref, w_ref, out_ref):
    out_ref[...] = dot(embed_ref[...], w_ref[...].astype(bf16), ((1,), (0,)))


def turned_copy(source_ref, low, out_ref, block):
    def one(j, _):
        at = pl.ds(pl.multiple_of(j * block, block), block)
        out_ref[:, at] = jnp.transpose(source_ref[at, low : low + HD].astype(f32)).astype(bf16)
        return 0

    lax.fori_loop(0, source_ref.shape[0] // block, one, 0, unroll=source_ref.shape[0] <= 2048)


def self_kernel(table, q_ref, all_ref, sq_ref, sk_ref, out_ref, stat_ref, k_ref, vt_ref, *, block_k):
    i = pl.program_id(0)

    @pl.when(i == 0)
    def _():
        k_ref[...] = all_ref[:, HD : 2 * HD]
        turned_copy(all_ref, 2 * HD, vt_ref, block_k)

    q = q_ref[:, :HD]
    item_of_q = sq_ref[...]
    width = q.shape[0]

    def step(j, carry):
        top, total, out = carry
        at = pl.ds(pl.multiple_of(j * block_k, block_k), block_k)
        scores = dot(k_ref[at, :], q, ((1,), (1,)))
        scores = jnp.where(sk_ref[at, :] == item_of_q, scores, masked_score)
        new_top = jnp.maximum(top, jnp.max(scores, axis=0, keepdims=True))
        weights = jnp.exp(scores - new_top)
        shrink = jnp.exp(top - new_top)
        total = total * shrink + jnp.sum(weights, axis=0, keepdims=True)
        out = out * shrink + dot(vt_ref[:, at], weights.astype(bf16), ((1,), (0,)))
        return (new_top, total, out)

    start = (
        jnp.full((1, width), lowest_max, f32),
        jnp.zeros((1, width), f32),
        jnp.zeros((HD, width), f32),
    )
    top, total, out = lax.fori_loop(table[0, i], table[1, i], step, start)
    out_ref[...] = out / total
    stat_ref[...] = top + jnp.log(total)


def text_kernel(table, gate, q_ref, kv_ref, self_ref, sq_ref,
                mixed_ref, out_ref, stat_ref, k_ref, vt_ref):
    i = pl.program_id(0)

    @pl.when(i == 0)
    def _():
        k_ref[...] = kv_ref[:, :HD]
        turned_copy(kv_ref, HD, vt_ref, TEXT)

    q = q_ref[:, :HD]
    item_of_q = sq_ref[...]

    def step(item, carry):
        out, stat = carry
        at = pl.ds(pl.multiple_of(item * TEXT, TEXT), TEXT)
        scores = dot(k_ref[at, :], q, ((1,), (1,)))
        top = jnp.max(scores, axis=0, keepdims=True)
        weights = jnp.exp(scores - top)
        total = jnp.sum(weights, axis=0, keepdims=True)
        probs = (weights / total).astype(bf16)
        part = dot(vt_ref[:, at], probs, ((1,), (0,)))
        here = item_of_q == item
        return (jnp.where(here, part, out), jnp.where(here, top + jnp.log(total), stat))

    start = (jnp.zeros((HD, q.shape[0]), f32), jnp.zeros((1, q.shape[0]), f32))
    text_out, stat = lax.fori_loop(table[2, i], table[3, i], step, start)
    out_ref[...] = text_out
    stat_ref[...] = stat
    mixed_ref[...] = jnp.transpose(self_ref[...] + gate[0] * text_out).astype(bf16)


def text_back_kernel(table, gate, q_ref, g_ref, kv_ref, text_ref, stat_ref, sq_ref,
                     dkv_ref, dq_ref, cross_ref, k_ref, v_ref, kt_ref, dk_sum, dv_sum):
    i = pl.program_id(0)

    @pl.when(i == 0)
    def _():
        k_ref[...] = kv_ref[:, :HD]
        v_ref[...] = kv_ref[:, HD:]
        turned_copy(kv_ref, 0, kt_ref, TEXT)
        dk_sum[...] = jnp.zeros_like(dk_sum)
        dv_sum[...] = jnp.zeros_like(dv_sum)

    q = q_ref[:, :HD]
    item_of_q = sq_ref[...]
    g_value = g_ref[...].astype(f32)
    g = (g_value * gate[0]).astype(bf16)
    text_out = text_ref[...]
    cross_ref[...] = jnp.sum(jnp.transpose(g_value) * text_out, axis=0, keepdims=True)
    delta = jnp.sum(jnp.transpose(g.astype(f32)) * text_out, axis=0, keepdims=True)
    stat = stat_ref[...]

    def step(item, total):
        at = pl.ds(pl.multiple_of(item * TEXT, TEXT), TEXT)
        scores = dot(k_ref[at, :], q, ((1,), (1,)))
        probs = jnp.exp(jnp.where(item_of_q == item, scores - stat, masked_score))
        prob_grad = dot(v_ref[at, :], g, ((1,), (1,)))
        score_grad = (probs * (prob_grad - delta)).astype(bf16)
        dk_sum[at, :] += dot(score_grad, q, ((1,), (0,)))
        dv_sum[at, :] += dot(probs.astype(bf16), g, ((1,), (0,)))
        return total + dot(kt_ref[:, at], score_grad, ((1,), (0,)))

    start = jnp.zeros((HD, q.shape[0]), f32)
    dq_ref[...] = lax.fori_loop(table[2, i], table[3, i], step, start)

    @pl.when(i == pl.num_programs(0) - 1)
    def _():
        dkv_ref[:, :HD] = dk_sum[...].astype(bf16)
        dkv_ref[:, HD:] = dv_sum[...].astype(bf16)


def self_back_kernel(table, q_ref, g_ref, all_ref, self_ref, stat_ref, start_ref, sq_ref, sk_ref,
                     dqkv_ref, k_ref, v_ref, kt_ref, dk_sum, dv_sum, *, block_k):
    i = pl.program_id(0)

    @pl.when(i == 0)
    def _():
        k_ref[...] = all_ref[:, HD : 2 * HD]
        v_ref[...] = all_ref[:, 2 * HD :]
        turned_copy(all_ref, HD, kt_ref, block_k)
        dk_sum[...] = jnp.zeros_like(dk_sum)
        dv_sum[...] = jnp.zeros_like(dv_sum)

    q = q_ref[:, :HD]
    g = g_ref[...]
    item_of_q = sq_ref[...]
    delta = jnp.sum(jnp.transpose(g.astype(f32)) * self_ref[...], axis=0, keepdims=True)
    stat = stat_ref[...]

    def step(j, total):
        at = pl.ds(pl.multiple_of(j * block_k, block_k), block_k)
        scores = dot(k_ref[at, :], q, ((1,), (1,)))
        allowed = sk_ref[at, :] == item_of_q
        probs = jnp.exp(jnp.where(allowed, scores - stat, masked_score))
        prob_grad = dot(v_ref[at, :], g, ((1,), (1,)))
        score_grad = (probs * (prob_grad - delta)).astype(bf16)
        dk_sum[at, :] += dot(score_grad, q, ((1,), (0,)))
        dv_sum[at, :] += dot(probs.astype(bf16), g, ((1,), (0,)))
        return total + dot(kt_ref[:, at], score_grad, ((1,), (0,)))

    total = lax.fori_loop(table[0, i], table[1, i], step, start_ref[...])
    rows = q.shape[0]
    dqkv_ref[pl.ds(pl.multiple_of(i * rows, rows), rows), :HD] = jnp.transpose(
        total * score_scale
    ).astype(bf16)

    @pl.when(i == pl.num_programs(0) - 1)
    def _():
        dqkv_ref[:, HD : 2 * HD] = dk_sum[...].astype(bf16)
        dqkv_ref[:, 2 * HD :] = dv_sum[...].astype(bf16)


def attention_table(segments, block_q, block_k):
    by_block = segments.reshape(-1, block_q)
    low_item, high_item = by_block[:, 0], by_block[:, -1]
    first_key = jnp.sum(segments[None, :] < low_item[:, None], axis=1)
    end_key = jnp.sum(segments[None, :] <= high_item[:, None], axis=1)
    return jnp.stack(
        [first_key // block_k, (end_key + block_k - 1) // block_k, low_item, high_item + 1]
    ).astype(jnp.int32)


def per_device(
    x_tokens, caption, timesteps, segment_ids, out_grad,
    mod_weight, mod_first, mod_second,
    norm_gains, gains_first, gains_second,
    qkv_weight, qkv_first, qkv_second,
    out_weight, out_first, out_second,
    text_weight, text_first, text_second,
    cross_gates, cross_first, cross_second,
    updown_weight, updown_first, updown_second,
    down_weight, down_first, down_second,
    *, seq_size, tp_size,
):
    seq_index = lax.axis_index("seq")
    tp_index = lax.axis_index("tp")
    ring = Ring(seq_size)
    here, width = x_tokens.shape
    heads = cross_gates.shape[0]
    local_width = heads * HD
    count = here * seq_size
    units = down_weight.shape[0]
    quarter = width // tp_size
    first_owner = 1 if seq_size >= heads + 2 else 0
    owners = range(first_owner, first_owner + heads)
    seqs = jnp.full((seq_size,), seq_index)
    place = jnp.where(seqs % 2 == 0, seqs // 2, (15 - seqs) // 2)
    places = (place + jnp.arange(seq_size)) % seq_size
    slab_owner = jnp.where(places < 4, 2 * places, 15 - 2 * places).astype(jnp.int32)
    slab_head = jnp.clip(slab_owner - first_owner, 0, heads - 1)
    my_head = jnp.clip(seq_index - first_owner, 0, heads - 1)
    is_owner = (seq_index >= first_owner) & (seq_index < first_owner + heads)
    tps = jnp.full((1,), tp_index)
    scal = jnp.concatenate([place[:1], tps % 2, tps]).astype(jnp.int32)
    which = {"size": seq_size, "ring": ring.ring}

    def exchange(slabs):
        return lax.all_to_all(slabs, "seq", 0, 0, tiled=True)

    cap_rows = caption.shape[0]
    cap_cols = caption.shape[1] // seq_size
    cap_part = cap_cols // tp_size
    text_rows = cap_rows * seq_size
    if cap_part % 128 == 0:
        cap_own = call(
            lambda scal, in_ref, out_ref: out_ref.__setitem__(0, in_ref[...]),
            "caption_slabs", seq_size, [scal],
            [(caption, pl.BlockSpec((cap_rows, cap_part), lambda i, s: (0, i * tp_size + s[2])))],
            [
                (
                    (seq_size, cap_rows, cap_part), bf16,
                    pl.BlockSpec((1, cap_rows, cap_part), lambda i, s: (i, 0, 0)),
                )
            ],
            moved=2 * cap_rows * cap_cols * 4,
        )[0]
    else:
        cap_own = lax.dynamic_index_in_dim(
            caption.reshape(cap_rows, seq_size, tp_size, cap_part), tp_index, 2, keepdims=False
        )
        cap_own = jnp.transpose(cap_own, (1, 0, 2))
    silu_embed = jax.nn.silu(time_embed(timesteps)).astype(bf16)
    mod_rows = mod_weight.shape[0]
    silu_embed = once(silu_embed, cap_own)
    embed_rows = lax.dynamic_slice_in_dim(silu_embed, seq_index * mod_rows, mod_rows, 1)
    mod_part = call(
        mod_kernel, "modulation", 6, [scal],
        [
            (embed_rows, whole((ITEMS, mod_rows))),
            (mod_weight, pl.BlockSpec((mod_rows, quarter), lambda i, s: (0, i * tp_size + s[2]))),
        ],
        [((6 * ITEMS, quarter), f32, rows_block(ITEMS, quarter))],
        moved=mod_rows * 6 * quarter * 4, flops=2 * ITEMS * mod_rows * 6 * quarter,
    )[0]
    is_here = jnp.arange(seq_size) == seq_index
    slots = jnp.where(is_here[:, None], segment_ids.astype(f32)[None, :], 0.0).reshape(-1)
    gain_cols = norm_gains.shape[1]
    gain_slots = jnp.where(is_here[None, :, None], norm_gains[:, None, :], 0.0).reshape(-1)
    spare = -(slots.size + gain_slots.size) % (8 * quarter)
    packed = jnp.concatenate([slots, gain_slots, jnp.zeros((spare,), f32)]).reshape(-1, quarter)
    packed = butterfly(jnp.concatenate([mod_part, packed]), "seq", seq_size)
    modulation = gather_tp(packed[: 6 * ITEMS], 1)
    packed = packed[6 * ITEMS :].reshape(-1)
    segments = packed[:count].astype(jnp.int32)
    gains_value = packed[count : count + 2 * width].reshape(2, width).astype(bf16).astype(f32)
    gains_value = jnp.concatenate([gains_value] * 4)

    def turned(shard):
        return jnp.transpose(shard.astype(bf16), (1, 0, 2)).reshape(shard.shape[1], -1)

    attn_chunks = ring.gather(
        jnp.concatenate([turned(qkv_weight), out_weight.astype(bf16).T], axis=1)
    )
    pieces = len(attn_chunks)
    piece_sems = pltpu.SemaphoreType.DMA((pieces,))
    attn_ins = [(chunk, anywhere()) for chunk in attn_chunks]
    qkv_width = 3 * local_width

    def hop(chunks, k):
        return (chunks[k], chunks[-k]) if ring.ring else ()

    cap_own = once(exchange(cap_own), *hop(attn_chunks, 1))
    caption_cols = gather_tp(cap_own.reshape(text_rows, cap_part), 1)
    if ring.ring:
        text_slabs = call(
            text_heads_kernel, "text_heads", 1, [slab_head],
            [(text_weight, whole(text_weight.shape))],
            [((cap_cols, seq_size * 2 * HD), bf16, whole((cap_cols, seq_size * 2 * HD)))],
            [pltpu.VMEM((heads, cap_cols, 2 * HD), bf16)],
            moved=text_weight.size * 6,
        )[0]
        text_parts = dot(caption_cols, text_slabs, ((1,), (0,))).astype(bf16)

        text_sum = ring.reduce(
            lambda k: text_parts[:, 2 * k * HD : 2 * (k + 1) * HD], owners
        )
        next(text_sum)
    else:
        parts = jnp.einsum(
            "rc,jchd->hrjd", caption_cols,
            text_weight.astype(bf16).reshape(2, cap_cols, heads, HD), preferred_element_type=f32,
        ).reshape(heads, text_rows, 2 * HD)
        after = seq_size - heads - first_owner
        parts = jnp.pad(parts.astype(bf16), ((first_owner, after), (0, 0), (0, 0)))
        text_kv = lax.psum_scatter(parts, "seq", scatter_dimension=0, tiled=False)

    ffn_shard = jnp.concatenate([turned(updown_weight), down_weight.astype(bf16).T], axis=1)
    ffn_chunks = ring.gather(once(ffn_shard, packed, *([text_parts] if ring.ring else [])))
    ffn_ins = [(chunk, anywhere()) for chunk in ffn_chunks]
    text_sent = text_sum.send(()) if ring.ring else ()
    modulation = once(modulation, *hop(attn_chunks, 3), *hop(ffn_chunks, 1), *text_sent)
    segment_col = segment_ids[:, None]
    steps = here // ROWS
    segment_row = segment_ids.reshape(steps, 1, ROWS)
    row_ins = [
        (segment_col, rows_block(ROWS, 1)),
        (segment_row, pl.BlockSpec((1, 1, ROWS), lambda i, *_: (i, 0, 0))),
    ]
    block = rows_block(ROWS, width)
    mod_shape, gain_shape = modulation.shape, gains_value.shape
    x_rel, g_rel, mod_rel, gain_rel, hidden_attn = call(
        functools.partial(enter_kernel, **which), "enter", steps, [scal],
        [
            (x_tokens, block), (out_grad, block), (modulation, whole(mod_shape)),
            (gains_value, whole(gain_shape)), row_ins[0],
        ],
        [
            ((here, width), bf16, block), ((here, width), bf16, block),
            (mod_shape, f32, whole(mod_shape)), (gain_shape, f32, whole(gain_shape)),
            ((here, width), bf16, block),
        ],
        moved=here * width * 10,
    )
    mod_ins = [(mod_rel, whole(mod_shape)), (gain_rel, whole(gain_shape))]
    full_ins = mod_ins + [(segment_col, whole((here, 1)))]
    slab_shape = (seq_size, here, 3 * HD)
    slabs = call(
        functools.partial(
            project_kernel, heads=heads, first_owner=first_owner, count=pieces
        ),
        "project", 1, [],
        [(hidden_attn, whole((here, width)))] + attn_ins,
        [(slab_shape, bf16, whole(slab_shape))],
        [pltpu.VMEM((width, qkv_width), bf16), piece_sems],
        moved=width * qkv_width * 2, flops=2 * here * width * qkv_width,
    )[0]
    qkv_head = exchange(slabs).reshape(count, 3 * HD)

    most = 1024 if count <= 4096 else 512
    block_q = math.gcd(count, most)
    block_k = math.gcd(count, most)
    table = attention_table(segments, block_q, block_k)
    tanh_cross = jnp.tanh(cross_gates)
    my_gate = jnp.sum(jnp.where(jnp.arange(heads) == my_head, tanh_cross, 0.0)).reshape(1)
    blocks = count // block_q
    q_ins = [(qkv_head, rows_block(block_q, 3 * HD))]
    seg_row = (segments[None, :], lanes_block(1, block_q))
    seg_col = (segments[:, None], whole((count, 1)))
    turned_out = ((HD, count), f32, lanes_block(HD, block_q))
    stat_out = ((1, count), f32, lanes_block(1, block_q))
    area = count * count * HD
    self_out, stat = call(
        functools.partial(self_kernel, block_k=block_k), "attend", blocks, [table],
        q_ins + [(qkv_head, whole(qkv_head.shape)), seg_row, seg_col],
        [turned_out, stat_out],
        [pltpu.VMEM((count, HD), bf16), pltpu.VMEM((HD, count), bf16)],
        flops=4 * area, moved=count * HD * 20, exps=count * count,
    )
    self_out = once(self_out, *hop(ffn_chunks, 2))
    if ring.ring:
        for held in ((slabs,), (qkv_head,), ()):
            text_kv = text_sum.send(held)
        text_kv = text_kv.astype(bf16)
    mixed_head, text_out, text_stat = call(
        text_kernel, "attend_text", blocks, [table, my_gate],
        q_ins
        + [(text_kv, whole(text_kv.shape)), (self_out, lanes_block(HD, block_q)), seg_row],
        [((count, HD), bf16, rows_block(block_q, HD)), turned_out, stat_out],
        [pltpu.VMEM((text_rows, HD), bf16), pltpu.VMEM((HD, text_rows), bf16)],
        flops=4 * count * TEXT * HD, moved=count * HD * 20, exps=count * TEXT,
    )
    mixed_head = once(mixed_head, *hop(ffn_chunks, 3))
    mixed_slabs = exchange(mixed_head.reshape(seq_size, here, HD))
    mixed_slabs = once(mixed_slabs, *(ffn_chunks[4:6] if ring.ring else ()))
    low, high = qkv_width, qkv_width + local_width
    head_args = {"heads": heads, "first_owner": first_owner, "count": pieces}
    half_shape = (here // 2, width)
    half_out = (half_shape, bf16, whole(half_shape))
    slab64 = (seq_size, here, HD)
    held_out = [pltpu.VMEM((width, local_width), bf16)]
    full_sum = [pltpu.VMEM((here, width), bf16), piece_sems]
    mixed, *attn = call(
        functools.partial(out_kernel, low=low, high=high, **head_args), "out", 1, [scal],
        [(mixed_slabs, whole(slab64))] + attn_ins,
        [((here, local_width), bf16, whole((here, local_width))), half_out, half_out],
        held_out + full_sum,
        moved=width * local_width * 2, flops=2 * here * width * local_width,
    )
    attn = psum_tp(attn)

    def halves(pair, spec=None):
        return [(one, spec or whole(half_shape)) for one in pair]

    tokens = (here, width)
    x_mid, hidden_ffn, ffn_grad, inner, both_grads, hm, ho, fm, fo = call(
        functools.partial(ffn_kernel, count=pieces, units=units), "ffn", 1, [scal],
        [(x_rel, whole(tokens)), (g_rel, whole(tokens))] + halves(attn) + full_ins + ffn_ins,
        [
            (tokens, f32, whole(tokens)), (tokens, bf16, whole(tokens)),
            (tokens, bf16, whole(tokens)), ((here, units), bf16, whole((here, units))),
            ((here, 2 * units), bf16, whole((here, 2 * units))),
            half_out, half_out, half_out, half_out,
        ],
        [pltpu.VMEM((width, 3 * units), bf16), pltpu.VMEM(tokens, bf16)] + full_sum,
        moved=width * 3 * units * 2, flops=12 * here * width * units,
    )
    hgrad = psum_tp((hm, ho))
    ffn_out = psum_tp(lax.optimization_barrier((fm, fo, *hgrad))[:2])
    mid_grad, attn_grad, grad_slabs = call(
        functools.partial(mid_kernel, low=low, high=high, **head_args), "mid", 1, [scal],
        [(x_mid, whole(tokens)), (g_rel, whole(tokens))] + halves(hgrad) + full_ins + attn_ins,
        [(tokens, f32, whole(tokens)), (tokens, bf16, whole(tokens)), (slab64, bf16, whole(slab64))],
        held_out + full_sum,
        moved=width * local_width * 2, flops=2 * here * width * local_width,
    )
    head_grad = exchange(grad_slabs).reshape(count, HD)
    ffn_sum = ring.reduce_products([(hidden_ffn, both_grads), (ffn_grad, inner)])
    next(ffn_sum)
    ffn_sum.send((grad_slabs,))
    head_grad = once(head_grad, *ffn_sum.send((head_grad,)))
    half_block = pl.BlockSpec((ROWS, width), lambda i, *_: (i % (steps // 2), 0))
    sums_shape, one_gain = (4 * ITEMS, width), (8, width)

    g_ins = [(head_grad, rows_block(block_q, HD))]
    kv64 = pltpu.VMEM((text_rows, HD), bf16)
    text_dkv, text_dq, cross_rows = call(
        text_back_kernel, "attend_text_back", blocks, [table, my_gate],
        q_ins + g_ins
        + [
            (text_kv, whole(text_kv.shape)), (text_out, lanes_block(HD, block_q)),
            (text_stat, lanes_block(1, block_q)), seg_row,
        ],
        [((text_rows, 2 * HD), bf16, whole((text_rows, 2 * HD))), turned_out, stat_out],
        [kv64, kv64, pltpu.VMEM((HD, text_rows), bf16)] + [pltpu.VMEM((text_rows, HD), f32)] * 2,
        flops=10 * count * TEXT * HD, moved=count * HD * 20, exps=count * TEXT,
    )
    head64 = pltpu.VMEM((count, HD), bf16)
    dqkv = call(
        functools.partial(self_back_kernel, block_k=block_k), "attend_back", blocks, [table],
        q_ins + g_ins
        + [
            (qkv_head, whole(qkv_head.shape)), (self_out, lanes_block(HD, block_q)),
            (stat, lanes_block(1, block_q)), (text_dq, lanes_block(HD, block_q)), seg_row, seg_col,
        ],
        [(qkv_head.shape, bf16, whole(qkv_head.shape))],
        [head64, head64, pltpu.VMEM((HD, count), bf16)] + [pltpu.VMEM((count, HD), f32)] * 2,
        flops=10 * area, moved=count * HD * 20, exps=count * count,
    )[0]

    back_slabs = exchange(dqkv.reshape(slab_shape))
    qkv_grads, *hidden_grad = call(
        functools.partial(qkv_back_kernel, **head_args), "qkv_back", 1, [scal],
        [(back_slabs, whole(slab_shape))] + attn_ins,
        [((here, qkv_width), bf16, whole((here, qkv_width))), half_out, half_out],
        [pltpu.VMEM((width, qkv_width), bf16)] + full_sum,
        moved=width * qkv_width * 2, flops=2 * here * width * qkv_width,
    )
    text_grads = ring.gather(text_dkv)
    if ring.ring:
        slab_at = jnp.argmax(
            slab_owner[None, :] == jnp.arange(first_owner, first_owner + heads)[:, None], axis=1
        ).astype(jnp.int32)
        text_owned = call(
            text_grad_kernel, "text_grad", 1, [slab_at],
            [(caption_cols.T, whole((cap_cols, text_rows)))]
            + [(one, anywhere()) for one in text_grads],
            [(text_weight.shape, f32, whole(text_weight.shape))],
            [
                pltpu.VMEM((seq_size * text_rows, 2 * HD), bf16),
                pltpu.SemaphoreType.DMA((len(text_grads),)),
            ],
            flops=4 * text_rows * cap_cols * local_width, moved=text_rows * cap_cols * 4,
        )[0]
    else:
        text_grads = text_grads[0].reshape(seq_size, text_rows, 2, HD)
        text_owned = jnp.einsum(
            "rc,hrjd->jchd", caption_cols, text_grads[first_owner : first_owner + heads],
            preferred_element_type=f32,
        ).reshape(text_weight.shape)

    attn_sum = ring.reduce_products([(hidden_attn, qkv_grads), (attn_grad, mixed)])
    next(attn_sum)
    ffn_sent = ffn_sum.send((dqkv,))
    updown_rows, down_owned = ffn_sum.send(())
    side_mid = once(x_mid, *ffn_sent)
    block_out, early_sums, early_gain = call(
        functools.partial(side_kernel, **which), "side", steps, [scal],
        [(side_mid, block), (mid_grad, block), (g_rel, block)]
        + halves(attn, half_block) + halves(ffn_out, half_block) + halves(hgrad, half_block)
        + mod_ins + row_ins,
        [(tokens, f32, block), (sums_shape, f32, whole(sums_shape)), (one_gain, f32, whole(one_gain))],
        moved=here * width * 24,
    )
    for _ in range(4):
        attn_grads = attn_sum.send(())
    qkv_rows, out_owned = attn_grads
    hidden_grad = psum_tp(hidden_grad)
    all_sums = (6 * ITEMS, quarter)
    input_grad, item_sums, gain_sums = call(
        functools.partial(leave_kernel, **which), "leave", steps, [scal],
        [(x_rel, block), (mid_grad, block)] + halves(hidden_grad, half_block) + mod_ins + row_ins
        + [(early_sums, whole(sums_shape)), (early_gain, whole(one_gain))],
        [(tokens, f32, block), (all_sums, f32, whole(all_sums)), (one_gain, f32, whole(one_gain))],
        [pltpu.VMEM((6 * ITEMS + 8, width), f32)] * 2,
        moved=here * width * 16,
    )

    cross_here = jnp.where(
        is_owner & (jnp.arange(quarter) == my_head), jnp.sum(cross_rows), 0.0
    )
    packed = jnp.concatenate(
        [
            item_sums, gain_sums[:2].reshape(-1, quarter), cross_here[None],
            jnp.zeros((-(2 * tp_size + 1) % 8, quarter), f32),
        ]
    )
    packed = butterfly(packed, "seq", seq_size)
    item_mod_low = packed[: 6 * ITEMS].astype(bf16)
    gain_grads = packed[6 * ITEMS : 6 * ITEMS + 2 * tp_size].reshape(2, seq_size, gain_cols)
    gains_owned = jnp.sum(jnp.where(is_here[None, :, None], gain_grads, 0.0), axis=1)
    cross_total = packed[6 * ITEMS + 2 * tp_size, :heads] * (1.0 - tanh_cross * tanh_cross)

    def by_block(sums):
        return jnp.transpose(sums.reshape(6, ITEMS, -1), (1, 0, 2)).reshape(ITEMS, -1)

    mod_weight_grad = dot(embed_rows, by_block(gather_tp(item_mod_low, 1)), ((0,), (0,)))
    mod_quarter_grad = dot(embed_rows, by_block(item_mod_low), ((0,), (0,)))

    owned_square = (
        square_sum(qkv_rows)
        + square_sum(out_owned)
        + square_sum(text_owned)
        + square_sum(updown_rows)
        + square_sum(down_owned)
        + square_sum(mod_quarter_grad)
    )
    owned_square = owned_square + jnp.where(tp_index == 0, square_sum(gains_owned), 0.0)
    owned_square = owned_square + jnp.where(seq_index == 0, square_sum(cross_total), 0.0)
    total_square = jnp.full((8, 128), owned_square)
    total_square = butterfly(butterfly(total_square, "tp", tp_size), "seq", seq_size)[0, 0]
    grad_norm = jnp.sqrt(total_square)
    clip = jnp.minimum(1.0, clip_limit / (grad_norm + 1e-06))

    def unturned(rows, blocks):
        return jnp.transpose(rows.reshape(rows.shape[0], blocks, -1), (1, 0, 2))

    matrix = functools.partial(adam_update, clip=clip, rate=rate_matrix, decay=decay_matrix)
    small = functools.partial(adam_update, clip=clip, rate=rate_small, decay=0.0)
    return (
        block_out,
        input_grad,
        grad_norm,
        *matrix(mod_weight, mod_first, mod_second, mod_weight_grad),
        *small(norm_gains, gains_first, gains_second, gains_owned),
        *matrix(qkv_weight, qkv_first, qkv_second, unturned(qkv_rows, 3)),
        *matrix(out_weight, out_first, out_second, out_owned.T),
        *matrix(text_weight, text_first, text_second, text_owned),
        *small(cross_gates, cross_first, cross_second, cross_total),
        *matrix(updown_weight, updown_first, updown_second, unturned(updown_rows, 2)),
        *matrix(down_weight, down_first, down_second, down_owned.T),
    )


def solution(mesh):
    rows = P("seq", None)
    cols = P(None, "seq")
    split = P(None, "seq", "tp")
    turned = P("tp", "seq")
    heads = P("tp")
    weights = (rows,) * 3 + (cols,) * 3 + (split,) * 3 + (turned,) * 3 + (split,) * 3
    weights = weights + (heads,) * 3 + (split,) * 3 + (turned,) * 3
    return jax.shard_map(
        functools.partial(per_device, seq_size=mesh.shape["seq"], tp_size=mesh.shape["tp"]),
        mesh=mesh,
        in_specs=(rows, rows, P(), P("seq"), rows) + weights,
        out_specs=(rows, rows, P()) + weights,
        check_vma=False,
    )
```
